32 devices in a mesh: farm: 4 (over z), nx: 4 (over y, core), ny: 2 (over x).
Axes of the slice: x: 2, y: 2, z: 4, core: 2. Of those that a mesh axis runs over, the one named last changes fastest.
Arguments:
- coarse_tiles: float32 [256, 32, 2048], P('farm', ('nx', 'ny')), may hold values from -6 to 6
- prolong_taps: float32 [3, 8], replicated, may hold values from 0.2 to 0.8
- tile_lists: int32 [4, 4], replicated, may hold values from 0 to 255, as said below
- nest_owner: int32 [4], replicated, may hold values from 0 to 3, each once
Outputs:
- updated_tiles: float32 [256, 32, 2048], P('farm', ('nx', 'ny'))
- nest_pressure: float32 [4, 256, 128, 128], P('farm', None, ('nx', 'ny'))
The draws below stay inside these ranges and needn't reach their ends.
Inputs may be any that keep to these rules, and one draw needn't show every extreme that they name: `tile_lists`: all entries are distinct; in each nest's row the values tile // 64 take every farm index exactly once. `nest_owner`: each farm index runs exactly one nest.
All inputs are finite; a program needn't handle non-finite values.
Results may differ from the reference program's by a relative error of at most 0.0003.
Values sent between devices are 32-bit elements; how exact they have to be, the bound alone decides.
No kernel may reach another device: no remote copies, remote signals or barrier semaphores. Data moves between devices by JAX's collectives and lax.ppermute only.
A program may use at most 384 MiB of HBM per device.

```python
import math
import jax
import jax.numpy as jnp
from jax import lax

TILE_Y = 32
TILE_Z = 32
REFINE = 4
TAPS = 8
CH = 4
TILES_DEV = 64
NT = 4
TILE_X = 16
NESTS = 4
TILES = 256
NFX = 256
NFY = 128
NFZ = 128
N_FARM = 4


def draw_tile_lists(key, part):
    local_key = jax.random.fold_in(key, 11)
    order_key = jax.random.fold_in(key, 23)
    ends = jnp.array([0, TILES_DEV - 1], dtype=jnp.int32)

    def per_source(source_key):
        middle = 1 + jax.random.permutation(source_key, TILES_DEV - 2)[:NESTS - 2]
        picked = jnp.concatenate([ends, middle.astype(jnp.int32)])
        return jax.random.permutation(jax.random.fold_in(source_key, 5), picked)
    local = jax.vmap(per_source)(jax.random.split(local_key, NESTS))
    orders = jax.vmap(lambda one_key: jax.random.permutation(one_key, NESTS))(jax.random.split(order_key, NESTS))
    orders = orders.astype(jnp.int32)
    nest_ids = jnp.arange(NESTS, dtype=jnp.int32)[:, None]
    return (orders * TILES_DEV + local[orders, nest_ids]).astype(jnp.int32)


def steps_of(key, dims, cuts, least, top_value):
    level = 1.0
    for dim, blocks in cuts:
        heights = jax.random.uniform(jax.random.fold_in(jax.random.fold_in(key, 6), dim), (blocks,), jnp.float32, least / len(cuts), top_value / len(cuts))
        level = level * jnp.repeat(jnp.exp(heights), dims[dim] // blocks).reshape((-1,) + (1,) * (len(dims) - 1 - dim))
    return level


def noise(own_key, dims, scale, reach, cuts=(), held_as=jnp.bfloat16):
    gain = steps_of(own_key, dims, cuts, -0.22, 0.18) if cuts else 1.0
    values = jax.random.normal(own_key, dims, jnp.float32) * scale * gain
    return jnp.minimum(jnp.maximum(values, -reach), reach).astype(held_as)


def setup_inputs(seed: int = 0) -> dict:
    keys = jax.random.split(jax.random.key(seed), 5)
    return {
        "coarse_tiles": noise(keys[0], (TILES, TILE_Y, CH * TILE_X * TILE_Z), 1.0, 6.0, ((0, 4), (1, 8)), jnp.float32),
        "prolong_taps": jnp.clip(jax.random.uniform(keys[1], (3, TAPS), jnp.float32, 0.2, 0.8), 0.2, 0.8),
        "tile_lists": draw_tile_lists(jax.random.fold_in(keys[4], 71), 0),
        "nest_owner": jax.random.permutation(keys[3], NESTS).astype(jnp.int32),
    }


exact_mode = lax.Precision.HIGHEST


def prolong_matrix(taps_row, fine_count, coarse_count, fine_start, coarse_start, period):
    fine_index = fine_start + jnp.arange(fine_count, dtype=jnp.int32)
    coarse_index = coarse_start + jnp.arange(coarse_count, dtype=jnp.int32)
    offset = jnp.mod(fine_index[:, None] - REFINE * coarse_index[None, :] + 2, period)
    tap_match = offset[:, :, None] == jnp.arange(TAPS, dtype=jnp.int32)[None, None, :]
    return jnp.sum(jnp.where(tap_match, taps_row[None, None, :], jnp.zeros((), jnp.float32)), axis=2)


def eigen_part(freq_start, freq_count, length):
    freq_index = (freq_start + jnp.arange(freq_count, dtype=jnp.int32)).astype(jnp.float32)
    return 4.0 * jnp.sin(freq_index * (math.pi / length)) ** 2


def slot_lists(tile_lists, nest_owner, slot_ids):
    owner_match = nest_owner[None, :] == slot_ids[:, None]
    return jnp.sum(jnp.where(owner_match[:, :, None], tile_lists[None, :, :], 0), axis=1).astype(jnp.int32)


def reference(coarse_tiles, prolong_taps, tile_lists, nest_owner):
    slot_ids = jnp.arange(N_FARM, dtype=jnp.int32)
    slot_tiles = slot_lists(tile_lists, nest_owner, slot_ids)
    width_x = NT * TILE_X
    row_width = CH * TILE_X * TILE_Z
    matrix_x = prolong_matrix(prolong_taps[0], NFX, width_x, 0, 0, NFX)
    matrix_y = prolong_matrix(prolong_taps[1], NFY, TILE_Y, 0, 0, NFY)
    matrix_z = prolong_matrix(prolong_taps[2], NFZ, TILE_Z, 0, 0, NFZ)
    eigen_sum = (eigen_part(0, NFX, NFX)[:, None, None] + eigen_part(0, NFY, NFY)[None, :, None]
                 + eigen_part(0, NFZ, NFZ)[None, None, :])
    nonzero = eigen_sum > 0
    factor = jnp.where(nonzero, -1.0 / jnp.where(nonzero, eigen_sum, 1.0), 0.0)

    def one_nest(tile_ids):
        chosen = coarse_tiles[tile_ids]
        coarse = chosen.reshape(NT, TILE_Y, CH, TILE_X, TILE_Z).transpose(2, 0, 3, 1, 4).reshape(CH, width_x, TILE_Y, TILE_Z)
        refined = jnp.einsum("xa,cayz->cxyz", matrix_x, coarse, precision=exact_mode)
        refined = jnp.einsum("zb,cxyb->cxyz", matrix_z, refined, precision=exact_mode)
        refined = jnp.einsum("yb,cxbz->cxyz", matrix_y, refined, precision=exact_mode)
        speed_x, speed_y, speed_z, pressure_old = refined[0], refined[1], refined[2], refined[3]
        spread = ((jnp.roll(speed_x, -1, 0) - speed_x) + (jnp.roll(speed_y, -1, 1) - speed_y)
                  + (jnp.roll(speed_z, -1, 2) - speed_z))
        spectrum = jnp.fft.fftn(spread) * factor
        pressure = jnp.real(jnp.fft.ifftn(spectrum)).astype(jnp.float32)
        new_fields = jnp.stack([
            speed_x - (pressure - jnp.roll(pressure, 1, 0)),
            speed_y - (pressure - jnp.roll(pressure, 1, 1)),
            speed_z - (pressure - jnp.roll(pressure, 1, 2)),
            pressure_old + pressure])
        blocks = new_fields.reshape(CH, width_x, REFINE, TILE_Y, REFINE, TILE_Z, REFINE).mean(axis=(2, 4, 6))
        restored = blocks.reshape(CH, NT, TILE_X, TILE_Y, TILE_Z).transpose(1, 3, 0, 2, 4).reshape(NT, TILE_Y, row_width)
        return restored, pressure

    restricted, pressures = lax.map(one_nest, slot_tiles)
    updated = coarse_tiles.at[slot_tiles.reshape(-1)].set(restricted.reshape(N_FARM * NT, TILE_Y, row_width))
    return updated, pressures
```

```python
import math

import jax
import jax.numpy as jnp
import numpy as np
from jax import lax
from jax.experimental import pallas as pl
from jax.experimental.pallas import tpu as pltpu
from jax.sharding import PartitionSpec as P

TILE_Z = 32
REFINE = 4
TAPS = 8
CH = 4
NFX = 256
NFY = 128
NFZ = 128


exact_mode = lax.Precision.HIGHEST


def with_halo(block, sides, width):
    for axis, dim in sides:
        count = lax.axis_size(axis)
        forward = [(i, i + 1) for i in range(count - 1)]
        forward.append((count - 1, 0))
        backward = [(target, source) for source, target in forward]
        low = lax.ppermute(
            lax.slice_in_dim(block, block.shape[dim] - width, None, axis=dim), axis, forward
        )
        high = lax.ppermute(lax.slice_in_dim(block, 0, width, axis=dim), axis, backward)
        block = jnp.concatenate([low, block, high], axis=dim)
    return block


def prolong_matrix(taps_row, fine_count, coarse_count, fine_start, coarse_start, period):
    fine_index = fine_start + jnp.arange(fine_count, dtype=jnp.int32)
    coarse_index = coarse_start + jnp.arange(coarse_count, dtype=jnp.int32)
    offset = jnp.mod(fine_index[:, None] - REFINE * coarse_index[None, :] + 2, period)
    tap_match = offset[:, :, None] == jnp.arange(TAPS, dtype=jnp.int32)[None, None, :]
    return jnp.sum(
        jnp.where(tap_match, taps_row[None, None, :], jnp.zeros((), jnp.float32)), axis=2
    )


def eigen_part(freq_start, freq_count, length):
    freq_index = (freq_start + jnp.arange(freq_count, dtype=jnp.int32)).astype(jnp.float32)
    return 4.0 * jnp.sin(freq_index * (math.pi / length)) ** 2


def slot_lists(tile_lists, nest_owner, slot_ids):
    owner_match = nest_owner[None, :] == slot_ids[:, None]
    return jnp.sum(jnp.where(owner_match[:, :, None], tile_lists[None, :, :], 0), axis=1)


def wave_tables(length):
    index_row = jnp.arange(length, dtype=jnp.int32)
    turns = jnp.mod(index_row[:, None] * index_row[None, :], length).astype(jnp.float32)
    phase_angle = turns * (2.0 * math.pi / length)
    return (jnp.cos(phase_angle), jnp.sin(phase_angle))


def apply_along(matrix, values, axis_id):
    moved = jnp.tensordot(matrix, values, axes=([1], [axis_id]), precision=exact_mode)
    return jnp.moveaxis(moved, 0, axis_id)


def forward_pair(real_part, imag_part, cosines, sines, axis_id):
    return (
        apply_along(cosines, real_part, axis_id) + apply_along(sines, imag_part, axis_id),
        apply_along(cosines, imag_part, axis_id) - apply_along(sines, real_part, axis_id),
    )


def inverse_pair(real_part, imag_part, cosines, sines, axis_id, length):
    return (
        (apply_along(cosines, real_part, axis_id) - apply_along(sines, imag_part, axis_id))
        / length,
        (apply_along(sines, real_part, axis_id) + apply_along(cosines, imag_part, axis_id))
        / length,
    )


def to_real_space(real_part, imag_part, cos_x, sin_x, cos_z, sin_z):
    real_z, imag_z = inverse_pair(real_part, imag_part, cos_z, sin_z, 2, NFZ)
    return (apply_along(cos_x, real_z, 0) - apply_along(sin_x, imag_z, 0)) / NFX


def local(coarse_tiles, prolong_taps, tile_lists, nest_owner):
    farm_count = lax.axis_size("farm")
    farm_index = lax.axis_index("farm")
    groups = lax.axis_size(("nx", "ny"))
    group_index = lax.axis_index(("nx", "ny"))
    local_tiles, row_count, row_width = coarse_tiles.shape
    tile_edge = row_width // (CH * TILE_Z)
    pair_count = tile_lists.shape[1]
    slot_ids = jnp.arange(farm_count, dtype=jnp.int32)
    slot_tiles = slot_lists(tile_lists, nest_owner, slot_ids)
    owned_ids = farm_index * local_tiles + jnp.arange(local_tiles, dtype=jnp.int32)
    selector = (slot_tiles[:, :, None] == owned_ids[None, None, :]).astype(jnp.float32)
    send_pick = jnp.sum(selector, axis=1)
    flat_tiles = coarse_tiles.reshape(local_tiles, row_count * row_width)
    outgoing = jnp.dot(send_pick, flat_tiles, precision=exact_mode)
    incoming = lax.all_to_all(
        outgoing.reshape(farm_count, row_count, row_width),
        "farm",
        split_axis=0,
        concat_axis=0,
        tiled=True,
    )
    my_tiles = slot_tiles[farm_index]
    home_index = my_tiles // local_tiles
    order_pick = (home_index[:, None] == slot_ids[None, :]).astype(jnp.float32)
    nest_rows = jnp.dot(
        order_pick, incoming.reshape(farm_count, row_count * row_width), precision=exact_mode
    )
    nest_rows = nest_rows.reshape(pair_count, row_count, row_width)
    framed = with_halo(nest_rows, ((("nx", "ny"), 1),), 1)
    width_x = pair_count * tile_edge
    coarse = framed.reshape(pair_count, row_count + 2, CH, tile_edge, TILE_Z).transpose(
        2, 0, 3, 1, 4
    )
    coarse = coarse.reshape(CH, width_x, row_count + 2, TILE_Z)
    fine_rows = REFINE * row_count
    matrix_x = prolong_matrix(prolong_taps[0], NFX, width_x, 0, 0, NFX)
    matrix_y = prolong_matrix(
        prolong_taps[1],
        fine_rows + 1,
        row_count + 2,
        fine_rows * group_index,
        row_count * group_index - 1,
        NFY,
    )
    matrix_z = prolong_matrix(prolong_taps[2], NFZ, TILE_Z, 0, 0, NFZ)
    refined = apply_along(matrix_x, coarse, 1)
    refined = apply_along(matrix_z, refined, 3)
    refined = apply_along(matrix_y, refined, 2)
    own_rows = refined[:, :, :fine_rows, :]
    spread = (
        jnp.roll(own_rows[0], -1, 0)
        - own_rows[0]
        + (refined[1, :, 1:, :] - own_rows[1])
        + (jnp.roll(own_rows[2], -1, 2) - own_rows[2])
    )
    cos_y, sin_y = wave_tables(NFY)
    cos_z, sin_z = wave_tables(NFZ)
    ahead_cos, ahead_sin = wave_tables(NFX)
    behind_cos, behind_sin = (ahead_cos, ahead_sin)
    real_x = apply_along(ahead_cos, spread, 0)
    imag_x = -apply_along(ahead_sin, spread, 0)
    real_xz, imag_xz = forward_pair(real_x, imag_x, cos_z, sin_z, 2)
    columns = lax.all_to_all(
        jnp.stack([real_xz, imag_xz]), ("nx", "ny"), split_axis=1, concat_axis=2, tiled=True
    )
    span = ahead_cos.shape[0] // groups
    real_y, imag_y = forward_pair(columns[0], columns[1], cos_y, sin_y, 1)
    eigen_y = eigen_part(0, NFY, NFY)
    eigen_z = eigen_part(0, NFZ, NFZ)
    eigen_sum = (
        eigen_part(group_index * span, span, NFX)[:, None, None]
        + eigen_y[None, :, None]
        + eigen_z[None, None, :]
    )
    nonzero = eigen_sum > 0
    factor = jnp.where(nonzero, -1.0 / jnp.where(nonzero, eigen_sum, 1.0), 0.0)
    real_p = real_y * factor
    imag_p = imag_y * factor
    back_real, back_imag = inverse_pair(real_p, imag_p, cos_y, sin_y, 1, NFY)
    theta = jnp.arange(NFY, dtype=jnp.float32) * (2.0 * math.pi / NFY)
    cos_diff = (1.0 - jnp.cos(theta))[None, :, None]
    sin_diff = jnp.sin(theta)[None, :, None]
    real_g = real_p * cos_diff - imag_p * sin_diff
    imag_g = real_p * sin_diff + imag_p * cos_diff
    grad_real, grad_imag = inverse_pair(real_g, imag_g, cos_y, sin_y, 1, NFY)
    returned = lax.all_to_all(
        jnp.stack([back_real, back_imag, grad_real, grad_imag]),
        ("nx", "ny"),
        split_axis=2,
        concat_axis=1,
        tiled=True,
    )
    pressure = to_real_space(returned[0], returned[1], behind_cos, behind_sin, cos_z, sin_z)
    grad_y = to_real_space(returned[2], returned[3], behind_cos, behind_sin, cos_z, sin_z)
    new_fields = jnp.stack(
        [
            own_rows[0] - (pressure - jnp.roll(pressure, 1, 0)),
            own_rows[1] - grad_y,
            own_rows[2] - (pressure - jnp.roll(pressure, 1, 2)),
            own_rows[3] + pressure,
        ]
    )
    blocks = new_fields.reshape(CH, width_x, REFINE, row_count, REFINE, TILE_Z, REFINE).mean(
        axis=(2, 4, 6)
    )
    restored = blocks.reshape(CH, pair_count, tile_edge, row_count, TILE_Z).transpose(1, 3, 0, 2, 4)
    restored = restored.reshape(pair_count, row_count * row_width)
    returning = jnp.dot(order_pick.T, restored, precision=exact_mode)
    arrived = lax.all_to_all(
        returning.reshape(farm_count, row_count, row_width),
        "farm",
        split_axis=0,
        concat_axis=0,
        tiled=True,
    )
    placed = jnp.dot(
        send_pick.T, arrived.reshape(farm_count, row_count * row_width), precision=exact_mode
    )
    covered = jnp.sum(send_pick, axis=0)
    updated = coarse_tiles * (1.0 - covered)[:, None, None] + placed.reshape(
        local_tiles, row_count, row_width
    )
    return (updated, pressure[None])


BF = jnp.bfloat16
F32 = jnp.float32
GROUP = ("nx", "ny")


def split_np(table):
    hi = jnp.asarray(table, F32).astype(BF)
    return hi


def halves(value):
    hi = value.astype(BF)
    return hi, (value - hi.astype(F32)).astype(BF)


def halves_np(table):
    table = np.asarray(table, np.float32)
    hi = table.astype(BF)
    return hi, (table - hi.astype(np.float32)).astype(BF)


def mm(left, right):
    return jnp.dot(left, right, preferred_element_type=F32)


def x_slots(nfx):
    quarter = nfx // 4
    low = np.arange(quarter)
    freq = np.concatenate([low, low, low + quarter, low + quarter])
    phase = np.concatenate(
        [np.ones(quarter), 1j * np.ones(quarter), np.ones(quarter), 1j * np.ones(quarter)]
    ).astype(np.complex128)
    freq[quarter] = nfx // 2
    phase[quarter] = 1.0
    phase[2 * quarter] = 1.0 - 1.0j
    weight = np.where((freq == 0) | (freq == nfx // 2), 1.0, 2.0)
    return freq, phase, weight


def z_slots(nfz):
    half = nfz // 2
    low = np.arange(half)
    freq = np.concatenate([low, low])
    imag = np.concatenate([np.zeros(half, bool), np.ones(half, bool)])
    freq[half] = half
    imag[half] = False
    weight = np.where((freq == 0) | (freq == half), 1.0, 2.0)
    return freq, imag, weight


def tables(nfx, nfy, nfz, rows):
    out = {}
    quarter = nfx // 4
    fx, phase, wx = x_slots(nfx)
    theta = 2 * np.pi * fx / nfx
    tap = np.arange(TAPS)[:, None] - 2
    gamma = (wx / nfx) * phase * np.exp(-1j * theta[None] * tap)
    mean = sum(np.exp(1j * theta * q) for q in range(REFINE)) / REFINE
    step = (np.exp(1j * theta * (REFINE - 1)) - np.exp(-1j * theta)) / REFINE
    gx = np.stack([gamma, gamma * mean, gamma * step])
    out["gx"] = np.stack([gx.real, gx.imag])
    turns = (np.arange(nfx)[:, None] * fx[None, :]) % nfx
    out["ex"] = np.stack([np.cos(turns * 2 * np.pi / nfx), np.sin(turns * 2 * np.pi / nfx)])
    out["e4"] = out["ex"][:, ::REFINE]
    fz, imag, wz = z_slots(nfz)
    phi = 2 * np.pi * fz / nfz
    psi = np.where(imag, -1j, 1.0)
    gz = psi * np.exp(-1j * phi[None] * tap)
    gz = np.stack([gz, gz * (np.exp(1j * phi) - 1.0)])
    out["gz"] = np.stack([gz.real, gz.imag])
    coarse_z = nfz // REFINE
    turns = (REFINE * np.arange(coarse_z)[:, None] * fz[None, :]) % nfz
    zz = np.stack([np.cos(turns * 2 * np.pi / nfz), np.sin(turns * 2 * np.pi / nfz)])
    out["zz"] = np.tile(zz, (1, rows, 1))
    turns = (fz[:, None] * np.arange(nfz)[None, :]) % nfz
    angle = turns * 2 * np.pi / nfz
    iz = (wz / nfz)[:, None] * np.where(imag[:, None], -np.sin(angle), np.cos(angle))
    hi, lo = halves_np(iz)
    out["iz"] = np.concatenate(
        [np.concatenate([hi, lo], 1), np.concatenate([hi, np.zeros_like(lo)], 1)], 0
    )
    rz = iz.reshape(nfz, coarse_z, REFINE).mean(2)
    dz = (iz[:, REFINE - 1 :: REFINE] - np.roll(iz, 1, 1)[:, ::REFINE]) / REFINE
    eye = np.eye(rows)
    for name, mat in (("rz", rz), ("dz", dz)):
        big = np.einsum("ij,kz->ikjz", eye, mat).reshape(rows * nfz, rows * coarse_z)
        hi, lo = halves_np(big)
        out[name] = np.stack([hi, lo])
    coarse = np.arange(quarter)
    turns = (coarse[:, None] * coarse[None, :]) % quarter
    angle = turns * 2 * np.pi / quarter
    fwd = np.concatenate([np.cos(angle), -np.sin(angle)], 0)
    fwd[quarter] = 1.0
    hi, lo = halves_np(fwd)
    out["fx"] = np.concatenate([hi, hi, lo], 1)
    mu = 4 * np.sin(np.pi * fx / nfx)[:, None] ** 2 + 4 * np.sin(np.pi * fz / nfz)[None, :] ** 2
    root = 1 + mu / 2 - np.sqrt(mu + mu * mu / 4)
    root = np.where(mu == 0, 0.0, root)
    kappa = -root / (1 - root**2)
    per = 1 / (1 - root**nfy)
    dx = np.exp(1j * theta) - 1
    own = dx.real.copy()
    other = np.concatenate(
        [-dx.imag[:quarter], dx.imag[:quarter], -dx.imag[2 * quarter : 3 * quarter],
         dx.imag[2 * quarter : 3 * quarter]]
    )
    own[0], own[quarter], own[2 * quarter], own[3 * quarter] = 0.0, -2.0, -1.0, 0.0
    other[[0, quarter, 2 * quarter, 3 * quarter]] = 0.0
    wide = np.ones((1, nfz))
    out["planes"] = np.stack([root, kappa, per, own[:, None] * wide, other[:, None] * wide])
    for key in ("gx", "ex", "e4", "gz", "zz", "planes"):
        out[key] = out[key].astype(np.float32)
    return out


def pick_indices(ids_ref, lists_ref, owner_ref, local_tiles, farm_count, pairs):
    me = ids_ref[0]
    found = []
    for shift in range(farm_count):
        target = me ^ shift
        tile = jnp.int32(0)
        for nest in range(farm_count):
            for pair in range(pairs):
                entry = lists_ref[nest, pair]
                hit = (owner_ref[nest] == target) & (entry // local_tiles == me)
                tile = jnp.where(hit, entry, tile)
        found.append(tile - me * local_tiles)
    return found


def home_shifts(ids_ref, lists_ref, owner_ref, local_tiles, farm_count, pairs):
    me = ids_ref[0]
    shifts = []
    for pair in range(pairs):
        tile = jnp.int32(0)
        for nest in range(farm_count):
            tile = jnp.where(owner_ref[nest] == me, lists_ref[nest, pair], tile)
        shifts.append((tile // local_tiles) ^ me)
    return shifts


def swap_blocks(value, rows, width):
    lane = lax.broadcasted_iota(jnp.int32, value.shape, 1) // width
    sub = lax.broadcasted_iota(jnp.int32, value.shape, 0) % rows
    delta = lane - sub
    result = value
    lanes = value.shape[1]
    height = value.shape[0]
    for shift in range(1, rows):
        for sign in (1, -1):
            amount = sign * shift
            moved = pltpu.roll(value, (amount * width) % lanes, 1)
            moved = pltpu.roll(moved, (-amount) % height, 0)
            result = jnp.where(delta == amount, moved, result)
    return result


def pick_kernel(local_tiles, farm_count, pairs, ids, lists, owner, tiles, *refs):
    outs, stage, sems = refs[:farm_count], refs[farm_count], refs[farm_count + 1]
    found = pick_indices(ids, lists, owner, local_tiles, farm_count, pairs)
    copies = []
    for shift in range(farm_count):
        copies.append(
            pltpu.make_async_copy(tiles.at[found[shift]], stage.at[shift], sems.at[shift])
        )
        copies[-1].start()
    for shift in range(farm_count):
        copies[shift].wait()
        outs[shift][...] = stage[shift]


def arrange_kernel(local_tiles, farm_count, pairs, ids, lists, owner, *refs):
    tiles, out, stage = refs[:farm_count], refs[farm_count], refs[farm_count + 1]
    for shift in range(farm_count):
        stage[shift] = tiles[shift][...]
    rows = stage.shape[1]
    channels, width_x, lanes = out.shape
    edge = width_x // pairs
    per = lanes // rows
    row_lanes = edge * per
    shifts = home_shifts(ids, lists, owner, local_tiles, farm_count, pairs)
    for pair in range(pairs):
        tile = stage[shifts[pair]]
        for channel in range(channels):
            for part in range(edge * per // (2 * lanes)):
                base = channel * row_lanes + 2 * part * lanes
                block = jnp.concatenate(
                    [tile[:, base : base + lanes], tile[:, base + lanes : base + 2 * lanes]], 0
                )
                at = pair * edge + 2 * part * rows
                out[channel, at : at + 2 * rows, :] = swap_blocks(block, rows, per)


def prep_kernel(taps, gx, gz, ex, e4, zz, tiles, mats, rmats, wu, ww, base, stage, sems):
    into = pltpu.make_async_copy(tiles, stage, sems.at[0])
    into.start()
    nfx = mats.shape[1]
    lanes = zz.shape[2]
    rows = wu.shape[1] // lanes
    per = lanes // rows

    def weighted(table, part, which, axis):
        total = taps[axis, 0] * table[part, which, 0:1, :]
        for tap in range(1, TAPS):
            total = total + taps[axis, tap] * table[part, which, tap : tap + 1, :]
        return total

    full = weighted(gx, 0, 0, 0) * ex[0] - weighted(gx, 1, 0, 0) * ex[1]
    hi, lo = halves(full)
    mats[0:nfx, :] = hi
    mats[nfx : 2 * nfx, :] = lo
    quarter = nfx // REFINE
    for which in (1, 2):
        at = (which - 1) * quarter
        coarse = weighted(gx, 0, which, 0) * e4[0] - weighted(gx, 1, which, 0) * e4[1]
        hi, lo = halves(coarse)
        rmats[0, at : at + quarter, :] = hi
        rmats[1, at : at + quarter, :] = lo
    band = lax.broadcasted_iota(jnp.int32, (lanes, lanes), 0) // per
    for which, target in ((0, wu), (1, ww)):
        value = weighted(gz, 0, which, 2) * zz[0] + weighted(gz, 1, which, 2) * zz[1]
        for row in range(rows):
            hi, lo = halves(jnp.where(band == row, value, 0.0))
            at = row * lanes
            target[0:lanes, at : at + lanes] = hi
            target[lanes : 2 * lanes, at : at + lanes] = hi
            target[2 * lanes : 3 * lanes, at : at + lanes] = lo
    into.wait()
    back = pltpu.make_async_copy(stage, base, sems.at[1])
    back.start()
    back.wait()


def solve_kernel(local_tiles, farm_count, pairs, groups, ids, lists, owner, taps, *refs):
    pieces = refs[:groups]
    (fx, wu_any, ww_any, planes_any, rmats, rz, dz, spectrum) = refs[groups : groups + 8]
    outs = refs[groups + 8 : groups + 8 + farm_count]
    (data, wu, ww, planes, left, field, mean_p, step_p, fresh, out_stage, zero_add, sems) = refs[
        groups + 8 + farm_count :
    ]
    group = ids[1]
    copies = []
    for shift in range(groups):
        copies.append(
            pltpu.make_async_copy(pieces[shift], data.at[group ^ shift], sems.at[shift])
        )
    weights = [
        pltpu.make_async_copy(wu_any, wu, sems.at[groups]),
        pltpu.make_async_copy(ww_any, ww, sems.at[groups + 1]),
        pltpu.make_async_copy(planes_any, planes, sems.at[groups + 2]),
    ]
    for copy in copies + weights:
        copy.start()
    for copy in copies:
        copy.wait()
    channels, width_x, lanes = data.shape[1:]
    rows = wu.shape[1] // lanes
    per = lanes // rows
    coarse_y = groups * rows
    fine_y = coarse_y * REFINE
    own_fine = rows * REFINE
    coarse_rows = fx.shape[0]

    for block in range(groups):
        hi_lo = [halves(data[block, channel]) for channel in range(3)]
        hi = jnp.concatenate([pair[0] for pair in hi_lo], 1)
        lo = jnp.concatenate([pair[1] for pair in hi_lo], 1)
        turned = mm(fx[...], jnp.concatenate([hi, lo, hi], 0))
        for channel in range(3):
            hi, lo = halves(turned[:, channel * lanes : (channel + 1) * lanes])
            at = block * coarse_rows
            left[channel, at : at + coarse_rows, :] = jnp.concatenate([hi, lo, hi], 1)
    for copy in weights:
        copy.wait()
    chunk = min(groups, 4)
    for channel in range(3):
        weight = ww if channel == 2 else wu
        for block in range(0, groups, chunk):
            at = block * coarse_rows
            value = mm(left[channel, at : at + chunk * coarse_rows, :], weight[...])
            for inner in range(chunk):
                for row in range(rows):
                    field[channel, (block + inner) * rows + row] = value[
                        inner * coarse_rows : (inner + 1) * coarse_rows,
                        row * lanes : (row + 1) * lanes,
                    ]

    sums = jnp.concatenate(
        [jnp.sum(data[block, 1], axis=0, keepdims=True) for block in range(groups)], 0
    )
    total_z = taps[2, 0]
    for tap in range(1, TAPS):
        total_z = total_z + taps[2, tap]
    sums = sums * total_z
    shape = (groups, lanes)
    coarse_id = rows * lax.broadcasted_iota(jnp.int32, shape, 0)
    coarse_id = coarse_id + lax.broadcasted_iota(jnp.int32, shape, 1) // per
    corner = (lax.broadcasted_iota(jnp.int32, (8, lanes), 0) == 0) & (
        lax.broadcasted_iota(jnp.int32, (8, lanes), 1) == 0
    )
    for index in range(own_fine + 1):
        at = own_fine * group - 1 + index
        weight = jnp.zeros(shape, F32)
        for tap in range(TAPS):
            gap = (at - REFINE * coarse_id + 2 - tap) & (fine_y - 1)
            saw = 0.5 - (2 * gap + 1).astype(F32) * (0.5 / fine_y)
            weight = weight + taps[1, tap] * saw
        value = jnp.sum(jnp.sum(weight * sums, axis=1, keepdims=True), axis=0, keepdims=True)
        zero_add[index] = jnp.where(corner, value, 0.0)

    first = rows * group

    def at_row(offset):
        return (first + offset) & (coarse_y - 1)

    def tap_y(offset):
        return taps[1, offset + 2]

    half_rows = coarse_rows // 2

    def sweep(step, carry):
        low = pl.multiple_of(8 * step, 8)
        spots = (low, half_rows + low)
        slots = [pl.multiple_of(part * half_rows + low, 8) for part in range(4)]

        def plane(which, part):
            return planes[which, pl.ds(slots[part], 8), :]

        def coarse(channel, row, side):
            return field[channel, row, pl.ds(spots[side], 8), :]

        root = [plane(0, part) for part in range(4)]
        quad = [value * value for value in root]
        quad = [value * value for value in quad]

        def horner(offset, sign):
            def body(i, acc):
                row = at_row(offset + sign * (coarse_y - 1 - i))
                loaded = [[coarse(c, row, side) for side in range(2)] for c in range(3)]
                return tuple(
                    acc[c * 4 + part] * quad[part] + loaded[c][part % 2]
                    for c in range(3)
                    for part in range(4)
                )

            zeros = tuple(jnp.zeros((8, lanes), F32) for _ in range(12))
            return lax.fori_loop(0, coarse_y, body, zeros, unroll=4)

        below = horner(-2, -1)
        above = horner(rows + 1, 1)
        near = list(range(-1, rows + 1))
        near_u = {m: [coarse(0, at_row(m), side) for side in range(2)] for m in near}
        near_v = {m: [coarse(1, at_row(m), side) for side in range(2)] for m in near}
        near_w = {m: [coarse(2, at_row(m), side) for side in range(2)] for m in near}
        for part in range(4):
            side = part % 2
            mate = part + 1 if side == 0 else part - 1
            r = root[part]
            kappa, per_wrap = plane(1, part), plane(2, part)
            own, other = plane(3, part), plane(4, part)
            turn = {
                m: own * near_u[m][side] + other * near_u[m][1 - side] + near_w[m][side]
                for m in near
            }
            lift = {m: near_v[m][side] for m in near}
            poly_a2 = tap_y(-2) * r + tap_y(-1)
            poly_a1 = poly_a2
            for e in range(0, 4):
                poly_a1 = poly_a1 * r + tap_y(e)
            poly_a = (poly_a1 * r + tap_y(4)) * r + tap_y(5)
            poly_b2 = tap_y(5) * r + tap_y(4)
            poly_b1 = poly_b2
            for e in (3, 2, 1, 0):
                poly_b1 = poly_b1 * r + tap_y(e)
            poly_b = (poly_b1 * r + tap_y(-1)) * r + tap_y(-2)
            far_scale = per_wrap * r * r
            turn_l = own * below[part] + other * below[mate] + below[8 + part]
            turn_r = own * above[part] + other * above[mate] + above[8 + part]
            drop = r - 1.0
            start = far_scale * poly_a * (turn_l + drop * below[4 + part])
            start = start + poly_a1 * turn[-1] + (drop * poly_a1 + tap_y(4)) * lift[-1]
            start = start + poly_a2 * turn[0] + (drop * poly_a2 + tap_y(0)) * lift[0]
            end = far_scale * poly_b * (r * turn_r - drop * above[4 + part])
            end = end + r * poly_b1 * turn[rows] - (drop * poly_b1 + tap_y(0)) * lift[rows]
            end = end + r * poly_b2 * turn[rows - 1] - (drop * poly_b2 + tap_y(4)) * lift[rows - 1]
            source = []
            for j in range(own_fine):
                m0, q = j // REFINE, j % REFINE
                total = None
                for m in (m0 - 1, m0, m0 + 1):
                    e = j - REFINE * m
                    if -2 <= e <= 5:
                        term = tap_y(e) * turn[m]
                        total = term if total is None else total + term
                    if -3 <= e <= 5:
                        scale = (tap_y(e + 1) if e < 5 else 0.0) - (tap_y(e) if e > -3 else 0.0)
                        total = total + scale * lift[m] if total is not None else scale * lift[m]
                source.append(total)
            ahead = [start]
            for j in range(own_fine):
                ahead.append(ahead[-1] * r + source[j])
            back = end
            pressure = [None] * (own_fine + 1)
            pressure[own_fine] = kappa * (ahead[own_fine] + back)
            for j in range(own_fine - 1, -1, -1):
                back = r * (back + source[j])
                pressure[j] = kappa * (ahead[j] + back)
            spot = pl.ds(slots[part], 8)
            for j in range(own_fine):
                spectrum[j, spot, :] = pressure[j + 1]
            for m in range(rows):
                at = REFINE * m
                total = pressure[at + 1]
                for q in range(1, REFINE):
                    total = total + pressure[at + 1 + q]
                mean_p[m, spot, :] = total * (1.0 / REFINE)
                step_p[m, spot, :] = (pressure[at + REFINE] - pressure[at]) * (1.0 / REFINE)
        return carry

    lax.fori_loop(0, half_rows // 8, sweep, 0)
    for j in range(own_fine):
        spectrum[j, 0:8, :] = spectrum[j, 0:8, :] + zero_add[j + 1]
    for m in range(rows):
        at = REFINE * m
        total = zero_add[at + 1]
        for q in range(1, REFINE):
            total = total + zero_add[at + 1 + q]
        mean_p[m, 0:8, :] = mean_p[m, 0:8, :] + total * (1.0 / REFINE)
        step = (zero_add[at + REFINE] - zero_add[at]) * (1.0 / REFINE)
        step_p[m, 0:8, :] = step_p[m, 0:8, :] + step

    def left_three(count, stacked):
        hi, lo = halves(stacked)
        value = mm(rmats[0, 0:count, :], hi) + mm(rmats[0, 0:count, :], lo)
        return value + mm(rmats[1, 0:count, :], hi)

    def right_three(value, table):
        hi, lo = halves(value)
        return mm(hi, table[0]) + mm(lo, table[0]) + mm(hi, table[1])

    smooth = left_three(2 * width_x, jnp.concatenate([mean_p[m] for m in range(rows)], 1))
    slope = left_three(width_x, jnp.concatenate([step_p[m] for m in range(rows)], 1))
    mean_x, step_x = smooth[0:width_x], smooth[width_x : 2 * width_x]
    through = right_three(jnp.concatenate([step_x, slope, mean_x], 0), rz)
    part_w = right_three(mean_x, dz)
    change = [
        -through[0:width_x],
        -through[width_x : 2 * width_x],
        -part_w,
        through[2 * width_x : 3 * width_x],
    ]

    def band(axis):
        quarter = 1.0 / REFINE
        return (
            (taps[axis, 6] + taps[axis, 7]) * quarter,
            (taps[axis, 2] + taps[axis, 3] + taps[axis, 4] + taps[axis, 5]) * quarter,
            (taps[axis, 0] + taps[axis, 1]) * quarter,
        )

    lane = lax.broadcasted_iota(jnp.int32, (width_x, lanes), 1)
    previous = (group + groups - 1) & (groups - 1)
    following = (group + 1) & (groups - 1)
    for channel in range(channels):
        here = data[group, channel]
        before, after = data[previous, channel], data[following, channel]
        lag, mid, lead = band(1)
        low = jnp.where(lane < per, pltpu.roll(before, per, 1), pltpu.roll(here, per, 1))
        high = jnp.where(
            lane >= lanes - per, pltpu.roll(after, lanes - per, 1), pltpu.roll(here, lanes - per, 1)
        )
        value = mid * here + lag * low + lead * high
        lag, mid, lead = band(2)
        spot = lane % per
        low = jnp.where(spot == 0, pltpu.roll(value, lanes - per + 1, 1), pltpu.roll(value, 1, 1))
        high = jnp.where(
            spot == per - 1, pltpu.roll(value, per - 1, 1), pltpu.roll(value, lanes - 1, 1)
        )
        value = mid * value + lag * low + lead * high
        lag, mid, lead = band(0)
        value = (
            mid * value
            + lag * pltpu.roll(value, 1, 0)
            + lead * pltpu.roll(value, width_x - 1, 0)
        )
        fresh[channel] = value + change[channel]
    shifts = home_shifts(ids, lists, owner, local_tiles, farm_count, pairs)
    edge = width_x // pairs
    row_lanes = edge * per
    for pair in range(pairs):
        for channel in range(channels):
            for part in range(row_lanes // (2 * lanes)):
                at = pair * edge + 2 * part * rows
                block = swap_blocks(fresh[channel, at : at + 2 * rows, :], rows, per)
                base = channel * row_lanes + 2 * part * lanes
                out_stage[shifts[pair], :, base : base + lanes] = block[0:rows]
                out_stage[shifts[pair], :, base + lanes : base + 2 * lanes] = block[rows:]
    for shift in range(farm_count):
        outs[shift][...] = out_stage[shift]


def inverse_kernel(iz, mats, spectrum, out):
    count, nfx, lanes = spectrum.shape
    for at in range(0, count, 2):
        value = []
        for row in (at, at + 1):
            hi, lo = halves(spectrum[row])
            both = mm(jnp.concatenate([hi, lo], 1), iz[...])
            value.append(both[:, 0:lanes] + both[:, lanes : 2 * lanes])
        hi, lo = halves(jnp.concatenate(value, 1))
        upper = mm(mats[...], hi)
        final = upper[0:nfx] + upper[nfx : 2 * nfx] + mm(mats[0:nfx, :], lo)
        for row in range(2):
            out[:, at + row, :] = final[:, row * lanes : (row + 1) * lanes]


def patch_kernel(local_tiles, farm_count, pairs, ids, lists, owner, base, *refs):
    tiles, out, sems = refs[:farm_count], refs[farm_count], refs[farm_count + 1]
    found = pick_indices(ids, lists, owner, local_tiles, farm_count, pairs)
    copies = []
    for shift in range(farm_count):
        copies.append(
            pltpu.make_async_copy(tiles[shift], out.at[found[shift]], sems.at[shift])
        )
        copies[-1].start()
    for copy in copies:
        copy.wait()


def in_vmem():
    return pl.BlockSpec(memory_space=pltpu.VMEM)


def in_smem():
    return pl.BlockSpec(memory_space=pltpu.SMEM)


def anywhere():
    return pl.BlockSpec(memory_space=pl.ANY)


def limit(mib):
    return pltpu.CompilerParams(vmem_limit_bytes=mib << 20)


def cost(flops, nbytes):
    return pl.CostEstimate(flops=flops, bytes_accessed=nbytes, transcendentals=0)


def flip(value, axis, bits):
    count = lax.axis_size(axis)
    return lax.ppermute(value, axis, [(i, i ^ bits) for i in range(count)])


def fast_local(coarse_tiles, prolong_taps, tile_lists, nest_owner):
    farm_count = lax.axis_size("farm")
    groups = lax.axis_size(GROUP)
    local_tiles, rows, row_width = coarse_tiles.shape
    pairs = tile_lists.shape[1]
    edge = row_width // (CH * TILE_Z)
    width_x = pairs * edge
    lanes = rows * TILE_Z
    own_fine = rows * REFINE
    table = tables(NFX, NFY, NFZ, rows)
    const = {key: jnp.asarray(value) for key, value in table.items()}
    ids = jnp.stack([lax.axis_index("farm"), lax.axis_index(GROUP)]).astype(jnp.int32)
    sizes = (local_tiles, farm_count, pairs)
    bind = lambda kernel, *extra: (lambda *refs: kernel(*sizes, *extra, *refs))
    tile_shape = jax.ShapeDtypeStruct((rows, row_width), F32)
    scalars = [in_smem()] * 3

    picked = pl.pallas_call(
        bind(pick_kernel),
        name="pick",
        out_shape=[tile_shape] * farm_count,
        in_specs=scalars + [anywhere()],
        out_specs=[in_vmem()] * farm_count,
        scratch_shapes=[
            pltpu.VMEM((farm_count, rows, row_width), F32),
            pltpu.SemaphoreType.DMA((farm_count,)),
        ],
        compiler_params=limit(8),
        cost_estimate=cost(0, 1 << 18),
    )(ids, tile_lists, nest_owner, coarse_tiles)
    moved = [picked[0]] + [flip(picked[s], "farm", s) for s in range(1, farm_count)]
    piece = pl.pallas_call(
        bind(arrange_kernel),
        name="arrange",
        out_shape=jax.ShapeDtypeStruct((CH, width_x, lanes), F32),
        in_specs=scalars + [in_vmem()] * farm_count,
        out_specs=in_vmem(),
        scratch_shapes=[pltpu.VMEM((farm_count, rows, row_width), F32)],
        compiler_params=limit(8),
        cost_estimate=cost(0, 1 << 18),
    )(ids, tile_lists, nest_owner, *moved)
    far_bit, core_bit, near_bit = 4, 2, 1
    held = {0: piece}
    for bits in (near_bit, far_bit, near_bit | far_bit):
        held[bits] = flip(piece, GROUP, bits)
    for bits in (0, near_bit, far_bit, near_bit | far_bit):
        held[bits | core_bit] = flip(held[bits], GROUP, core_bit)

    mats, rmats, wu, ww, base = pl.pallas_call(
        prep_kernel,
        name="prep",
        out_shape=[
            jax.ShapeDtypeStruct((2 * NFX, NFX), BF),
            jax.ShapeDtypeStruct((2, 2 * width_x, NFX), BF),
            jax.ShapeDtypeStruct((3 * lanes, rows * NFZ), BF),
            jax.ShapeDtypeStruct((3 * lanes, rows * NFZ), BF),
            jax.ShapeDtypeStruct(coarse_tiles.shape, F32),
        ],
        in_specs=[in_smem()] + [in_vmem()] * 5 + [anywhere()],
        out_specs=[in_vmem()] * 4 + [anywhere()],
        scratch_shapes=[
            pltpu.VMEM(coarse_tiles.shape, F32),
            pltpu.SemaphoreType.DMA((2,)),
        ],
        compiler_params=limit(16),
        cost_estimate=cost(0, 6 << 20),
    )(prolong_taps, const["gx"], const["gz"], const["ex"], const["e4"], const["zz"], coarse_tiles)

    coarse_rows = 2 * width_x
    coarse_y = groups * rows
    spectrum, *fresh = pl.pallas_call(
        bind(solve_kernel, groups),
        name="solve",
        out_shape=[jax.ShapeDtypeStruct((own_fine, NFX, NFZ), F32)] + [tile_shape] * farm_count,
        in_specs=scalars
        + [in_smem()]
        + [anywhere()] * groups
        + [in_vmem()]
        + [anywhere()] * 3
        + [in_vmem()] * 3,
        out_specs=[in_vmem()] * (farm_count + 1),
        scratch_shapes=[
            pltpu.VMEM((groups, CH, width_x, lanes), F32),
            pltpu.VMEM((3 * lanes, rows * NFZ), BF),
            pltpu.VMEM((3 * lanes, rows * NFZ), BF),
            pltpu.VMEM(const["planes"].shape, F32),
            pltpu.VMEM((3, groups * coarse_rows, 3 * lanes), BF),
            pltpu.VMEM((3, coarse_y, coarse_rows, NFZ), F32),
            pltpu.VMEM((rows, NFX, NFZ), F32),
            pltpu.VMEM((rows, NFX, NFZ), F32),
            pltpu.VMEM((CH, width_x, lanes), F32),
            pltpu.VMEM((farm_count, rows, row_width), F32),
            pltpu.VMEM((own_fine + 1, 8, lanes), F32),
            pltpu.SemaphoreType.DMA((groups + 3,)),
        ],
        compiler_params=limit(40),
        cost_estimate=cost(4 << 30, 8 << 20),
    )(
        ids, tile_lists, nest_owner, prolong_taps,
        *[held[s] for s in range(groups)],
        const["fx"], wu, ww, const["planes"], rmats, const["rz"], const["dz"],
    )
    returned = [fresh[0]] + [flip(fresh[s], "farm", s) for s in range(1, farm_count)]

    half = 8
    pressure = pl.pallas_call(
        inverse_kernel,
        name="inverse",
        out_shape=jax.ShapeDtypeStruct((NFX, own_fine, NFZ), F32),
        grid=(own_fine // half,),
        in_specs=[
            pl.BlockSpec((2 * NFZ, 2 * NFZ), lambda i: (0, 0)),
            pl.BlockSpec((2 * NFX, NFX), lambda i: (0, 0)),
            pl.BlockSpec((half, NFX, NFZ), lambda i: (i, 0, 0)),
        ],
        out_specs=pl.BlockSpec((NFX, half, NFZ), lambda i: (0, i, 0)),
        compiler_params=limit(24),
        cost_estimate=cost(4 << 30, 4 << 20),
    )(const["iz"], mats, spectrum)

    updated = pl.pallas_call(
        bind(patch_kernel),
        name="patch",
        out_shape=jax.ShapeDtypeStruct(coarse_tiles.shape, F32),
        in_specs=scalars + [anywhere()] + [in_vmem()] * farm_count,
        out_specs=anywhere(),
        scratch_shapes=[pltpu.SemaphoreType.DMA((farm_count,))],
        input_output_aliases={3: 0},
        compiler_params=limit(8),
        cost_estimate=cost(0, 1 << 18),
    )(ids, tile_lists, nest_owner, base, *returned)
    return updated, pressure[None]


def fits_fast(mesh):
    return dict(mesh.shape) == {"farm": 4, "nx": 4, "ny": 2}


def solution(mesh):
    def body(coarse_tiles, prolong_taps, tile_lists, nest_owner):
        rows, row_width = coarse_tiles.shape[1:]
        edge = row_width // (CH * TILE_Z)
        dense = rows * TILE_Z == NFZ and edge % (2 * rows) == 0
        whole = tile_lists.shape[1] * edge * REFINE == NFX
        if fits_fast(mesh) and dense and whole:
            return fast_local(coarse_tiles, prolong_taps, tile_lists, nest_owner)
        return local(coarse_tiles, prolong_taps, tile_lists, nest_owner)

    return jax.shard_map(
        body,
        mesh=mesh,
        in_specs=(P("farm", GROUP, None), P(), P(), P()),
        out_specs=(P("farm", GROUP, None), P("farm", None, GROUP, None)),
        check_vma=False,
    )
```

```python
import math

import jax
import jax.numpy as jnp
import numpy as np
from jax import lax
from jax.experimental import pallas as pl
from jax.experimental.pallas import tpu as pltpu
from jax.sharding import PartitionSpec as P

TILE_Z = 32
REFINE = 4
TAPS = 8
CH = 4
NFX = 256
NFY = 128
NFZ = 128


exact_mode = lax.Precision.HIGHEST


def with_halo(block, sides, width):
    for axis, dim in sides:
        count = lax.axis_size(axis)
        forward = [(i, i + 1) for i in range(count - 1)]
        forward.append((count - 1, 0))
        backward = [(target, source) for source, target in forward]
        low = lax.ppermute(
            lax.slice_in_dim(block, block.shape[dim] - width, None, axis=dim), axis, forward
        )
        high = lax.ppermute(lax.slice_in_dim(block, 0, width, axis=dim), axis, backward)
        block = jnp.concatenate([low, block, high], axis=dim)
    return block


def prolong_matrix(taps_row, fine_count, coarse_count, fine_start, coarse_start, period):
    fine_index = fine_start + jnp.arange(fine_count, dtype=jnp.int32)
    coarse_index = coarse_start + jnp.arange(coarse_count, dtype=jnp.int32)
    offset = jnp.mod(fine_index[:, None] - REFINE * coarse_index[None, :] + 2, period)
    tap_match = offset[:, :, None] == jnp.arange(TAPS, dtype=jnp.int32)[None, None, :]
    return jnp.sum(
        jnp.where(tap_match, taps_row[None, None, :], jnp.zeros((), jnp.float32)), axis=2
    )


def eigen_part(freq_start, freq_count, length):
    freq_index = (freq_start + jnp.arange(freq_count, dtype=jnp.int32)).astype(jnp.float32)
    return 4.0 * jnp.sin(freq_index * (math.pi / length)) ** 2


def slot_lists(tile_lists, nest_owner, slot_ids):
    owner_match = nest_owner[None, :] == slot_ids[:, None]
    return jnp.sum(jnp.where(owner_match[:, :, None], tile_lists[None, :, :], 0), axis=1)


def wave_tables(length):
    index_row = jnp.arange(length, dtype=jnp.int32)
    turns = jnp.mod(index_row[:, None] * index_row[None, :], length).astype(jnp.float32)
    phase_angle = turns * (2.0 * math.pi / length)
    return (jnp.cos(phase_angle), jnp.sin(phase_angle))


def apply_along(matrix, values, axis_id):
    moved = jnp.tensordot(matrix, values, axes=([1], [axis_id]), precision=exact_mode)
    return jnp.moveaxis(moved, 0, axis_id)


def forward_pair(real_part, imag_part, cosines, sines, axis_id):
    return (
        apply_along(cosines, real_part, axis_id) + apply_along(sines, imag_part, axis_id),
        apply_along(cosines, imag_part, axis_id) - apply_along(sines, real_part, axis_id),
    )


def inverse_pair(real_part, imag_part, cosines, sines, axis_id, length):
    return (
        (apply_along(cosines, real_part, axis_id) - apply_along(sines, imag_part, axis_id))
        / length,
        (apply_along(sines, real_part, axis_id) + apply_along(cosines, imag_part, axis_id))
        / length,
    )


def to_real_space(real_part, imag_part, cos_x, sin_x, cos_z, sin_z):
    real_z, imag_z = inverse_pair(real_part, imag_part, cos_z, sin_z, 2, NFZ)
    return (apply_along(cos_x, real_z, 0) - apply_along(sin_x, imag_z, 0)) / NFX


def local(coarse_tiles, prolong_taps, tile_lists, nest_owner):
    farm_count = lax.axis_size("farm")
    farm_index = lax.axis_index("farm")
    groups = lax.axis_size(("nx", "ny"))
    group_index = lax.axis_index(("nx", "ny"))
    local_tiles, row_count, row_width = coarse_tiles.shape
    tile_edge = row_width // (CH * TILE_Z)
    pair_count = tile_lists.shape[1]
    slot_ids = jnp.arange(farm_count, dtype=jnp.int32)
    slot_tiles = slot_lists(tile_lists, nest_owner, slot_ids)
    owned_ids = farm_index * local_tiles + jnp.arange(local_tiles, dtype=jnp.int32)
    selector = (slot_tiles[:, :, None] == owned_ids[None, None, :]).astype(jnp.float32)
    send_pick = jnp.sum(selector, axis=1)
    flat_tiles = coarse_tiles.reshape(local_tiles, row_count * row_width)
    outgoing = jnp.dot(send_pick, flat_tiles, precision=exact_mode)
    incoming = lax.all_to_all(
        outgoing.reshape(farm_count, row_count, row_width),
        "farm",
        split_axis=0,
        concat_axis=0,
        tiled=True,
    )
    my_tiles = slot_tiles[farm_index]
    home_index = my_tiles // local_tiles
    order_pick = (home_index[:, None] == slot_ids[None, :]).astype(jnp.float32)
    nest_rows = jnp.dot(
        order_pick, incoming.reshape(farm_count, row_count * row_width), precision=exact_mode
    )
    nest_rows = nest_rows.reshape(pair_count, row_count, row_width)
    framed = with_halo(nest_rows, ((("nx", "ny"), 1),), 1)
    width_x = pair_count * tile_edge
    coarse = framed.reshape(pair_count, row_count + 2, CH, tile_edge, TILE_Z).transpose(
        2, 0, 3, 1, 4
    )
    coarse = coarse.reshape(CH, width_x, row_count + 2, TILE_Z)
    fine_rows = REFINE * row_count
    matrix_x = prolong_matrix(prolong_taps[0], NFX, width_x, 0, 0, NFX)
    matrix_y = prolong_matrix(
        prolong_taps[1],
        fine_rows + 1,
        row_count + 2,
        fine_rows * group_index,
        row_count * group_index - 1,
        NFY,
    )
    matrix_z = prolong_matrix(prolong_taps[2], NFZ, TILE_Z, 0, 0, NFZ)
    refined = apply_along(matrix_x, coarse, 1)
    refined = apply_along(matrix_z, refined, 3)
    refined = apply_along(matrix_y, refined, 2)
    own_rows = refined[:, :, :fine_rows, :]
    spread = (
        jnp.roll(own_rows[0], -1, 0)
        - own_rows[0]
        + (refined[1, :, 1:, :] - own_rows[1])
        + (jnp.roll(own_rows[2], -1, 2) - own_rows[2])
    )
    cos_y, sin_y = wave_tables(NFY)
    cos_z, sin_z = wave_tables(NFZ)
    ahead_cos, ahead_sin = wave_tables(NFX)
    behind_cos, behind_sin = (ahead_cos, ahead_sin)
    real_x = apply_along(ahead_cos, spread, 0)
    imag_x = -apply_along(ahead_sin, spread, 0)
    real_xz, imag_xz = forward_pair(real_x, imag_x, cos_z, sin_z, 2)
    columns = lax.all_to_all(
        jnp.stack([real_xz, imag_xz]), ("nx", "ny"), split_axis=1, concat_axis=2, tiled=True
    )
    span = ahead_cos.shape[0] // groups
    real_y, imag_y = forward_pair(columns[0], columns[1], cos_y, sin_y, 1)
    eigen_y = eigen_part(0, NFY, NFY)
    eigen_z = eigen_part(0, NFZ, NFZ)
    eigen_sum = (
        eigen_part(group_index * span, span, NFX)[:, None, None]
        + eigen_y[None, :, None]
        + eigen_z[None, None, :]
    )
    nonzero = eigen_sum > 0
    factor = jnp.where(nonzero, -1.0 / jnp.where(nonzero, eigen_sum, 1.0), 0.0)
    real_p = real_y * factor
    imag_p = imag_y * factor
    back_real, back_imag = inverse_pair(real_p, imag_p, cos_y, sin_y, 1, NFY)
    theta = jnp.arange(NFY, dtype=jnp.float32) * (2.0 * math.pi / NFY)
    cos_diff = (1.0 - jnp.cos(theta))[None, :, None]
    sin_diff = jnp.sin(theta)[None, :, None]
    real_g = real_p * cos_diff - imag_p * sin_diff
    imag_g = real_p * sin_diff + imag_p * cos_diff
    grad_real, grad_imag = inverse_pair(real_g, imag_g, cos_y, sin_y, 1, NFY)
    returned = lax.all_to_all(
        jnp.stack([back_real, back_imag, grad_real, grad_imag]),
        ("nx", "ny"),
        split_axis=2,
        concat_axis=1,
        tiled=True,
    )
    pressure = to_real_space(returned[0], returned[1], behind_cos, behind_sin, cos_z, sin_z)
    grad_y = to_real_space(returned[2], returned[3], behind_cos, behind_sin, cos_z, sin_z)
    new_fields = jnp.stack(
        [
            own_rows[0] - (pressure - jnp.roll(pressure, 1, 0)),
            own_rows[1] - grad_y,
            own_rows[2] - (pressure - jnp.roll(pressure, 1, 2)),
            own_rows[3] + pressure,
        ]
    )
    blocks = new_fields.reshape(CH, width_x, REFINE, row_count, REFINE, TILE_Z, REFINE).mean(
        axis=(2, 4, 6)
    )
    restored = blocks.reshape(CH, pair_count, tile_edge, row_count, TILE_Z).transpose(1, 3, 0, 2, 4)
    restored = restored.reshape(pair_count, row_count * row_width)
    returning = jnp.dot(order_pick.T, restored, precision=exact_mode)
    arrived = lax.all_to_all(
        returning.reshape(farm_count, row_count, row_width),
        "farm",
        split_axis=0,
        concat_axis=0,
        tiled=True,
    )
    placed = jnp.dot(
        send_pick.T, arrived.reshape(farm_count, row_count * row_width), precision=exact_mode
    )
    covered = jnp.sum(send_pick, axis=0)
    updated = coarse_tiles * (1.0 - covered)[:, None, None] + placed.reshape(
        local_tiles, row_count, row_width
    )
    return (updated, pressure[None])


BF = jnp.bfloat16
F32 = jnp.float32
GROUP = ("nx", "ny")


def split_np(table):
    hi = jnp.asarray(table, F32).astype(BF)
    return hi


def halves(value):
    hi = value.astype(BF)
    return hi, (value - hi.astype(F32)).astype(BF)


def halves_np(table):
    table = np.asarray(table, np.float32)
    hi = table.astype(BF)
    return hi, (table - hi.astype(np.float32)).astype(BF)


def mm(left, right):
    return jnp.dot(left, right, preferred_element_type=F32)


def x_slots(nfx):
    quarter = nfx // 4
    low = np.arange(quarter)
    freq = np.concatenate([low, low, low + quarter, low + quarter])
    phase = np.concatenate(
        [np.ones(quarter), 1j * np.ones(quarter), np.ones(quarter), 1j * np.ones(quarter)]
    ).astype(np.complex128)
    freq[quarter] = nfx // 2
    phase[quarter] = 1.0
    phase[2 * quarter] = 1.0 - 1.0j
    weight = np.where((freq == 0) | (freq == nfx // 2), 1.0, 2.0)
    return freq, phase, weight


def z_slots(nfz):
    half = nfz // 2
    low = np.arange(half)
    freq = np.concatenate([low, low])
    imag = np.concatenate([np.zeros(half, bool), np.ones(half, bool)])
    freq[half] = half
    imag[half] = False
    weight = np.where((freq == 0) | (freq == half), 1.0, 2.0)
    return freq, imag, weight


def tables(nfx, nfy, nfz, rows):
    out = {}
    quarter = nfx // 4
    fx, phase, wx = x_slots(nfx)
    theta = 2 * np.pi * fx / nfx
    tap = np.arange(TAPS)[:, None] - 2
    gamma = (wx / nfx) * phase * np.exp(-1j * theta[None] * tap)
    mean = sum(np.exp(1j * theta * q) for q in range(REFINE)) / REFINE
    step = (np.exp(1j * theta * (REFINE - 1)) - np.exp(-1j * theta)) / REFINE
    gx = np.stack([gamma, gamma * mean, gamma * step])
    out["gx"] = np.stack([gx.real, gx.imag])
    turns = (np.arange(nfx)[:, None] * fx[None, :]) % nfx
    out["ex"] = np.stack([np.cos(turns * 2 * np.pi / nfx), np.sin(turns * 2 * np.pi / nfx)])
    out["e4"] = out["ex"][:, ::REFINE]
    fz, imag, wz = z_slots(nfz)
    phi = 2 * np.pi * fz / nfz
    psi = np.where(imag, -1j, 1.0)
    gz = psi * np.exp(-1j * phi[None] * tap)
    gz = np.stack([gz, gz * (np.exp(1j * phi) - 1.0)])
    out["gz"] = np.stack([gz.real, gz.imag])
    coarse_z = nfz // REFINE
    turns = (REFINE * np.arange(coarse_z)[:, None] * fz[None, :]) % nfz
    zz = np.stack([np.cos(turns * 2 * np.pi / nfz), np.sin(turns * 2 * np.pi / nfz)])
    out["zz"] = np.tile(zz, (1, rows, 1))
    turns = (fz[:, None] * np.arange(nfz)[None, :]) % nfz
    angle = turns * 2 * np.pi / nfz
    iz = (wz / nfz)[:, None] * np.where(imag[:, None], -np.sin(angle), np.cos(angle))
    hi, lo = halves_np(iz)
    out["iz"] = np.concatenate(
        [np.concatenate([hi, lo], 1), np.concatenate([hi, np.zeros_like(lo)], 1)], 0
    )
    rz = iz.reshape(nfz, coarse_z, REFINE).mean(2)
    dz = (iz[:, REFINE - 1 :: REFINE] - np.roll(iz, 1, 1)[:, ::REFINE]) / REFINE
    eye = np.eye(rows)
    for name, mat in (("rz", rz), ("dz", dz)):
        big = np.einsum("ij,kz->ikjz", eye, mat).reshape(rows * nfz, rows * coarse_z)
        hi, lo = halves_np(big)
        out[name] = np.stack([hi, lo])
    coarse = np.arange(quarter)
    turns = (coarse[:, None] * coarse[None, :]) % quarter
    angle = turns * 2 * np.pi / quarter
    fwd = np.concatenate([np.cos(angle), -np.sin(angle)], 0)
    fwd[quarter] = 1.0
    hi, lo = halves_np(fwd)
    out["fx"] = np.concatenate([hi, hi, lo], 1)
    mu = 4 * np.sin(np.pi * fx / nfx)[:, None] ** 2 + 4 * np.sin(np.pi * fz / nfz)[None, :] ** 2
    root = 1 + mu / 2 - np.sqrt(mu + mu * mu / 4)
    root = np.where(mu == 0, 0.0, root)
    kappa = -root / (1 - root**2)
    per = 1 / (1 - root**nfy)
    dx = np.exp(1j * theta) - 1
    own = dx.real.copy()
    other = np.concatenate(
        [-dx.imag[:quarter], dx.imag[:quarter], -dx.imag[2 * quarter : 3 * quarter],
         dx.imag[2 * quarter : 3 * quarter]]
    )
    own[0], own[quarter], own[2 * quarter], own[3 * quarter] = 0.0, -2.0, -1.0, 0.0
    other[[0, quarter, 2 * quarter, 3 * quarter]] = 0.0
    wide = np.ones((1, nfz))
    out["planes"] = np.stack([root, kappa, per, own[:, None] * wide, other[:, None] * wide])
    out["planes"] = out["planes"].astype(np.float32)
    flat = [out.pop("gx").reshape(-1, nfx), out.pop("ex").reshape(-1, nfx)]
    flat += [out.pop("e4").reshape(-1, nfx)]
    flat += [np.concatenate([part[0], part[1]], -1).reshape(-1, nfx) for part in (out.pop("gz"), out.pop("zz"))]
    out["bank"] = np.concatenate(flat, 0).astype(np.float32)
    return out


def find_tiles(me, lists, owner, local_tiles, farm_count, pairs):
    found, shifts = [], []
    for shift in range(farm_count):
        target = me ^ shift
        tile = jnp.int32(0)
        for nest in range(farm_count):
            for pair in range(pairs):
                entry = lists[nest, pair]
                hit = (owner[nest] == target) & (entry // local_tiles == me)
                tile = jnp.where(hit, entry, tile)
        found.append(tile - me * local_tiles)
    for pair in range(pairs):
        tile = jnp.int32(0)
        for nest in range(farm_count):
            tile = jnp.where(owner[nest] == me, lists[nest, pair], tile)
        shifts.append((tile // local_tiles) ^ me)
    return found, shifts


def swap_blocks(value, rows, width):
    lane = lax.broadcasted_iota(jnp.int32, value.shape, 1) // width
    sub = lax.broadcasted_iota(jnp.int32, value.shape, 0) % rows
    delta = lane - sub
    result = value
    lanes = value.shape[1]
    height = value.shape[0]
    for shift in range(1, rows):
        for sign in (1, -1):
            amount = sign * shift
            moved = pltpu.roll(value, (amount * width) % lanes, 1)
            moved = pltpu.roll(moved, (-amount) % height, 0)
            result = jnp.where(delta == amount, moved, result)
    return result


def pick_kernel(local_tiles, farm_count, pairs, lists_any, owner_any, tiles, *refs):
    info, outs = refs[0], refs[1 : 1 + farm_count]
    lists, owner, sems = refs[1 + farm_count :]
    reads = [
        pltpu.make_async_copy(lists_any, lists, sems.at[farm_count]),
        pltpu.make_async_copy(owner_any, owner, sems.at[farm_count + 1]),
    ]
    for copy in reads:
        copy.start()
    for copy in reads:
        copy.wait()
    me = lax.axis_index("farm")
    found, shifts = find_tiles(me, lists, owner, local_tiles, farm_count, pairs)
    copies = []
    for shift in range(farm_count):
        copies.append(
            pltpu.make_async_copy(tiles.at[found[shift]], outs[shift], sems.at[shift])
        )
        copies[-1].start()
    for shift in range(farm_count):
        info[shift] = found[shift]
    for pair in range(pairs):
        info[farm_count + pair] = shifts[pair]
    info[farm_count + pairs] = lax.axis_index(GROUP)
    for copy in copies:
        copy.wait()


def arrange_kernel(farm_count, pairs, info, gate, *refs):
    tiles, out, stage = refs[:farm_count], refs[farm_count], refs[farm_count + 1]
    for shift in range(farm_count):
        stage[shift] = tiles[farm_count - 1 - shift][...]
    rows = stage.shape[1]
    channels, width_x, lanes = out.shape
    edge = width_x // pairs
    per = lanes // rows
    row_lanes = edge * per
    for pair in range(pairs):
        tile = stage[info[farm_count + pair]]
        for channel in range(channels):
            for part in range(edge * per // (2 * lanes)):
                base = channel * row_lanes + 2 * part * lanes
                block = jnp.concatenate(
                    [tile[:, base : base + lanes], tile[:, base + lanes : base + 2 * lanes]], 0
                )
                at = pair * edge + 2 * part * rows
                out[channel, at : at + 2 * rows, :] = swap_blocks(block, rows, per)


def prep_kernel(taps, bank, mats, rmats, wu, ww):
    nfx = mats.shape[1]
    quarter = nfx // REFINE
    lanes = wu.shape[0] // 3
    rows = wu.shape[1] // lanes
    per = lanes // rows
    at_ex = 6 * TAPS
    at_e4 = at_ex + 2 * nfx
    at_gz = at_e4 + 2 * quarter
    at_zz = at_gz + 2 * TAPS

    def weighted(at, axis):
        total = taps[axis, 0] * bank[at : at + 1, :]
        for tap in range(1, TAPS):
            total = total + taps[axis, tap] * bank[at + tap : at + tap + 1, :]
        return total

    full = weighted(0, 0) * bank[at_ex : at_ex + nfx, :]
    full = full - weighted(3 * TAPS, 0) * bank[at_ex + nfx : at_ex + 2 * nfx, :]
    hi, lo = halves(full)
    mats[0:nfx, :] = hi
    mats[nfx : 2 * nfx, :] = lo
    for which in (1, 2):
        at = (which - 1) * quarter
        coarse = weighted(which * TAPS, 0) * bank[at_e4 : at_e4 + quarter, :]
        second = bank[at_e4 + quarter : at_e4 + 2 * quarter, :]
        coarse = coarse - weighted((3 + which) * TAPS, 0) * second
        hi, lo = halves(coarse)
        rmats[0, at : at + quarter, :] = hi
        rmats[1, at : at + quarter, :] = lo
    band = lax.broadcasted_iota(jnp.int32, (lanes, lanes), 0) // per
    for which, target in ((0, wu), (1, ww)):
        value = weighted(at_gz + which * TAPS, 2) * bank[at_zz : at_zz + lanes, :]
        value = value[:, 0:lanes] + value[:, lanes : 2 * lanes]
        for row in range(rows):
            hi, lo = halves(jnp.where(band == row, value, 0.0))
            at = row * lanes
            target[0:lanes, at : at + lanes] = hi
            target[lanes : 2 * lanes, at : at + lanes] = hi
            target[2 * lanes : 3 * lanes, at : at + lanes] = lo


def solve_kernel(farm_count, pairs, groups, info, taps, *refs):
    pieces = refs[:groups]
    (fx, wu_any, ww_any, planes_any, rmats, rz, dz, tiles, spectrum) = refs[groups : groups + 9]
    outs = refs[groups + 9 : groups + 9 + farm_count]
    base = refs[groups + 9 + farm_count]
    (data, wu, ww, planes, left, field, mean_p, step_p, fresh, out_stage, zero_add, shelf, sems) = refs[
        groups + 10 + farm_count :
    ]
    take = pltpu.make_async_copy(tiles, shelf, sems.at[groups + 3])
    take.start()
    group = info[farm_count + pairs]
    copies = []
    for shift in range(groups):
        copies.append(
            pltpu.make_async_copy(pieces[shift], data.at[group ^ shift], sems.at[shift])
        )
    weights = [
        pltpu.make_async_copy(wu_any, wu, sems.at[groups]),
        pltpu.make_async_copy(ww_any, ww, sems.at[groups + 1]),
        pltpu.make_async_copy(planes_any, planes, sems.at[groups + 2]),
    ]
    for copy in copies + weights:
        copy.start()
    for copy in copies:
        copy.wait()
    channels, width_x, lanes = data.shape[1:]
    rows = wu.shape[1] // lanes
    per = lanes // rows
    coarse_y = groups * rows
    fine_y = coarse_y * REFINE
    own_fine = rows * REFINE
    coarse_rows = fx.shape[0]

    for block in range(groups):
        hi_lo = [halves(data[block, channel]) for channel in range(3)]
        hi = jnp.concatenate([pair[0] for pair in hi_lo], 1)
        lo = jnp.concatenate([pair[1] for pair in hi_lo], 1)
        turned = mm(fx[...], jnp.concatenate([hi, lo, hi], 0))
        for channel in range(3):
            hi, lo = halves(turned[:, channel * lanes : (channel + 1) * lanes])
            at = block * coarse_rows
            left[channel, at : at + coarse_rows, :] = jnp.concatenate([hi, lo, hi], 1)
    for copy in weights:
        copy.wait()
    chunk = min(groups, 4)
    for channel in range(3):
        weight = ww if channel == 2 else wu
        for block in range(0, groups, chunk):
            at = block * coarse_rows
            value = mm(left[channel, at : at + chunk * coarse_rows, :], weight[...])
            for inner in range(chunk):
                for row in range(rows):
                    field[channel, (block + inner) * rows + row] = value[
                        inner * coarse_rows : (inner + 1) * coarse_rows,
                        row * lanes : (row + 1) * lanes,
                    ]

    sums = jnp.concatenate(
        [jnp.sum(data[block, 1], axis=0, keepdims=True) for block in range(groups)], 0
    )
    total_z = taps[2, 0]
    for tap in range(1, TAPS):
        total_z = total_z + taps[2, tap]
    sums = sums * total_z
    shape = (groups, lanes)
    coarse_id = rows * lax.broadcasted_iota(jnp.int32, shape, 0)
    coarse_id = coarse_id + lax.broadcasted_iota(jnp.int32, shape, 1) // per
    corner = (lax.broadcasted_iota(jnp.int32, (8, lanes), 0) == 0) & (
        lax.broadcasted_iota(jnp.int32, (8, lanes), 1) == 0
    )
    for index in range(own_fine + 1):
        at = own_fine * group - 1 + index
        weight = jnp.zeros(shape, F32)
        for tap in range(TAPS):
            gap = (at - REFINE * coarse_id + 2 - tap) & (fine_y - 1)
            saw = 0.5 - (2 * gap + 1).astype(F32) * (0.5 / fine_y)
            weight = weight + taps[1, tap] * saw
        value = jnp.sum(jnp.sum(weight * sums, axis=1, keepdims=True), axis=0, keepdims=True)
        zero_add[index] = jnp.where(corner, value, 0.0)

    take.wait()
    give = pltpu.make_async_copy(shelf, base, sems.at[groups + 4])
    give.start()
    first = rows * group

    def at_row(offset):
        return (first + offset) & (coarse_y - 1)

    def tap_y(offset):
        return taps[1, offset + 2]

    half_rows = coarse_rows // 2

    def sweep(step, carry):
        low = pl.multiple_of(8 * step, 8)
        spots = (low, half_rows + low)
        slots = [pl.multiple_of(part * half_rows + low, 8) for part in range(4)]

        def plane(which, part):
            return planes[which, pl.ds(slots[part], 8), :]

        def coarse(channel, row, side):
            return field[channel, row, pl.ds(spots[side], 8), :]

        root = [plane(0, part) for part in range(4)]
        quad = [value * value for value in root]
        quad = [value * value for value in quad]

        def horner(offset, sign):
            def body(i, acc):
                row = at_row(offset + sign * (coarse_y - 1 - i))
                loaded = [[coarse(c, row, side) for side in range(2)] for c in range(3)]
                return tuple(
                    acc[c * 4 + part] * quad[part] + loaded[c][part % 2]
                    for c in range(3)
                    for part in range(4)
                )

            zeros = tuple(jnp.zeros((8, lanes), F32) for _ in range(12))
            return lax.fori_loop(0, coarse_y, body, zeros, unroll=4)

        below = horner(-2, -1)
        above = horner(rows + 1, 1)
        near = list(range(-1, rows + 1))
        near_u = {m: [coarse(0, at_row(m), side) for side in range(2)] for m in near}
        near_v = {m: [coarse(1, at_row(m), side) for side in range(2)] for m in near}
        near_w = {m: [coarse(2, at_row(m), side) for side in range(2)] for m in near}
        for part in range(4):
            side = part % 2
            mate = part + 1 if side == 0 else part - 1
            r = root[part]
            kappa, per_wrap = plane(1, part), plane(2, part)
            own, other = plane(3, part), plane(4, part)
            turn = {
                m: own * near_u[m][side] + other * near_u[m][1 - side] + near_w[m][side]
                for m in near
            }
            lift = {m: near_v[m][side] for m in near}
            poly_a2 = tap_y(-2) * r + tap_y(-1)
            poly_a1 = poly_a2
            for e in range(0, 4):
                poly_a1 = poly_a1 * r + tap_y(e)
            poly_a = (poly_a1 * r + tap_y(4)) * r + tap_y(5)
            poly_b2 = tap_y(5) * r + tap_y(4)
            poly_b1 = poly_b2
            for e in (3, 2, 1, 0):
                poly_b1 = poly_b1 * r + tap_y(e)
            poly_b = (poly_b1 * r + tap_y(-1)) * r + tap_y(-2)
            far_scale = per_wrap * r * r
            turn_l = own * below[part] + other * below[mate] + below[8 + part]
            turn_r = own * above[part] + other * above[mate] + above[8 + part]
            drop = r - 1.0
            start = far_scale * poly_a * (turn_l + drop * below[4 + part])
            start = start + poly_a1 * turn[-1] + (drop * poly_a1 + tap_y(4)) * lift[-1]
            start = start + poly_a2 * turn[0] + (drop * poly_a2 + tap_y(0)) * lift[0]
            end = far_scale * poly_b * (r * turn_r - drop * above[4 + part])
            end = end + r * poly_b1 * turn[rows] - (drop * poly_b1 + tap_y(0)) * lift[rows]
            end = end + r * poly_b2 * turn[rows - 1] - (drop * poly_b2 + tap_y(4)) * lift[rows - 1]
            source = []
            for j in range(own_fine):
                m0, q = j // REFINE, j % REFINE
                total = None
                for m in (m0 - 1, m0, m0 + 1):
                    e = j - REFINE * m
                    if -2 <= e <= 5:
                        term = tap_y(e) * turn[m]
                        total = term if total is None else total + term
                    if -3 <= e <= 5:
                        scale = (tap_y(e + 1) if e < 5 else 0.0) - (tap_y(e) if e > -3 else 0.0)
                        total = total + scale * lift[m] if total is not None else scale * lift[m]
                source.append(total)
            ahead = [start]
            for j in range(own_fine):
                ahead.append(ahead[-1] * r + source[j])
            back = end
            pressure = [None] * (own_fine + 1)
            pressure[own_fine] = kappa * (ahead[own_fine] + back)
            for j in range(own_fine - 1, -1, -1):
                back = r * (back + source[j])
                pressure[j] = kappa * (ahead[j] + back)
            spot = pl.ds(slots[part], 8)
            for j in range(own_fine):
                spectrum[j, spot, :] = pressure[j + 1]
            for m in range(rows):
                at = REFINE * m
                total = pressure[at + 1]
                for q in range(1, REFINE):
                    total = total + pressure[at + 1 + q]
                mean_p[m, spot, :] = total * (1.0 / REFINE)
                step_p[m, spot, :] = (pressure[at + REFINE] - pressure[at]) * (1.0 / REFINE)
        return carry

    lax.fori_loop(0, half_rows // 8, sweep, 0)
    for j in range(own_fine):
        spectrum[j, 0:8, :] = spectrum[j, 0:8, :] + zero_add[j + 1]
    for m in range(rows):
        at = REFINE * m
        total = zero_add[at + 1]
        for q in range(1, REFINE):
            total = total + zero_add[at + 1 + q]
        mean_p[m, 0:8, :] = mean_p[m, 0:8, :] + total * (1.0 / REFINE)
        step = (zero_add[at + REFINE] - zero_add[at]) * (1.0 / REFINE)
        step_p[m, 0:8, :] = step_p[m, 0:8, :] + step

    def left_three(count, stacked):
        hi, lo = halves(stacked)
        value = mm(rmats[0, 0:count, :], hi) + mm(rmats[0, 0:count, :], lo)
        return value + mm(rmats[1, 0:count, :], hi)

    def right_three(value, table):
        hi, lo = halves(value)
        return mm(hi, table[0]) + mm(lo, table[0]) + mm(hi, table[1])

    smooth = left_three(2 * width_x, jnp.concatenate([mean_p[m] for m in range(rows)], 1))
    slope = left_three(width_x, jnp.concatenate([step_p[m] for m in range(rows)], 1))
    mean_x, step_x = smooth[0:width_x], smooth[width_x : 2 * width_x]
    through = right_three(jnp.concatenate([step_x, slope, mean_x], 0), rz)
    part_w = right_three(mean_x, dz)
    change = [
        -through[0:width_x],
        -through[width_x : 2 * width_x],
        -part_w,
        through[2 * width_x : 3 * width_x],
    ]

    def band(axis):
        quarter = 1.0 / REFINE
        return (
            (taps[axis, 6] + taps[axis, 7]) * quarter,
            (taps[axis, 2] + taps[axis, 3] + taps[axis, 4] + taps[axis, 5]) * quarter,
            (taps[axis, 0] + taps[axis, 1]) * quarter,
        )

    lane = lax.broadcasted_iota(jnp.int32, (width_x, lanes), 1)
    previous = (group + groups - 1) & (groups - 1)
    following = (group + 1) & (groups - 1)
    for channel in range(channels):
        here = data[group, channel]
        before, after = data[previous, channel], data[following, channel]
        lag, mid, lead = band(1)
        low = jnp.where(lane < per, pltpu.roll(before, per, 1), pltpu.roll(here, per, 1))
        high = jnp.where(
            lane >= lanes - per, pltpu.roll(after, lanes - per, 1), pltpu.roll(here, lanes - per, 1)
        )
        value = mid * here + lag * low + lead * high
        lag, mid, lead = band(2)
        spot = lane % per
        low = jnp.where(spot == 0, pltpu.roll(value, lanes - per + 1, 1), pltpu.roll(value, 1, 1))
        high = jnp.where(
            spot == per - 1, pltpu.roll(value, per - 1, 1), pltpu.roll(value, lanes - 1, 1)
        )
        value = mid * value + lag * low + lead * high
        lag, mid, lead = band(0)
        value = (
            mid * value
            + lag * pltpu.roll(value, 1, 0)
            + lead * pltpu.roll(value, width_x - 1, 0)
        )
        fresh[channel] = value + change[channel]
    shifts = [info[farm_count + pair] for pair in range(pairs)]
    edge = width_x // pairs
    row_lanes = edge * per
    for pair in range(pairs):
        for channel in range(channels):
            for part in range(row_lanes // (2 * lanes)):
                at = pair * edge + 2 * part * rows
                block = swap_blocks(fresh[channel, at : at + 2 * rows, :], rows, per)
                base = channel * row_lanes + 2 * part * lanes
                out_stage[shifts[pair], :, base : base + lanes] = block[0:rows]
                out_stage[shifts[pair], :, base + lanes : base + 2 * lanes] = block[rows:]
    for shift in range(farm_count):
        outs[shift][...] = out_stage[shift]
    give.wait()


def inverse_kernel(iz, mats, spectrum, out):
    count, nfx, lanes = spectrum.shape
    for at in range(0, count, 2):
        value = []
        for row in (at, at + 1):
            hi, lo = halves(spectrum[row])
            both = mm(jnp.concatenate([hi, lo], 1), iz[...])
            value.append(both[:, 0:lanes] + both[:, lanes : 2 * lanes])
        hi, lo = halves(jnp.concatenate(value, 1))
        upper = mm(mats[...], hi)
        final = upper[0:nfx] + upper[nfx : 2 * nfx] + mm(mats[0:nfx, :], lo)
        for row in range(2):
            out[:, at + row, :] = final[:, row * lanes : (row + 1) * lanes]


def patch_kernel(farm_count, info, base, *refs):
    tiles, out, sems = refs[:farm_count], refs[farm_count], refs[farm_count + 1]
    copies = []
    for shift in range(farm_count):
        copies.append(
            pltpu.make_async_copy(
                tiles[farm_count - 1 - shift], out.at[info[shift]], sems.at[shift]
            )
        )
        copies[-1].start()
    for copy in copies:
        copy.wait()


def in_vmem():
    return pl.BlockSpec(memory_space=pltpu.VMEM)


def in_smem():
    return pl.BlockSpec(memory_space=pltpu.SMEM)


def anywhere():
    return pl.BlockSpec(memory_space=pl.ANY)


def in_hbm():
    return pl.BlockSpec(memory_space=pltpu.HBM)


def keep_hbm(value):
    return pltpu.with_memory_space_constraint(value, pltpu.HBM)


def limit(mib):
    return pltpu.CompilerParams(vmem_limit_bytes=mib << 20)


def cost(flops, nbytes):
    return pl.CostEstimate(flops=flops, bytes_accessed=nbytes, transcendentals=0)


def flip(value, axis, bits):
    count = lax.axis_size(axis)
    return lax.ppermute(value, axis, [(i, i ^ bits) for i in range(count)])


def fast_local(coarse_tiles, prolong_taps, tile_lists, nest_owner):
    farm_count = lax.axis_size("farm")
    groups = lax.axis_size(GROUP)
    local_tiles, rows, row_width = coarse_tiles.shape
    pairs = tile_lists.shape[1]
    edge = row_width // (CH * TILE_Z)
    width_x = pairs * edge
    lanes = rows * TILE_Z
    own_fine = rows * REFINE
    table = tables(NFX, NFY, NFZ, rows)
    const = {key: jnp.asarray(value) for key, value in table.items()}
    bind = lambda kernel, *sizes: (lambda *refs: kernel(*sizes, *refs))
    tile_shape = jax.ShapeDtypeStruct((rows, row_width), F32)

    info, *picked = pl.pallas_call(
        bind(pick_kernel, local_tiles, farm_count, pairs),
        name="pick",
        out_shape=[jax.ShapeDtypeStruct((farm_count + pairs + 1,), jnp.int32)]
        + [tile_shape] * farm_count,
        in_specs=[in_hbm()] * 3,
        out_specs=[in_smem()] + [in_vmem()] * farm_count,
        scratch_shapes=[
            pltpu.SMEM(tile_lists.shape, jnp.int32),
            pltpu.SMEM(nest_owner.shape, jnp.int32),
            pltpu.SemaphoreType.DMA((farm_count + 2,)),
        ],
        compiler_params=limit(8),
        cost_estimate=cost(0, 1 << 18),
    )(keep_hbm(tile_lists), keep_hbm(nest_owner), keep_hbm(coarse_tiles))
    moved = {s: flip(picked[s], "farm", s) for s in range(farm_count - 1, 0, -1)}
    moved = [picked[0]] + [moved[s] for s in range(1, farm_count)]
    mats, rmats, wu, ww = pl.pallas_call(
        prep_kernel,
        name="prep",
        out_shape=[
            jax.ShapeDtypeStruct((2 * NFX, NFX), BF),
            jax.ShapeDtypeStruct((2, 2 * width_x, NFX), BF),
            jax.ShapeDtypeStruct((3 * lanes, rows * NFZ), BF),
            jax.ShapeDtypeStruct((3 * lanes, rows * NFZ), BF),
        ],
        in_specs=[in_smem(), in_vmem()],
        out_specs=[in_vmem()] * 4,
        compiler_params=limit(8),
        cost_estimate=cost(0, 6 << 20),
    )(prolong_taps, const["bank"])

    piece = pl.pallas_call(
        bind(arrange_kernel, farm_count, pairs),
        name="arrange",
        out_shape=jax.ShapeDtypeStruct((CH, width_x, lanes), F32),
        in_specs=[in_smem(), anywhere()] + [in_vmem()] * farm_count,
        out_specs=in_vmem(),
        scratch_shapes=[pltpu.VMEM((farm_count, rows, row_width), F32)],
        compiler_params=limit(8),
        cost_estimate=cost(0, 1 << 18),
    )(info, rmats, *moved[::-1])
    far_bit, core_bit, near_bit = 4, 2, 1
    held = {0: piece}
    for bits in (near_bit, far_bit, near_bit | far_bit):
        held[bits] = flip(piece, GROUP, bits)
    for bits in (0, near_bit, far_bit, near_bit | far_bit):
        held[bits | core_bit] = flip(held[bits], GROUP, core_bit)

    coarse_rows = 2 * width_x
    coarse_y = groups * rows
    spectrum, *fresh, base = pl.pallas_call(
        bind(solve_kernel, farm_count, pairs, groups),
        name="solve",
        out_shape=[jax.ShapeDtypeStruct((own_fine, NFX, NFZ), F32)]
        + [tile_shape] * farm_count
        + [jax.ShapeDtypeStruct(coarse_tiles.shape, F32)],
        in_specs=[in_smem()] * 2
        + [anywhere()] * groups
        + [in_vmem()]
        + [anywhere()] * 3
        + [in_vmem()] * 3
        + [in_hbm()],
        out_specs=[in_vmem()] * (farm_count + 1) + [in_hbm()],
        scratch_shapes=[
            pltpu.VMEM((groups, CH, width_x, lanes), F32),
            pltpu.VMEM((3 * lanes, rows * NFZ), BF),
            pltpu.VMEM((3 * lanes, rows * NFZ), BF),
            pltpu.VMEM(const["planes"].shape, F32),
            pltpu.VMEM((3, groups * coarse_rows, 3 * lanes), BF),
            pltpu.VMEM((3, coarse_y, coarse_rows, NFZ), F32),
            pltpu.VMEM((rows, NFX, NFZ), F32),
            pltpu.VMEM((rows, NFX, NFZ), F32),
            pltpu.VMEM((CH, width_x, lanes), F32),
            pltpu.VMEM((farm_count, rows, row_width), F32),
            pltpu.VMEM((own_fine + 1, 8, lanes), F32),
            pltpu.VMEM(coarse_tiles.shape, F32),
            pltpu.SemaphoreType.DMA((groups + 5,)),
        ],
        compiler_params=limit(40),
        cost_estimate=cost(4 << 30, 8 << 20),
    )(
        info, prolong_taps,
        *[held[s] for s in range(groups)],
        const["fx"], wu, ww, const["planes"], rmats, const["rz"], const["dz"],
        keep_hbm(coarse_tiles),
    )
    returned = [fresh[0]] + [flip(fresh[s], "farm", s) for s in range(1, farm_count)]

    half = 8
    pressure = pl.pallas_call(
        inverse_kernel,
        name="inverse",
        out_shape=jax.ShapeDtypeStruct((NFX, own_fine, NFZ), F32),
        grid=(own_fine // half,),
        in_specs=[
            pl.BlockSpec((2 * NFZ, 2 * NFZ), lambda i: (0, 0)),
            pl.BlockSpec((2 * NFX, NFX), lambda i: (0, 0)),
            pl.BlockSpec((half, NFX, NFZ), lambda i: (i, 0, 0)),
        ],
        out_specs=pl.BlockSpec((NFX, half, NFZ), lambda i: (0, i, 0)),
        compiler_params=limit(24),
        cost_estimate=cost(4 << 30, 4 << 20),
    )(const["iz"], mats, spectrum)

    updated = pl.pallas_call(
        bind(patch_kernel, farm_count),
        name="patch",
        out_shape=jax.ShapeDtypeStruct(coarse_tiles.shape, F32),
        in_specs=[in_smem(), in_hbm()] + [in_vmem()] * farm_count,
        out_specs=in_hbm(),
        scratch_shapes=[pltpu.SemaphoreType.DMA((farm_count,))],
        input_output_aliases={1: 0},
        compiler_params=limit(8),
        cost_estimate=cost(0, 1 << 18),
    )(info, base, *returned[::-1])
    return updated, pressure[None]


def fits_fast(mesh):
    return dict(mesh.shape) == {"farm": 4, "nx": 4, "ny": 2}


def solution(mesh):
    def body(coarse_tiles, prolong_taps, tile_lists, nest_owner):
        rows, row_width = coarse_tiles.shape[1:]
        edge = row_width // (CH * TILE_Z)
        dense = rows * TILE_Z == NFZ and edge % (2 * rows) == 0
        whole = tile_lists.shape[1] * edge * REFINE == NFX
        if fits_fast(mesh) and dense and whole:
            return fast_local(coarse_tiles, prolong_taps, tile_lists, nest_owner)
        return local(coarse_tiles, prolong_taps, tile_lists, nest_owner)

    return jax.shard_map(
        body,
        mesh=mesh,
        in_specs=(P("farm", GROUP, None), P(), P(), P()),
        out_specs=(P("farm", GROUP, None), P("farm", None, GROUP, None)),
        check_vma=False,
    )
```

```python
import math

import jax
import jax.numpy as jnp
import numpy as np
from jax import lax
from jax.experimental import pallas as pl
from jax.experimental.pallas import tpu as pltpu
from jax.sharding import PartitionSpec as P

TILE_Z = 32
REFINE = 4
TAPS = 8
CH = 4
NFX = 256
NFY = 128
NFZ = 128


exact_mode = lax.Precision.HIGHEST


def with_halo(block, sides, width):
    for axis, dim in sides:
        count = lax.axis_size(axis)
        forward = [(i, i + 1) for i in range(count - 1)]
        forward.append((count - 1, 0))
        backward = [(target, source) for source, target in forward]
        low = lax.ppermute(
            lax.slice_in_dim(block, block.shape[dim] - width, None, axis=dim), axis, forward
        )
        high = lax.ppermute(lax.slice_in_dim(block, 0, width, axis=dim), axis, backward)
        block = jnp.concatenate([low, block, high], axis=dim)
    return block


def prolong_matrix(taps_row, fine_count, coarse_count, fine_start, coarse_start, period):
    fine_index = fine_start + jnp.arange(fine_count, dtype=jnp.int32)
    coarse_index = coarse_start + jnp.arange(coarse_count, dtype=jnp.int32)
    offset = jnp.mod(fine_index[:, None] - REFINE * coarse_index[None, :] + 2, period)
    tap_match = offset[:, :, None] == jnp.arange(TAPS, dtype=jnp.int32)[None, None, :]
    return jnp.sum(
        jnp.where(tap_match, taps_row[None, None, :], jnp.zeros((), jnp.float32)), axis=2
    )


def eigen_part(freq_start, freq_count, length):
    freq_index = (freq_start + jnp.arange(freq_count, dtype=jnp.int32)).astype(jnp.float32)
    return 4.0 * jnp.sin(freq_index * (math.pi / length)) ** 2


def slot_lists(tile_lists, nest_owner, slot_ids):
    owner_match = nest_owner[None, :] == slot_ids[:, None]
    return jnp.sum(jnp.where(owner_match[:, :, None], tile_lists[None, :, :], 0), axis=1)


def wave_tables(length):
    index_row = jnp.arange(length, dtype=jnp.int32)
    turns = jnp.mod(index_row[:, None] * index_row[None, :], length).astype(jnp.float32)
    phase_angle = turns * (2.0 * math.pi / length)
    return (jnp.cos(phase_angle), jnp.sin(phase_angle))


def apply_along(matrix, values, axis_id):
    moved = jnp.tensordot(matrix, values, axes=([1], [axis_id]), precision=exact_mode)
    return jnp.moveaxis(moved, 0, axis_id)


def forward_pair(real_part, imag_part, cosines, sines, axis_id):
    return (
        apply_along(cosines, real_part, axis_id) + apply_along(sines, imag_part, axis_id),
        apply_along(cosines, imag_part, axis_id) - apply_along(sines, real_part, axis_id),
    )


def inverse_pair(real_part, imag_part, cosines, sines, axis_id, length):
    return (
        (apply_along(cosines, real_part, axis_id) - apply_along(sines, imag_part, axis_id))
        / length,
        (apply_along(sines, real_part, axis_id) + apply_along(cosines, imag_part, axis_id))
        / length,
    )


def to_real_space(real_part, imag_part, cos_x, sin_x, cos_z, sin_z):
    real_z, imag_z = inverse_pair(real_part, imag_part, cos_z, sin_z, 2, NFZ)
    return (apply_along(cos_x, real_z, 0) - apply_along(sin_x, imag_z, 0)) / NFX


def local(coarse_tiles, prolong_taps, tile_lists, nest_owner):
    farm_count = lax.axis_size("farm")
    farm_index = lax.axis_index("farm")
    groups = lax.axis_size(("nx", "ny"))
    group_index = lax.axis_index(("nx", "ny"))
    local_tiles, row_count, row_width = coarse_tiles.shape
    tile_edge = row_width // (CH * TILE_Z)
    pair_count = tile_lists.shape[1]
    slot_ids = jnp.arange(farm_count, dtype=jnp.int32)
    slot_tiles = slot_lists(tile_lists, nest_owner, slot_ids)
    owned_ids = farm_index * local_tiles + jnp.arange(local_tiles, dtype=jnp.int32)
    selector = (slot_tiles[:, :, None] == owned_ids[None, None, :]).astype(jnp.float32)
    send_pick = jnp.sum(selector, axis=1)
    flat_tiles = coarse_tiles.reshape(local_tiles, row_count * row_width)
    outgoing = jnp.dot(send_pick, flat_tiles, precision=exact_mode)
    incoming = lax.all_to_all(
        outgoing.reshape(farm_count, row_count, row_width),
        "farm",
        split_axis=0,
        concat_axis=0,
        tiled=True,
    )
    my_tiles = slot_tiles[farm_index]
    home_index = my_tiles // local_tiles
    order_pick = (home_index[:, None] == slot_ids[None, :]).astype(jnp.float32)
    nest_rows = jnp.dot(
        order_pick, incoming.reshape(farm_count, row_count * row_width), precision=exact_mode
    )
    nest_rows = nest_rows.reshape(pair_count, row_count, row_width)
    framed = with_halo(nest_rows, ((("nx", "ny"), 1),), 1)
    width_x = pair_count * tile_edge
    coarse = framed.reshape(pair_count, row_count + 2, CH, tile_edge, TILE_Z).transpose(
        2, 0, 3, 1, 4
    )
    coarse = coarse.reshape(CH, width_x, row_count + 2, TILE_Z)
    fine_rows = REFINE * row_count
    matrix_x = prolong_matrix(prolong_taps[0], NFX, width_x, 0, 0, NFX)
    matrix_y = prolong_matrix(
        prolong_taps[1],
        fine_rows + 1,
        row_count + 2,
        fine_rows * group_index,
        row_count * group_index - 1,
        NFY,
    )
    matrix_z = prolong_matrix(prolong_taps[2], NFZ, TILE_Z, 0, 0, NFZ)
    refined = apply_along(matrix_x, coarse, 1)
    refined = apply_along(matrix_z, refined, 3)
    refined = apply_along(matrix_y, refined, 2)
    own_rows = refined[:, :, :fine_rows, :]
    spread = (
        jnp.roll(own_rows[0], -1, 0)
        - own_rows[0]
        + (refined[1, :, 1:, :] - own_rows[1])
        + (jnp.roll(own_rows[2], -1, 2) - own_rows[2])
    )
    cos_y, sin_y = wave_tables(NFY)
    cos_z, sin_z = wave_tables(NFZ)
    ahead_cos, ahead_sin = wave_tables(NFX)
    behind_cos, behind_sin = (ahead_cos, ahead_sin)
    real_x = apply_along(ahead_cos, spread, 0)
    imag_x = -apply_along(ahead_sin, spread, 0)
    real_xz, imag_xz = forward_pair(real_x, imag_x, cos_z, sin_z, 2)
    columns = lax.all_to_all(
        jnp.stack([real_xz, imag_xz]), ("nx", "ny"), split_axis=1, concat_axis=2, tiled=True
    )
    span = ahead_cos.shape[0] // groups
    real_y, imag_y = forward_pair(columns[0], columns[1], cos_y, sin_y, 1)
    eigen_y = eigen_part(0, NFY, NFY)
    eigen_z = eigen_part(0, NFZ, NFZ)
    eigen_sum = (
        eigen_part(group_index * span, span, NFX)[:, None, None]
        + eigen_y[None, :, None]
        + eigen_z[None, None, :]
    )
    nonzero = eigen_sum > 0
    factor = jnp.where(nonzero, -1.0 / jnp.where(nonzero, eigen_sum, 1.0), 0.0)
    real_p = real_y * factor
    imag_p = imag_y * factor
    back_real, back_imag = inverse_pair(real_p, imag_p, cos_y, sin_y, 1, NFY)
    theta = jnp.arange(NFY, dtype=jnp.float32) * (2.0 * math.pi / NFY)
    cos_diff = (1.0 - jnp.cos(theta))[None, :, None]
    sin_diff = jnp.sin(theta)[None, :, None]
    real_g = real_p * cos_diff - imag_p * sin_diff
    imag_g = real_p * sin_diff + imag_p * cos_diff
    grad_real, grad_imag = inverse_pair(real_g, imag_g, cos_y, sin_y, 1, NFY)
    returned = lax.all_to_all(
        jnp.stack([back_real, back_imag, grad_real, grad_imag]),
        ("nx", "ny"),
        split_axis=2,
        concat_axis=1,
        tiled=True,
    )
    pressure = to_real_space(returned[0], returned[1], behind_cos, behind_sin, cos_z, sin_z)
    grad_y = to_real_space(returned[2], returned[3], behind_cos, behind_sin, cos_z, sin_z)
    new_fields = jnp.stack(
        [
            own_rows[0] - (pressure - jnp.roll(pressure, 1, 0)),
            own_rows[1] - grad_y,
            own_rows[2] - (pressure - jnp.roll(pressure, 1, 2)),
            own_rows[3] + pressure,
        ]
    )
    blocks = new_fields.reshape(CH, width_x, REFINE, row_count, REFINE, TILE_Z, REFINE).mean(
        axis=(2, 4, 6)
    )
    restored = blocks.reshape(CH, pair_count, tile_edge, row_count, TILE_Z).transpose(1, 3, 0, 2, 4)
    restored = restored.reshape(pair_count, row_count * row_width)
    returning = jnp.dot(order_pick.T, restored, precision=exact_mode)
    arrived = lax.all_to_all(
        returning.reshape(farm_count, row_count, row_width),
        "farm",
        split_axis=0,
        concat_axis=0,
        tiled=True,
    )
    placed = jnp.dot(
        send_pick.T, arrived.reshape(farm_count, row_count * row_width), precision=exact_mode
    )
    covered = jnp.sum(send_pick, axis=0)
    updated = coarse_tiles * (1.0 - covered)[:, None, None] + placed.reshape(
        local_tiles, row_count, row_width
    )
    return (updated, pressure[None])


BF = jnp.bfloat16
F32 = jnp.float32
GROUP = ("nx", "ny")


def split_np(table):
    hi = jnp.asarray(table, F32).astype(BF)
    return hi


def halves(value):
    hi = value.astype(BF)
    return hi, (value - hi.astype(F32)).astype(BF)


def halves_np(table):
    table = np.asarray(table, np.float32)
    hi = table.astype(BF)
    return hi, (table - hi.astype(np.float32)).astype(BF)


def mm(left, right):
    return jnp.dot(left, right, preferred_element_type=F32)


def x_slots(nfx):
    quarter = nfx // 4
    low = np.arange(quarter)
    freq = np.concatenate([low, low, low + quarter, low + quarter])
    phase = np.concatenate(
        [np.ones(quarter), 1j * np.ones(quarter), np.ones(quarter), 1j * np.ones(quarter)]
    ).astype(np.complex128)
    freq[quarter] = nfx // 2
    phase[quarter] = 1.0
    phase[2 * quarter] = 1.0 - 1.0j
    weight = np.where((freq == 0) | (freq == nfx // 2), 1.0, 2.0)
    return freq, phase, weight


def z_slots(nfz):
    half = nfz // 2
    low = np.arange(half)
    freq = np.concatenate([low, low])
    imag = np.concatenate([np.zeros(half, bool), np.ones(half, bool)])
    freq[half] = half
    imag[half] = False
    weight = np.where((freq == 0) | (freq == half), 1.0, 2.0)
    return freq, imag, weight


def tables(nfx, nfy, nfz, rows):
    out = {}
    quarter = nfx // 4
    fx, phase, wx = x_slots(nfx)
    theta = 2 * np.pi * fx / nfx
    tap = np.arange(TAPS)[:, None] - 2
    gamma = (wx / nfx) * phase * np.exp(-1j * theta[None] * tap)
    mean = sum(np.exp(1j * theta * q) for q in range(REFINE)) / REFINE
    step = (np.exp(1j * theta * (REFINE - 1)) - np.exp(-1j * theta)) / REFINE
    gx = np.stack([gamma, gamma * mean, gamma * step])
    out["gx"] = np.stack([gx.real, gx.imag])
    turns = (np.arange(nfx)[:, None] * fx[None, :]) % nfx
    out["ex"] = np.stack([np.cos(turns * 2 * np.pi / nfx), np.sin(turns * 2 * np.pi / nfx)])
    out["e4"] = out["ex"][:, ::REFINE]
    fz, imag, wz = z_slots(nfz)
    phi = 2 * np.pi * fz / nfz
    psi = np.where(imag, -1j, 1.0)
    gz = psi * np.exp(-1j * phi[None] * tap)
    gz = np.stack([gz, gz * (np.exp(1j * phi) - 1.0)])
    out["gz"] = np.stack([gz.real, gz.imag])
    coarse_z = nfz // REFINE
    turns = (REFINE * np.arange(coarse_z)[:, None] * fz[None, :]) % nfz
    zz = np.stack([np.cos(turns * 2 * np.pi / nfz), np.sin(turns * 2 * np.pi / nfz)])
    out["zz"] = np.tile(zz, (1, rows, 1))
    turns = (fz[:, None] * np.arange(nfz)[None, :]) % nfz
    angle = turns * 2 * np.pi / nfz
    iz = (wz / nfz)[:, None] * np.where(imag[:, None], -np.sin(angle), np.cos(angle))
    hi, lo = halves_np(iz)
    out["iz"] = np.concatenate(
        [np.concatenate([hi, lo], 1), np.concatenate([hi, np.zeros_like(lo)], 1)], 0
    )
    rz = iz.reshape(nfz, coarse_z, REFINE).mean(2)
    dz = (iz[:, REFINE - 1 :: REFINE] - np.roll(iz, 1, 1)[:, ::REFINE]) / REFINE
    eye = np.eye(rows)
    big = [
        np.einsum("ij,kz->ikjz", eye, mat).reshape(rows * nfz, rows * coarse_z) for mat in (rz, dz)
    ]
    out["rz"] = np.stack(halves_np(np.concatenate(big, 1)))
    coarse = np.arange(quarter)
    turns = (coarse[:, None] * coarse[None, :]) % quarter
    angle = turns * 2 * np.pi / quarter
    fwd = np.concatenate([np.cos(angle), -np.sin(angle)], 0)
    fwd[quarter] = 1.0
    hi, lo = halves_np(fwd)
    out["fx"] = np.concatenate([hi, hi, lo], 1)
    mu = 4 * np.sin(np.pi * fx / nfx)[:, None] ** 2 + 4 * np.sin(np.pi * fz / nfz)[None, :] ** 2
    root = 1 + mu / 2 - np.sqrt(mu + mu * mu / 4)
    root = np.where(mu == 0, 0.0, root)
    kappa = -root / (1 - root**2)
    per = 1 / (1 - root**nfy)
    dx = np.exp(1j * theta) - 1
    own = dx.real.copy()
    other = np.concatenate(
        [-dx.imag[:quarter], dx.imag[:quarter], -dx.imag[2 * quarter : 3 * quarter],
         dx.imag[2 * quarter : 3 * quarter]]
    )
    own[0], own[quarter], own[2 * quarter], own[3 * quarter] = 0.0, -2.0, -1.0, 0.0
    other[[0, quarter, 2 * quarter, 3 * quarter]] = 0.0
    wide = np.ones((1, nfz))
    out["planes"] = np.stack([root, kappa, per, own[:, None] * wide, other[:, None] * wide])
    out["planes"] = out["planes"].astype(np.float32)
    flat = [out.pop("gx").reshape(-1, nfx), out.pop("ex").reshape(-1, nfx)]
    flat += [out.pop("e4").reshape(-1, nfx)]
    flat += [np.concatenate([part[0], part[1]], -1).reshape(-1, nfx) for part in (out.pop("gz"), out.pop("zz"))]
    out["bank"] = np.concatenate(flat, 0).astype(np.float32)
    return out


def find_tiles(me, lists, owner, local_tiles, farm_count, pairs):
    found, shifts = [], []
    for shift in range(farm_count):
        target = me ^ shift
        tile = jnp.int32(0)
        for nest in range(farm_count):
            for pair in range(pairs):
                entry = lists[nest, pair]
                hit = (owner[nest] == target) & (entry // local_tiles == me)
                tile = jnp.where(hit, entry, tile)
        found.append(tile - me * local_tiles)
    for pair in range(pairs):
        tile = jnp.int32(0)
        for nest in range(farm_count):
            tile = jnp.where(owner[nest] == me, lists[nest, pair], tile)
        shifts.append((tile // local_tiles) ^ me)
    return found, shifts


def swap_blocks(value, rows, width):
    lane = lax.broadcasted_iota(jnp.int32, value.shape, 1) // width
    sub = lax.broadcasted_iota(jnp.int32, value.shape, 0) % rows
    delta = lane - sub
    result = value
    lanes = value.shape[1]
    height = value.shape[0]
    for shift in range(1, rows):
        for sign in (1, -1):
            amount = sign * shift
            moved = pltpu.roll(value, (amount * width) % lanes, 1)
            moved = pltpu.roll(moved, (-amount) % height, 0)
            result = jnp.where(delta == amount, moved, result)
    return result


def pick_kernel(local_tiles, farm_count, pairs, lists_any, owner_any, tiles, *refs):
    info, outs = refs[0], refs[1 : 1 + farm_count]
    lists, owner, sems = refs[1 + farm_count :]
    reads = [
        pltpu.make_async_copy(lists_any, lists, sems.at[farm_count]),
        pltpu.make_async_copy(owner_any, owner, sems.at[farm_count + 1]),
    ]
    for copy in reads:
        copy.start()
    for copy in reads:
        copy.wait()
    me = lax.axis_index("farm")
    found, shifts = find_tiles(me, lists, owner, local_tiles, farm_count, pairs)
    copies = []
    for shift in range(farm_count):
        copies.append(
            pltpu.make_async_copy(tiles.at[found[shift]], outs[shift], sems.at[shift])
        )
        copies[-1].start()
    for shift in range(farm_count):
        info[shift] = found[shift]
    for pair in range(pairs):
        info[farm_count + pair] = shifts[pair]
    info[farm_count + pairs] = lax.axis_index(GROUP)
    for copy in copies:
        copy.wait()


def arrange_kernel(farm_count, pairs, info, gate, *refs):
    tiles, out, stage = refs[:farm_count], refs[farm_count], refs[farm_count + 1]
    for shift in range(farm_count):
        stage[shift] = tiles[farm_count - 1 - shift][...]
    rows = stage.shape[1]
    channels, width_x, lanes = out.shape
    edge = width_x // pairs
    per = lanes // rows
    row_lanes = edge * per
    for pair in range(pairs):
        tile = stage[info[farm_count + pair]]
        for channel in range(channels):
            for part in range(edge * per // (2 * lanes)):
                base = channel * row_lanes + 2 * part * lanes
                block = jnp.concatenate(
                    [tile[:, base : base + lanes], tile[:, base + lanes : base + 2 * lanes]], 0
                )
                at = pair * edge + 2 * part * rows
                out[channel, at : at + 2 * rows, :] = swap_blocks(block, rows, per)


def prep_kernel(taps, bank, mats, rmats, wu, ww):
    nfx = mats.shape[1]
    quarter = nfx // REFINE
    lanes = wu.shape[0] // 2
    duo = lanes // 2
    at_ex = 6 * TAPS
    at_e4 = at_ex + 2 * nfx
    at_gz = at_e4 + 2 * quarter
    at_zz = at_gz + 2 * TAPS

    def weighted(at, axis):
        total = taps[axis, 0] * bank[at : at + 1, :]
        for tap in range(1, TAPS):
            total = total + taps[axis, tap] * bank[at + tap : at + tap + 1, :]
        return total

    full = weighted(0, 0) * bank[at_ex : at_ex + nfx, :]
    full = full - weighted(3 * TAPS, 0) * bank[at_ex + nfx : at_ex + 2 * nfx, :]
    hi, lo = halves(full)
    mats[0:nfx, :] = hi
    mats[nfx : 2 * nfx, :] = lo
    for which in (1, 2):
        at = (which - 1) * quarter
        coarse = weighted(which * TAPS, 0) * bank[at_e4 : at_e4 + quarter, :]
        second = bank[at_e4 + quarter : at_e4 + 2 * quarter, :]
        coarse = coarse - weighted((3 + which) * TAPS, 0) * second
        hi, lo = halves(coarse)
        rmats[0, at : at + quarter, :] = hi
        rmats[1, at : at + quarter, :] = lo
    band = lax.broadcasted_iota(jnp.int32, (duo, lanes), 0) // (duo // 2)
    for which, target in ((0, wu), (1, ww)):
        value = weighted(at_gz + which * TAPS, 2) * bank[at_zz : at_zz + lanes, :]
        value = value[:, 0:lanes] + value[:, lanes : 2 * lanes]
        for row in range(2):
            hi, lo = halves(jnp.where(band == row, value[0:duo], 0.0))
            at = row * lanes
            target[0:duo, at : at + lanes] = hi
            target[duo:lanes, at : at + lanes] = hi
            target[lanes : lanes + duo, at : at + lanes] = lo
            target[lanes + duo : 2 * lanes, at : at + lanes] = jnp.zeros_like(lo)


def solve_kernel(farm_count, pairs, groups, info, taps, *refs):
    pieces = refs[:groups]
    (fx, wu, ww, planes, rmats, rz, tiles, spectrum) = refs[groups : groups + 8]
    outs = refs[groups + 8 : groups + 8 + farm_count]
    base = refs[groups + 8 + farm_count]
    (left, field, mean_p, step_p, fresh, out_stage, zero_add, shelf, sems) = refs[
        groups + 9 + farm_count :
    ]
    take = pltpu.make_async_copy(tiles, shelf, sems.at[0])
    take.start()
    group = info[farm_count + pairs]
    channels, width_x, lanes = pieces[0].shape
    rows = mean_p.shape[0]
    per = lanes // rows
    coarse_y = groups * rows
    fine_y = coarse_y * REFINE
    own_fine = rows * REFINE
    coarse_rows = fx.shape[0]

    def band(axis):
        quarter = 1.0 / REFINE
        return (
            (taps[axis, 6] + taps[axis, 7]) * quarter,
            (taps[axis, 2] + taps[axis, 3] + taps[axis, 4] + taps[axis, 5]) * quarter,
            (taps[axis, 0] + taps[axis, 1]) * quarter,
        )

    lane = lax.broadcasted_iota(jnp.int32, (width_x, lanes), 1)
    previous = group ^ ((group + groups - 1) & (groups - 1))
    following = group ^ ((group + 1) & (groups - 1))

    def beside(shift, channel):
        value = pieces[1][channel]
        mark = 3
        while mark < groups:
            value = jnp.where(shift == mark, pieces[mark][channel], value)
            mark = 2 * mark + 1
        return value

    for channel in range(channels):
        here = pieces[0][channel]
        before, after = beside(previous, channel), beside(following, channel)
        lag, mid, lead = band(1)
        low = jnp.where(lane < per, pltpu.roll(before, per, 1), pltpu.roll(here, per, 1))
        high = jnp.where(
            lane >= lanes - per, pltpu.roll(after, lanes - per, 1), pltpu.roll(here, lanes - per, 1)
        )
        value = mid * here + lag * low + lead * high
        lag, mid, lead = band(2)
        spot = lane % per
        low = jnp.where(spot == 0, pltpu.roll(value, lanes - per + 1, 1), pltpu.roll(value, 1, 1))
        high = jnp.where(
            spot == per - 1, pltpu.roll(value, per - 1, 1), pltpu.roll(value, lanes - 1, 1)
        )
        value = mid * value + lag * low + lead * high
        lag, mid, lead = band(0)
        value = (
            mid * value
            + lag * pltpu.roll(value, 1, 0)
            + lead * pltpu.roll(value, width_x - 1, 0)
        )
        fresh[channel] = value
    duo = lanes // 2
    front = lax.broadcasted_iota(jnp.int32, (width_x, lanes), 1) < duo
    ahead_half = lax.broadcasted_iota(jnp.int32, (coarse_rows, lanes), 1) < duo
    for block in range(groups):
        doubled = []
        for channel in range(3):
            value = pieces[block][channel]
            turned = pltpu.roll(value, duo, 1)
            doubled += [jnp.where(front, value, turned), jnp.where(front, turned, value)]
        hi, lo = halves(jnp.concatenate(doubled, 1))
        turned = mm(fx[...], jnp.concatenate([hi, lo, hi], 0))
        for channel in range(3):
            for pair in range(2):
                at = (2 * channel + pair) * lanes
                value = turned[:, at : at + lanes]
                hi = value.astype(BF)
                rest = jnp.where(ahead_half, value, value - hi.astype(F32)).astype(BF)
                at = (2 * block + pair) * coarse_rows
                left[channel, at : at + coarse_rows, :] = jnp.concatenate([rest, hi], 1)
    chunk = min(groups, 4)
    for channel in range(3):
        weight = ww if channel == 2 else wu
        for block in range(0, groups, chunk):
            at = 2 * block * coarse_rows
            value = mm(left[channel, at : at + 2 * chunk * coarse_rows, :], weight[...])
            for inner in range(chunk):
                for row in range(rows):
                    at_y = (((group ^ (block + inner)) - group) * rows + row) & (coarse_y - 1)
                    at = (2 * inner + row // 2) * coarse_rows
                    field[channel, at_y] = value[
                        at : at + coarse_rows, (row % 2) * lanes : (row % 2 + 1) * lanes
                    ]

    sums = jnp.concatenate(
        [jnp.sum(pieces[block][1], axis=0, keepdims=True) for block in range(groups)], 0
    )
    total_z = taps[2, 0]
    for tap in range(1, TAPS):
        total_z = total_z + taps[2, tap]
    sums = sums * total_z
    shape = (groups, lanes)
    coarse_id = rows * (lax.broadcasted_iota(jnp.int32, shape, 0) ^ group)
    coarse_id = coarse_id + lax.broadcasted_iota(jnp.int32, shape, 1) // per
    corner = (lax.broadcasted_iota(jnp.int32, (8, lanes), 0) == 0) & (
        lax.broadcasted_iota(jnp.int32, (8, lanes), 1) == 0
    )
    for index in range(own_fine + 1):
        at = own_fine * group - 1 + index
        weight = jnp.zeros(shape, F32)
        for tap in range(TAPS):
            gap = (at - REFINE * coarse_id + 2 - tap) & (fine_y - 1)
            saw = 0.5 - (2 * gap + 1).astype(F32) * (0.5 / fine_y)
            weight = weight + taps[1, tap] * saw
        value = jnp.sum(jnp.sum(weight * sums, axis=1, keepdims=True), axis=0, keepdims=True)
        zero_add[index] = jnp.where(corner, value, 0.0)

    take.wait()
    give = pltpu.make_async_copy(shelf, base, sems.at[1])
    give.start()

    def at_row(offset):
        return offset % coarse_y

    def tap_y(offset):
        return taps[1, offset + 2]

    half_rows = coarse_rows // 2

    def sweep(step, carry):
        low = pl.multiple_of(8 * step, 8)
        spots = (low, half_rows + low)
        slots = [pl.multiple_of(part * half_rows + low, 8) for part in range(4)]

        def plane(which, part):
            return planes[which, pl.ds(slots[part], 8), :]

        def coarse(channel, row, side):
            return field[channel, row, pl.ds(spots[side], 8), :]

        root = [plane(0, part) for part in range(4)]
        quad = [value * value for value in root]
        quad = [value * value for value in quad]

        def horner(i, acc):
            spread = []
            for way, (offset, sign) in enumerate(((-2, -1), (rows + 1, 1))):
                row = at_row(offset + sign * (coarse_y - 1 - i))
                loaded = [[coarse(c, row, side) for side in range(2)] for c in range(3)]
                spread += [
                    acc[12 * way + c * 4 + part] * quad[part] + loaded[c][part % 2]
                    for c in range(3)
                    for part in range(4)
                ]
            return tuple(spread)

        sums_far = tuple(jnp.zeros((8, lanes), F32) for _ in range(24))
        for i in range(coarse_y):
            sums_far = horner(i, sums_far)
        below, above = sums_far[:12], sums_far[12:]
        opening = jnp.where(step == 0, 1.0, 0.0)
        near = list(range(-1, rows + 1))
        near_u = {m: [coarse(0, at_row(m), side) for side in range(2)] for m in near}
        near_v = {m: [coarse(1, at_row(m), side) for side in range(2)] for m in near}
        near_w = {m: [coarse(2, at_row(m), side) for side in range(2)] for m in near}
        for part in range(4):
            side = part % 2
            mate = part + 1 if side == 0 else part - 1
            r = root[part]
            kappa, per_wrap = plane(1, part), plane(2, part)
            own, other = plane(3, part), plane(4, part)
            turn = {
                m: own * near_u[m][side] + other * near_u[m][1 - side] + near_w[m][side]
                for m in near
            }
            lift = {m: near_v[m][side] for m in near}
            poly_a2 = tap_y(-2) * r + tap_y(-1)
            poly_a1 = poly_a2
            for e in range(0, 4):
                poly_a1 = poly_a1 * r + tap_y(e)
            poly_a = (poly_a1 * r + tap_y(4)) * r + tap_y(5)
            poly_b2 = tap_y(5) * r + tap_y(4)
            poly_b1 = poly_b2
            for e in (3, 2, 1, 0):
                poly_b1 = poly_b1 * r + tap_y(e)
            poly_b = (poly_b1 * r + tap_y(-1)) * r + tap_y(-2)
            far_scale = per_wrap * r * r
            turn_l = own * below[part] + other * below[mate] + below[8 + part]
            turn_r = own * above[part] + other * above[mate] + above[8 + part]
            drop = r - 1.0
            start = far_scale * poly_a * (turn_l + drop * below[4 + part])
            start = start + poly_a1 * turn[-1] + (drop * poly_a1 + tap_y(4)) * lift[-1]
            start = start + poly_a2 * turn[0] + (drop * poly_a2 + tap_y(0)) * lift[0]
            end = far_scale * poly_b * (r * turn_r - drop * above[4 + part])
            end = end + r * poly_b1 * turn[rows] - (drop * poly_b1 + tap_y(0)) * lift[rows]
            end = end + r * poly_b2 * turn[rows - 1] - (drop * poly_b2 + tap_y(4)) * lift[rows - 1]
            source = []
            for j in range(own_fine):
                m0, q = j // REFINE, j % REFINE
                total = None
                for m in (m0 - 1, m0, m0 + 1):
                    e = j - REFINE * m
                    if -2 <= e <= 5:
                        term = tap_y(e) * turn[m]
                        total = term if total is None else total + term
                    if -3 <= e <= 5:
                        scale = (tap_y(e + 1) if e < 5 else 0.0) - (tap_y(e) if e > -3 else 0.0)
                        total = total + scale * lift[m] if total is not None else scale * lift[m]
                source.append(total)
            ahead = [start]
            for j in range(own_fine):
                ahead.append(ahead[-1] * r + source[j])
            back = end
            pressure = [None] * (own_fine + 1)
            pressure[own_fine] = kappa * (ahead[own_fine] + back)
            for j in range(own_fine - 1, -1, -1):
                back = r * (back + source[j])
                pressure[j] = kappa * (ahead[j] + back)
            if part == 0:
                pressure = [pressure[j] + opening * zero_add[j] for j in range(own_fine + 1)]
            spot = pl.ds(slots[part], 8)
            for j in range(own_fine):
                spectrum[j, spot, :] = pressure[j + 1]
            for m in range(rows):
                at = REFINE * m
                total = pressure[at + 1]
                for q in range(1, REFINE):
                    total = total + pressure[at + 1 + q]
                mean_p[m, spot, :] = total * (1.0 / REFINE)
                step_p[m, spot, :] = (pressure[at + REFINE] - pressure[at]) * (1.0 / REFINE)
        return carry

    lax.fori_loop(0, half_rows // 8, sweep, 0)
    def left_three(count, stacked):
        hi, lo = halves(stacked)
        value = mm(rmats[0, 0:count, :], hi) + mm(rmats[0, 0:count, :], lo)
        return value + mm(rmats[1, 0:count, :], hi)

    def right_three(value, table):
        hi, lo = halves(value)
        return mm(hi, table[0]) + mm(lo, table[0]) + mm(hi, table[1])

    smooth = left_three(2 * width_x, jnp.concatenate([mean_p[m] for m in range(rows)], 1))
    slope = left_three(width_x, jnp.concatenate([step_p[m] for m in range(rows)], 1))
    mean_x, step_x = smooth[0:width_x], smooth[width_x : 2 * width_x]
    through = right_three(jnp.concatenate([step_x, slope, mean_x], 0), rz)
    part_w = through[2 * width_x : 3 * width_x, lanes:]
    through = through[:, 0:lanes]
    change = [
        -through[0:width_x],
        -through[width_x : 2 * width_x],
        -part_w,
        through[2 * width_x : 3 * width_x],
    ]

    for channel in range(channels):
        fresh[channel] = fresh[channel] + change[channel]
    shifts = [info[farm_count + pair] for pair in range(pairs)]
    edge = width_x // pairs
    row_lanes = edge * per
    for pair in range(pairs):
        for channel in range(channels):
            for part in range(row_lanes // (2 * lanes)):
                at = pair * edge + 2 * part * rows
                block = swap_blocks(fresh[channel, at : at + 2 * rows, :], rows, per)
                base = channel * row_lanes + 2 * part * lanes
                out_stage[shifts[pair], :, base : base + lanes] = block[0:rows]
                out_stage[shifts[pair], :, base + lanes : base + 2 * lanes] = block[rows:]
    for shift in range(farm_count):
        outs[shift][...] = out_stage[shift]
    give.wait()


def inverse_kernel(iz, mats, spectrum, out, middle):
    count, nfx, lanes = spectrum.shape
    for at in range(0, count, 4):
        hi, lo = halves(spectrum[at : at + 4].reshape(4 * nfx, lanes))
        both = mm(jnp.concatenate([hi, lo], 1), iz[...])
        middle[at : at + 4] = (both[:, 0:lanes] + both[:, lanes : 2 * lanes]).reshape(4, nfx, lanes)
    for at in range(0, count, 2):
        hi, lo = halves(jnp.concatenate([middle[at], middle[at + 1]], 1))
        upper = mm(mats[...], hi)
        final = upper[0:nfx] + upper[nfx : 2 * nfx] + mm(mats[0:nfx, :], lo)
        for row in range(2):
            out[:, at + row, :] = final[:, row * lanes : (row + 1) * lanes]


def patch_kernel(farm_count, info, base, *refs):
    tiles, out, sems = refs[:farm_count], refs[farm_count], refs[farm_count + 1]
    copies = []
    for shift in range(farm_count):
        copies.append(
            pltpu.make_async_copy(
                tiles[farm_count - 1 - shift], out.at[info[shift]], sems.at[shift]
            )
        )
        copies[-1].start()
    for copy in copies:
        copy.wait()


def in_vmem():
    return pl.BlockSpec(memory_space=pltpu.VMEM)


def in_smem():
    return pl.BlockSpec(memory_space=pltpu.SMEM)


def anywhere():
    return pl.BlockSpec(memory_space=pl.ANY)


def in_hbm():
    return pl.BlockSpec(memory_space=pltpu.HBM)


def keep_hbm(value):
    return pltpu.with_memory_space_constraint(value, pltpu.HBM)


def limit(mib):
    return pltpu.CompilerParams(vmem_limit_bytes=mib << 20)


def cost(flops, nbytes):
    return pl.CostEstimate(flops=flops, bytes_accessed=nbytes, transcendentals=0)


def flip(value, axis, bits):
    count = lax.axis_size(axis)
    return lax.ppermute(value, axis, [(i, i ^ bits) for i in range(count)])


def fast_local(coarse_tiles, prolong_taps, tile_lists, nest_owner):
    farm_count = lax.axis_size("farm")
    groups = lax.axis_size(GROUP)
    local_tiles, rows, row_width = coarse_tiles.shape
    pairs = tile_lists.shape[1]
    edge = row_width // (CH * TILE_Z)
    width_x = pairs * edge
    lanes = rows * TILE_Z
    own_fine = rows * REFINE
    table = tables(NFX, NFY, NFZ, rows)
    const = {key: jnp.asarray(value) for key, value in table.items()}
    bind = lambda kernel, *sizes: (lambda *refs: kernel(*sizes, *refs))
    tile_shape = jax.ShapeDtypeStruct((rows, row_width), F32)

    info, *picked = pl.pallas_call(
        bind(pick_kernel, local_tiles, farm_count, pairs),
        name="pick",
        out_shape=[jax.ShapeDtypeStruct((farm_count + pairs + 1,), jnp.int32)]
        + [tile_shape] * farm_count,
        in_specs=[in_hbm()] * 3,
        out_specs=[in_smem()] + [in_vmem()] * farm_count,
        scratch_shapes=[
            pltpu.SMEM(tile_lists.shape, jnp.int32),
            pltpu.SMEM(nest_owner.shape, jnp.int32),
            pltpu.SemaphoreType.DMA((farm_count + 2,)),
        ],
        compiler_params=limit(8),
        cost_estimate=cost(0, 1 << 18),
    )(keep_hbm(tile_lists), keep_hbm(nest_owner), keep_hbm(coarse_tiles))
    moved = {s: flip(picked[s], "farm", s) for s in range(farm_count - 1, 0, -1)}
    moved = [picked[0]] + [moved[s] for s in range(1, farm_count)]
    mats, rmats, wu, ww = pl.pallas_call(
        prep_kernel,
        name="prep",
        out_shape=[
            jax.ShapeDtypeStruct((2 * NFX, NFX), BF),
            jax.ShapeDtypeStruct((2, 2 * width_x, NFX), BF),
            jax.ShapeDtypeStruct((2 * lanes, 2 * NFZ), BF),
            jax.ShapeDtypeStruct((2 * lanes, 2 * NFZ), BF),
        ],
        in_specs=[in_smem(), in_vmem()],
        out_specs=[in_vmem()] * 4,
        compiler_params=limit(8),
        cost_estimate=cost(0, 6 << 20),
    )(prolong_taps, const["bank"])

    piece = pl.pallas_call(
        bind(arrange_kernel, farm_count, pairs),
        name="arrange",
        out_shape=jax.ShapeDtypeStruct((CH, width_x, lanes), F32),
        in_specs=[in_smem(), anywhere()] + [in_vmem()] * farm_count,
        out_specs=in_vmem(),
        scratch_shapes=[pltpu.VMEM((farm_count, rows, row_width), F32)],
        compiler_params=limit(8),
        cost_estimate=cost(0, 1 << 18),
    )(info, rmats, *moved[::-1])
    far_bit, core_bit, near_bit = 4, 2, 1
    held = {0: piece}
    for bits in (near_bit, far_bit, near_bit | far_bit):
        held[bits] = flip(piece, GROUP, bits)
    for bits in (0, near_bit, far_bit, near_bit | far_bit):
        held[bits | core_bit] = flip(held[bits], GROUP, core_bit)

    coarse_rows = 2 * width_x
    coarse_y = groups * rows
    spectrum, *fresh, base = pl.pallas_call(
        bind(solve_kernel, farm_count, pairs, groups),
        name="solve",
        out_shape=[jax.ShapeDtypeStruct((own_fine, NFX, NFZ), F32)]
        + [tile_shape] * farm_count
        + [jax.ShapeDtypeStruct(coarse_tiles.shape, F32)],
        in_specs=[in_smem()] * 2
        + [in_vmem()] * (groups + 6)
        + [in_hbm()],
        out_specs=[in_vmem()] * (farm_count + 1) + [in_hbm()],
        scratch_shapes=[
            pltpu.VMEM((3, 2 * groups * coarse_rows, 2 * lanes), BF),
            pltpu.VMEM((3, coarse_y, coarse_rows, NFZ), F32),
            pltpu.VMEM((rows, NFX, NFZ), F32),
            pltpu.VMEM((rows, NFX, NFZ), F32),
            pltpu.VMEM((CH, width_x, lanes), F32),
            pltpu.VMEM((farm_count, rows, row_width), F32),
            pltpu.VMEM((own_fine + 1, 8, lanes), F32),
            pltpu.VMEM(coarse_tiles.shape, F32),
            pltpu.SemaphoreType.DMA((2,)),
        ],
        compiler_params=limit(40),
        cost_estimate=cost(4 << 30, 8 << 20),
    )(
        info, prolong_taps,
        *[held[s] for s in range(groups)],
        const["fx"], wu, ww, const["planes"], rmats, const["rz"],
        keep_hbm(coarse_tiles),
    )
    returned = [fresh[0]] + [flip(fresh[s], "farm", s) for s in range(1, farm_count)]

    half = 8
    pressure = pl.pallas_call(
        inverse_kernel,
        name="inverse",
        out_shape=jax.ShapeDtypeStruct((NFX, own_fine, NFZ), F32),
        grid=(own_fine // half,),
        in_specs=[
            pl.BlockSpec((2 * NFZ, 2 * NFZ), lambda i: (0, 0)),
            pl.BlockSpec((2 * NFX, NFX), lambda i: (0, 0)),
            pl.BlockSpec((half, NFX, NFZ), lambda i: (i, 0, 0)),
        ],
        out_specs=pl.BlockSpec((NFX, half, NFZ), lambda i: (0, i, 0)),
        scratch_shapes=[pltpu.VMEM((half, NFX, NFZ), F32)],
        compiler_params=limit(24),
        cost_estimate=cost(4 << 30, 4 << 20),
    )(const["iz"], mats, spectrum)

    updated = pl.pallas_call(
        bind(patch_kernel, farm_count),
        name="patch",
        out_shape=jax.ShapeDtypeStruct(coarse_tiles.shape, F32),
        in_specs=[in_smem(), in_hbm()] + [in_vmem()] * farm_count,
        out_specs=in_hbm(),
        scratch_shapes=[pltpu.SemaphoreType.DMA((farm_count,))],
        input_output_aliases={1: 0},
        compiler_params=limit(8),
        cost_estimate=cost(0, 1 << 18),
    )(info, base, *returned[::-1])
    return updated, pressure[None]


def fits_fast(mesh):
    return dict(mesh.shape) == {"farm": 4, "nx": 4, "ny": 2}


def solution(mesh):
    def body(coarse_tiles, prolong_taps, tile_lists, nest_owner):
        rows, row_width = coarse_tiles.shape[1:]
        edge = row_width // (CH * TILE_Z)
        dense = rows * TILE_Z == NFZ and edge % (2 * rows) == 0
        whole = tile_lists.shape[1] * edge * REFINE == NFX
        if fits_fast(mesh) and dense and whole:
            return fast_local(coarse_tiles, prolong_taps, tile_lists, nest_owner)
        return local(coarse_tiles, prolong_taps, tile_lists, nest_owner)

    return jax.shard_map(
        body,
        mesh=mesh,
        in_specs=(P("farm", GROUP, None), P(), P(), P()),
        out_specs=(P("farm", GROUP, None), P("farm", None, GROUP, None)),
        check_vma=False,
    )
```

```python
import math

import jax
import jax.numpy as jnp
import numpy as np
from jax import lax
from jax.experimental import pallas as pl
from jax.experimental.pallas import tpu as pltpu
from jax.sharding import PartitionSpec as P

TILE_Z = 32
REFINE = 4
TAPS = 8
CH = 4
NFX = 256
NFY = 128
NFZ = 128


exact_mode = lax.Precision.HIGHEST


def with_halo(block, sides, width):
    for axis, dim in sides:
        count = lax.axis_size(axis)
        forward = [(i, i + 1) for i in range(count - 1)]
        forward.append((count - 1, 0))
        backward = [(target, source) for source, target in forward]
        low = lax.ppermute(
            lax.slice_in_dim(block, block.shape[dim] - width, None, axis=dim), axis, forward
        )
        high = lax.ppermute(lax.slice_in_dim(block, 0, width, axis=dim), axis, backward)
        block = jnp.concatenate([low, block, high], axis=dim)
    return block


def prolong_matrix(taps_row, fine_count, coarse_count, fine_start, coarse_start, period):
    fine_index = fine_start + jnp.arange(fine_count, dtype=jnp.int32)
    coarse_index = coarse_start + jnp.arange(coarse_count, dtype=jnp.int32)
    offset = jnp.mod(fine_index[:, None] - REFINE * coarse_index[None, :] + 2, period)
    tap_match = offset[:, :, None] == jnp.arange(TAPS, dtype=jnp.int32)[None, None, :]
    return jnp.sum(
        jnp.where(tap_match, taps_row[None, None, :], jnp.zeros((), jnp.float32)), axis=2
    )


def eigen_part(freq_start, freq_count, length):
    freq_index = (freq_start + jnp.arange(freq_count, dtype=jnp.int32)).astype(jnp.float32)
    return 4.0 * jnp.sin(freq_index * (math.pi / length)) ** 2


def slot_lists(tile_lists, nest_owner, slot_ids):
    owner_match = nest_owner[None, :] == slot_ids[:, None]
    return jnp.sum(jnp.where(owner_match[:, :, None], tile_lists[None, :, :], 0), axis=1)


def wave_tables(length):
    index_row = jnp.arange(length, dtype=jnp.int32)
    turns = jnp.mod(index_row[:, None] * index_row[None, :], length).astype(jnp.float32)
    phase_angle = turns * (2.0 * math.pi / length)
    return (jnp.cos(phase_angle), jnp.sin(phase_angle))


def apply_along(matrix, values, axis_id):
    moved = jnp.tensordot(matrix, values, axes=([1], [axis_id]), precision=exact_mode)
    return jnp.moveaxis(moved, 0, axis_id)


def forward_pair(real_part, imag_part, cosines, sines, axis_id):
    return (
        apply_along(cosines, real_part, axis_id) + apply_along(sines, imag_part, axis_id),
        apply_along(cosines, imag_part, axis_id) - apply_along(sines, real_part, axis_id),
    )


def inverse_pair(real_part, imag_part, cosines, sines, axis_id, length):
    return (
        (apply_along(cosines, real_part, axis_id) - apply_along(sines, imag_part, axis_id))
        / length,
        (apply_along(sines, real_part, axis_id) + apply_along(cosines, imag_part, axis_id))
        / length,
    )


def to_real_space(real_part, imag_part, cos_x, sin_x, cos_z, sin_z):
    real_z, imag_z = inverse_pair(real_part, imag_part, cos_z, sin_z, 2, NFZ)
    return (apply_along(cos_x, real_z, 0) - apply_along(sin_x, imag_z, 0)) / NFX


def local(coarse_tiles, prolong_taps, tile_lists, nest_owner):
    farm_count = lax.axis_size("farm")
    farm_index = lax.axis_index("farm")
    groups = lax.axis_size(("nx", "ny"))
    group_index = lax.axis_index(("nx", "ny"))
    local_tiles, row_count, row_width = coarse_tiles.shape
    tile_edge = row_width // (CH * TILE_Z)
    pair_count = tile_lists.shape[1]
    slot_ids = jnp.arange(farm_count, dtype=jnp.int32)
    slot_tiles = slot_lists(tile_lists, nest_owner, slot_ids)
    owned_ids = farm_index * local_tiles + jnp.arange(local_tiles, dtype=jnp.int32)
    selector = (slot_tiles[:, :, None] == owned_ids[None, None, :]).astype(jnp.float32)
    send_pick = jnp.sum(selector, axis=1)
    flat_tiles = coarse_tiles.reshape(local_tiles, row_count * row_width)
    outgoing = jnp.dot(send_pick, flat_tiles, precision=exact_mode)
    incoming = lax.all_to_all(
        outgoing.reshape(farm_count, row_count, row_width),
        "farm",
        split_axis=0,
        concat_axis=0,
        tiled=True,
    )
    my_tiles = slot_tiles[farm_index]
    home_index = my_tiles // local_tiles
    order_pick = (home_index[:, None] == slot_ids[None, :]).astype(jnp.float32)
    nest_rows = jnp.dot(
        order_pick, incoming.reshape(farm_count, row_count * row_width), precision=exact_mode
    )
    nest_rows = nest_rows.reshape(pair_count, row_count, row_width)
    framed = with_halo(nest_rows, ((("nx", "ny"), 1),), 1)
    width_x = pair_count * tile_edge
    coarse = framed.reshape(pair_count, row_count + 2, CH, tile_edge, TILE_Z).transpose(
        2, 0, 3, 1, 4
    )
    coarse = coarse.reshape(CH, width_x, row_count + 2, TILE_Z)
    fine_rows = REFINE * row_count
    matrix_x = prolong_matrix(prolong_taps[0], NFX, width_x, 0, 0, NFX)
    matrix_y = prolong_matrix(
        prolong_taps[1],
        fine_rows + 1,
        row_count + 2,
        fine_rows * group_index,
        row_count * group_index - 1,
        NFY,
    )
    matrix_z = prolong_matrix(prolong_taps[2], NFZ, TILE_Z, 0, 0, NFZ)
    refined = apply_along(matrix_x, coarse, 1)
    refined = apply_along(matrix_z, refined, 3)
    refined = apply_along(matrix_y, refined, 2)
    own_rows = refined[:, :, :fine_rows, :]
    spread = (
        jnp.roll(own_rows[0], -1, 0)
        - own_rows[0]
        + (refined[1, :, 1:, :] - own_rows[1])
        + (jnp.roll(own_rows[2], -1, 2) - own_rows[2])
    )
    cos_y, sin_y = wave_tables(NFY)
    cos_z, sin_z = wave_tables(NFZ)
    ahead_cos, ahead_sin = wave_tables(NFX)
    behind_cos, behind_sin = (ahead_cos, ahead_sin)
    real_x = apply_along(ahead_cos, spread, 0)
    imag_x = -apply_along(ahead_sin, spread, 0)
    real_xz, imag_xz = forward_pair(real_x, imag_x, cos_z, sin_z, 2)
    columns = lax.all_to_all(
        jnp.stack([real_xz, imag_xz]), ("nx", "ny"), split_axis=1, concat_axis=2, tiled=True
    )
    span = ahead_cos.shape[0] // groups
    real_y, imag_y = forward_pair(columns[0], columns[1], cos_y, sin_y, 1)
    eigen_y = eigen_part(0, NFY, NFY)
    eigen_z = eigen_part(0, NFZ, NFZ)
    eigen_sum = (
        eigen_part(group_index * span, span, NFX)[:, None, None]
        + eigen_y[None, :, None]
        + eigen_z[None, None, :]
    )
    nonzero = eigen_sum > 0
    factor = jnp.where(nonzero, -1.0 / jnp.where(nonzero, eigen_sum, 1.0), 0.0)
    real_p = real_y * factor
    imag_p = imag_y * factor
    back_real, back_imag = inverse_pair(real_p, imag_p, cos_y, sin_y, 1, NFY)
    theta = jnp.arange(NFY, dtype=jnp.float32) * (2.0 * math.pi / NFY)
    cos_diff = (1.0 - jnp.cos(theta))[None, :, None]
    sin_diff = jnp.sin(theta)[None, :, None]
    real_g = real_p * cos_diff - imag_p * sin_diff
    imag_g = real_p * sin_diff + imag_p * cos_diff
    grad_real, grad_imag = inverse_pair(real_g, imag_g, cos_y, sin_y, 1, NFY)
    returned = lax.all_to_all(
        jnp.stack([back_real, back_imag, grad_real, grad_imag]),
        ("nx", "ny"),
        split_axis=2,
        concat_axis=1,
        tiled=True,
    )
    pressure = to_real_space(returned[0], returned[1], behind_cos, behind_sin, cos_z, sin_z)
    grad_y = to_real_space(returned[2], returned[3], behind_cos, behind_sin, cos_z, sin_z)
    new_fields = jnp.stack(
        [
            own_rows[0] - (pressure - jnp.roll(pressure, 1, 0)),
            own_rows[1] - grad_y,
            own_rows[2] - (pressure - jnp.roll(pressure, 1, 2)),
            own_rows[3] + pressure,
        ]
    )
    blocks = new_fields.reshape(CH, width_x, REFINE, row_count, REFINE, TILE_Z, REFINE).mean(
        axis=(2, 4, 6)
    )
    restored = blocks.reshape(CH, pair_count, tile_edge, row_count, TILE_Z).transpose(1, 3, 0, 2, 4)
    restored = restored.reshape(pair_count, row_count * row_width)
    returning = jnp.dot(order_pick.T, restored, precision=exact_mode)
    arrived = lax.all_to_all(
        returning.reshape(farm_count, row_count, row_width),
        "farm",
        split_axis=0,
        concat_axis=0,
        tiled=True,
    )
    placed = jnp.dot(
        send_pick.T, arrived.reshape(farm_count, row_count * row_width), precision=exact_mode
    )
    covered = jnp.sum(send_pick, axis=0)
    updated = coarse_tiles * (1.0 - covered)[:, None, None] + placed.reshape(
        local_tiles, row_count, row_width
    )
    return (updated, pressure[None])


BF = jnp.bfloat16
F32 = jnp.float32
GROUP = ("nx", "ny")


def split_np(table):
    hi = jnp.asarray(table, F32).astype(BF)
    return hi


def halves(value):
    hi = value.astype(BF)
    return hi, (value - hi.astype(F32)).astype(BF)


def halves_np(table):
    table = np.asarray(table, np.float32)
    hi = table.astype(BF)
    return hi, (table - hi.astype(np.float32)).astype(BF)


def mm(left, right):
    return jnp.dot(left, right, preferred_element_type=F32)


def x_slots(nfx):
    quarter = nfx // 4
    low = np.arange(quarter)
    freq = np.concatenate([low, low, low + quarter, low + quarter])
    phase = np.concatenate(
        [np.ones(quarter), 1j * np.ones(quarter), np.ones(quarter), 1j * np.ones(quarter)]
    ).astype(np.complex128)
    freq[quarter] = nfx // 2
    phase[quarter] = 1.0
    phase[2 * quarter] = 1.0 - 1.0j
    weight = np.where((freq == 0) | (freq == nfx // 2), 1.0, 2.0)
    return freq, phase, weight


def z_slots(nfz):
    half = nfz // 2
    low = np.arange(half)
    freq = np.concatenate([low, low])
    imag = np.concatenate([np.zeros(half, bool), np.ones(half, bool)])
    freq[half] = half
    imag[half] = False
    weight = np.where((freq == 0) | (freq == half), 1.0, 2.0)
    return freq, imag, weight


def tables(nfx, nfy, nfz, rows):
    out = {}
    quarter = nfx // 4
    fx, phase, wx = x_slots(nfx)
    theta = 2 * np.pi * fx / nfx
    tap = np.arange(TAPS)[:, None] - 2
    gamma = (wx / nfx) * phase * np.exp(-1j * theta[None] * tap)
    mean = sum(np.exp(1j * theta * q) for q in range(REFINE)) / REFINE
    step = (np.exp(1j * theta * (REFINE - 1)) - np.exp(-1j * theta)) / REFINE
    gx = np.stack([gamma, gamma * mean, gamma * step])
    out["gx"] = np.stack([gx.real, gx.imag])
    turns = (np.arange(nfx)[:, None] * fx[None, :]) % nfx
    out["ex"] = np.stack([np.cos(turns * 2 * np.pi / nfx), np.sin(turns * 2 * np.pi / nfx)])
    out["e4"] = out["ex"][:, ::REFINE]
    fz, imag, wz = z_slots(nfz)
    phi = 2 * np.pi * fz / nfz
    psi = np.where(imag, -1j, 1.0)
    gz = psi * np.exp(-1j * phi[None] * tap)
    gz = np.stack([gz, gz * (np.exp(1j * phi) - 1.0)])
    out["gz"] = np.stack([gz.real, gz.imag])
    coarse_z = nfz // REFINE
    turns = (REFINE * np.arange(coarse_z)[:, None] * fz[None, :]) % nfz
    zz = np.stack([np.cos(turns * 2 * np.pi / nfz), np.sin(turns * 2 * np.pi / nfz)])
    out["zz"] = np.tile(zz, (1, rows, 1))
    turns = (fz[:, None] * np.arange(nfz)[None, :]) % nfz
    angle = turns * 2 * np.pi / nfz
    iz = (wz / nfz)[:, None] * np.where(imag[:, None], -np.sin(angle), np.cos(angle))
    hi, lo = halves_np(iz)
    out["iz"] = np.concatenate(
        [np.concatenate([hi, lo], 1), np.concatenate([hi, np.zeros_like(lo)], 1)], 0
    )
    rz = iz.reshape(nfz, coarse_z, REFINE).mean(2)
    dz = (iz[:, REFINE - 1 :: REFINE] - np.roll(iz, 1, 1)[:, ::REFINE]) / REFINE
    eye = np.eye(rows)
    big = [
        np.einsum("ij,kz->ikjz", eye, mat).reshape(rows * nfz, rows * coarse_z) for mat in (rz, dz)
    ]
    out["rz"] = np.stack(halves_np(np.concatenate(big, 1)))
    coarse = np.arange(quarter)
    turns = (coarse[:, None] * coarse[None, :]) % quarter
    angle = turns * 2 * np.pi / quarter
    fwd = np.concatenate([np.cos(angle), -np.sin(angle)], 0)
    fwd[quarter] = 1.0
    hi, lo = halves_np(fwd)
    out["fx"] = np.concatenate([hi, hi, lo], 1)
    mu = 4 * np.sin(np.pi * fx / nfx)[:, None] ** 2 + 4 * np.sin(np.pi * fz / nfz)[None, :] ** 2
    root = 1 + mu / 2 - np.sqrt(mu + mu * mu / 4)
    root = np.where(mu == 0, 0.0, root)
    kappa = -root / (1 - root**2)
    per = 1 / (1 - root**nfy)
    dx = np.exp(1j * theta) - 1
    own = dx.real.copy()
    other = np.concatenate(
        [-dx.imag[:quarter], dx.imag[:quarter], -dx.imag[2 * quarter : 3 * quarter],
         dx.imag[2 * quarter : 3 * quarter]]
    )
    own[0], own[quarter], own[2 * quarter], own[3 * quarter] = 0.0, -2.0, -1.0, 0.0
    other[[0, quarter, 2 * quarter, 3 * quarter]] = 0.0
    wide = np.ones((1, nfz))
    out["planes"] = np.stack([root, kappa, per, own[:, None] * wide, other[:, None] * wide])
    out["planes"] = out["planes"].astype(np.float32)
    flat = [out.pop("gx").reshape(-1, nfx), out.pop("ex").reshape(-1, nfx)]
    flat += [out.pop("e4").reshape(-1, nfx)]
    flat += [np.concatenate([part[0], part[1]], -1).reshape(-1, nfx) for part in (out.pop("gz"), out.pop("zz"))]
    out["bank"] = np.concatenate(flat, 0).astype(np.float32)
    return out


def find_tiles(me, lists, owner, local_tiles, farm_count, pairs):
    found, shifts = [], []
    for shift in range(farm_count):
        target = me ^ shift
        tile = jnp.int32(0)
        for nest in range(farm_count):
            for pair in range(pairs):
                entry = lists[nest, pair]
                hit = (owner[nest] == target) & (entry // local_tiles == me)
                tile = jnp.where(hit, entry, tile)
        found.append(tile - me * local_tiles)
    for pair in range(pairs):
        tile = jnp.int32(0)
        for nest in range(farm_count):
            tile = jnp.where(owner[nest] == me, lists[nest, pair], tile)
        shifts.append((tile // local_tiles) ^ me)
    return found, shifts


def swap_blocks(value, rows, width):
    lane = lax.broadcasted_iota(jnp.int32, value.shape, 1) // width
    sub = lax.broadcasted_iota(jnp.int32, value.shape, 0) % rows
    delta = lane - sub
    result = value
    lanes = value.shape[1]
    height = value.shape[0]
    for shift in range(1, rows):
        for sign in (1, -1):
            amount = sign * shift
            moved = pltpu.roll(value, (amount * width) % lanes, 1)
            moved = pltpu.roll(moved, (-amount) % height, 0)
            result = jnp.where(delta == amount, moved, result)
    return result


def pick_kernel(local_tiles, farm_count, pairs, lists_any, owner_any, tiles, *refs):
    info, outs = refs[0], refs[1 : 1 + farm_count]
    lists, owner, sems = refs[1 + farm_count :]
    reads = [
        pltpu.make_async_copy(lists_any, lists, sems.at[farm_count]),
        pltpu.make_async_copy(owner_any, owner, sems.at[farm_count + 1]),
    ]
    for copy in reads:
        copy.start()
    for copy in reads:
        copy.wait()
    me = lax.axis_index("farm")
    found, shifts = find_tiles(me, lists, owner, local_tiles, farm_count, pairs)
    copies = []
    for shift in range(farm_count):
        copies.append(
            pltpu.make_async_copy(tiles.at[found[shift]], outs[shift], sems.at[shift])
        )
        copies[-1].start()
    for shift in range(farm_count):
        info[shift] = found[shift]
    for pair in range(pairs):
        info[farm_count + pair] = shifts[pair]
    info[farm_count + pairs] = lax.axis_index(GROUP)
    for copy in copies:
        copy.wait()


def arrange_kernel(farm_count, pairs, info, gate, *refs):
    tiles = refs[:farm_count]
    piece, own, stage = refs[farm_count:]
    for shift in range(farm_count):
        stage[shift] = tiles[farm_count - 1 - shift][...]
    rows = stage.shape[1]
    width_x, lanes = own.shape
    channels = stage.shape[2] * pairs // (width_x * (lanes // rows))
    edge = width_x // pairs
    per = lanes // rows
    row_lanes = edge * per
    for pair in range(pairs):
        tile = stage[info[farm_count + pair]]
        for channel in range(channels):
            for part in range(edge * per // (2 * lanes)):
                base = channel * row_lanes + 2 * part * lanes
                block = jnp.concatenate(
                    [tile[:, base : base + lanes], tile[:, base + lanes : base + 2 * lanes]], 0
                )
                at = pair * edge + 2 * part * rows
                if channel < channels - 1:
                    at = channel * width_x + at
                    piece[at : at + 2 * rows, :] = swap_blocks(block, rows, per)
                else:
                    own[at : at + 2 * rows, :] = swap_blocks(block, rows, per)
    rolled = pltpu.roll(own[...], per, 1)
    half = width_x // 2
    front = lax.broadcasted_iota(jnp.int32, (half, lanes), 1) < lanes // 2
    edges = jnp.where(front, rolled[0:half], pltpu.roll(rolled[half:], lanes // 2, 1))
    piece[(channels - 1) * width_x :, :] = edges


def prep_kernel(taps, bank, mats, rmats, wu, ww):
    nfx = mats.shape[1]
    quarter = nfx // REFINE
    lanes = wu.shape[0] // 2
    duo = lanes // 2
    at_ex = 6 * TAPS
    at_e4 = at_ex + 2 * nfx
    at_gz = at_e4 + 2 * quarter
    at_zz = at_gz + 2 * TAPS

    def weighted(at, axis):
        total = taps[axis, 0] * bank[at : at + 1, :]
        for tap in range(1, TAPS):
            total = total + taps[axis, tap] * bank[at + tap : at + tap + 1, :]
        return total

    full = weighted(0, 0) * bank[at_ex : at_ex + nfx, :]
    full = full - weighted(3 * TAPS, 0) * bank[at_ex + nfx : at_ex + 2 * nfx, :]
    hi, lo = halves(full)
    mats[0:nfx, :] = hi
    mats[nfx : 2 * nfx, :] = lo
    for which in (1, 2):
        at = (which - 1) * quarter
        coarse = weighted(which * TAPS, 0) * bank[at_e4 : at_e4 + quarter, :]
        second = bank[at_e4 + quarter : at_e4 + 2 * quarter, :]
        coarse = coarse - weighted((3 + which) * TAPS, 0) * second
        hi, lo = halves(coarse)
        rmats[0, at : at + quarter, :] = hi
        rmats[1, at : at + quarter, :] = lo
    band = lax.broadcasted_iota(jnp.int32, (duo, lanes), 0) // (duo // 2)
    for which, target in ((0, wu), (1, ww)):
        value = weighted(at_gz + which * TAPS, 2) * bank[at_zz : at_zz + lanes, :]
        value = value[:, 0:lanes] + value[:, lanes : 2 * lanes]
        for row in range(2):
            hi, lo = halves(jnp.where(band == row, value[0:duo], 0.0))
            at = row * lanes
            target[0:duo, at : at + lanes] = hi
            target[duo:lanes, at : at + lanes] = hi
            target[lanes : lanes + duo, at : at + lanes] = lo
            target[lanes + duo : 2 * lanes, at : at + lanes] = jnp.zeros_like(lo)


def solve_kernel(farm_count, pairs, groups, info, taps, *refs):
    blocks, own_q = refs[:groups], refs[groups]
    refs = refs[:groups] + refs[groups + 1 :]
    (fx, wu, ww, planes, rmats, rz, tiles, spectrum) = refs[groups : groups + 8]
    outs = refs[groups + 8 : groups + 8 + farm_count]
    base = refs[groups + 8 + farm_count]
    (left, field, mean_p, step_p, fresh, out_stage, zero_add, shelf, sems) = refs[
        groups + 9 + farm_count :
    ]
    take = pltpu.make_async_copy(tiles, shelf, sems.at[0])
    take.start()
    group = info[farm_count + pairs]
    width_x, lanes = own_q.shape
    channels = fresh.shape[0]
    pieces = [
        [block.at[pl.ds(channel * width_x, width_x)] for channel in range(channels - 1)]
        + [block.at[pl.ds((channels - 1) * width_x, width_x // 2)]]
        for block in blocks
    ]
    rows = mean_p.shape[0]
    per = lanes // rows
    coarse_y = groups * rows
    fine_y = coarse_y * REFINE
    own_fine = rows * REFINE
    coarse_rows = fx.shape[0]

    def band(axis):
        quarter = 1.0 / REFINE
        return (
            (taps[axis, 6] + taps[axis, 7]) * quarter,
            (taps[axis, 2] + taps[axis, 3] + taps[axis, 4] + taps[axis, 5]) * quarter,
            (taps[axis, 0] + taps[axis, 1]) * quarter,
        )

    lane = lax.broadcasted_iota(jnp.int32, (width_x, lanes), 1)
    previous = group ^ ((group + groups - 1) & (groups - 1))
    following = group ^ ((group + 1) & (groups - 1))

    def beside(shift, channel):
        value = pieces[1][channel][...]
        mark = 3
        while mark < groups:
            value = jnp.where(shift == mark, pieces[mark][channel][...], value)
            mark = 2 * mark + 1
        return value

    @pl.when(group >= 0)
    def _():
        for channel in range(channels):
            lag, mid, lead = band(1)
            if channel < channels - 1:
                here = pieces[0][channel][...]
                before = pltpu.roll(beside(previous, channel), per, 1)
                after = pltpu.roll(beside(following, channel), lanes - per, 1)
            else:
                here = own_q[...]
                prior, later = beside(previous, channel), beside(following, channel)
                before = jnp.concatenate([prior, pltpu.roll(prior, lanes // 2, 1)], 0)
                after = jnp.concatenate([pltpu.roll(later, lanes // 2, 1), later], 0)
            low = jnp.where(lane < per, before, pltpu.roll(here, per, 1))
            high = jnp.where(lane >= lanes - per, after, pltpu.roll(here, lanes - per, 1))
            value = mid * here + lag * low + lead * high
            lag, mid, lead = band(2)
            spot = lane % per
            low = jnp.where(spot == 0, pltpu.roll(value, lanes - per + 1, 1), pltpu.roll(value, 1, 1))
            high = jnp.where(
                spot == per - 1, pltpu.roll(value, per - 1, 1), pltpu.roll(value, lanes - 1, 1)
            )
            value = mid * value + lag * low + lead * high
            lag, mid, lead = band(0)
            value = (
                mid * value
                + lag * pltpu.roll(value, 1, 0)
                + lead * pltpu.roll(value, width_x - 1, 0)
            )
            fresh[channel] = value
    duo = lanes // 2
    ahead_half = lax.broadcasted_iota(jnp.int32, (coarse_rows, lanes), 1) < duo
    for block in range(groups):
        @pl.when(group >= 0)
        def _():
            hi, lo = halves(jnp.concatenate([pieces[block][channel][...] for channel in range(3)], 1))
            turned = mm(fx[...], jnp.concatenate([hi, lo, hi], 0))
            for channel in range(3):
                value = turned[:, channel * lanes : (channel + 1) * lanes]
                moved = pltpu.roll(value, duo, 1)
                twins = (
                    jnp.where(ahead_half, value, moved),
                    jnp.where(ahead_half, moved, value),
                )
                for pair in range(2):
                    value = twins[pair]
                    hi = value.astype(BF)
                    rest = jnp.where(ahead_half, value, value - hi.astype(F32)).astype(BF)
                    at = (2 * block + pair) * coarse_rows
                    left[channel, at : at + coarse_rows, :] = jnp.concatenate([rest, hi], 1)
    chunk = min(groups, 4)
    for channel in range(3):
        @pl.when(group >= 0)
        def _():
            weight = ww if channel == 2 else wu
            for block in range(0, groups, chunk):
                at = 2 * block * coarse_rows
                value = mm(left[channel, at : at + 2 * chunk * coarse_rows, :], weight[...])
                for inner in range(chunk):
                    for row in range(rows):
                        at_y = (((group ^ (block + inner)) - group) * rows + row) & (coarse_y - 1)
                        at = (2 * inner + row // 2) * coarse_rows
                        field[channel, at_y] = value[
                            at : at + coarse_rows, (row % 2) * lanes : (row % 2 + 1) * lanes
                        ]

    @pl.when(group >= 0)
    def _():
        sums = jnp.concatenate(
            [jnp.sum(pieces[block][1][...], axis=0, keepdims=True) for block in range(groups)], 0
        )
        total_z = taps[2, 0]
        for tap in range(1, TAPS):
            total_z = total_z + taps[2, tap]
        sums = sums * total_z
        shape = (groups, lanes)
        coarse_id = rows * (lax.broadcasted_iota(jnp.int32, shape, 0) ^ group)
        coarse_id = coarse_id + lax.broadcasted_iota(jnp.int32, shape, 1) // per
        corner = (lax.broadcasted_iota(jnp.int32, (8, lanes), 0) == 0) & (
            lax.broadcasted_iota(jnp.int32, (8, lanes), 1) == 0
        )
        for index in range(own_fine + 1):
            at = own_fine * group - 1 + index
            weight = jnp.zeros(shape, F32)
            for tap in range(TAPS):
                gap = (at - REFINE * coarse_id + 2 - tap) & (fine_y - 1)
                saw = 0.5 - (2 * gap + 1).astype(F32) * (0.5 / fine_y)
                weight = weight + taps[1, tap] * saw
            value = jnp.sum(jnp.sum(weight * sums, axis=1, keepdims=True), axis=0, keepdims=True)
            zero_add[index] = jnp.where(corner, value, 0.0)

    take.wait()
    give = pltpu.make_async_copy(shelf, base, sems.at[1])
    give.start()

    def at_row(offset):
        return offset % coarse_y

    def tap_y(offset):
        return taps[1, offset + 2]

    half_rows = coarse_rows // 2

    def sweep(step, carry):
        low = pl.multiple_of(8 * step, 8)
        spots = (low, half_rows + low)
        slots = [pl.multiple_of(part * half_rows + low, 8) for part in range(4)]

        def plane(which, part):
            return planes[which, pl.ds(slots[part], 8), :]

        def coarse(channel, row, side):
            return field[channel, row, pl.ds(spots[side], 8), :]

        root = [plane(0, part) for part in range(4)]
        quad = [value * value for value in root]
        quad = [value * value for value in quad]

        def horner(i, acc):
            spread = []
            for way, (offset, sign) in enumerate(((-2, -1), (rows + 1, 1))):
                row = at_row(offset + sign * (coarse_y - 1 - i))
                loaded = [[coarse(c, row, side) for side in range(2)] for c in range(3)]
                spread += [
                    acc[12 * way + c * 4 + part] * quad[part] + loaded[c][part % 2]
                    for c in range(3)
                    for part in range(4)
                ]
            return tuple(spread)

        sums_far = tuple(jnp.zeros((8, lanes), F32) for _ in range(24))
        for i in range(coarse_y):
            sums_far = horner(i, sums_far)
        below, above = sums_far[:12], sums_far[12:]
        opening = jnp.where(step == 0, 1.0, 0.0)
        near = list(range(-1, rows + 1))
        near_u = {m: [coarse(0, at_row(m), side) for side in range(2)] for m in near}
        near_v = {m: [coarse(1, at_row(m), side) for side in range(2)] for m in near}
        near_w = {m: [coarse(2, at_row(m), side) for side in range(2)] for m in near}
        for part in range(4):
            side = part % 2
            mate = part + 1 if side == 0 else part - 1
            r = root[part]
            kappa, per_wrap = plane(1, part), plane(2, part)
            own, other = plane(3, part), plane(4, part)
            turn = {
                m: own * near_u[m][side] + other * near_u[m][1 - side] + near_w[m][side]
                for m in near
            }
            lift = {m: near_v[m][side] for m in near}
            poly_a2 = tap_y(-2) * r + tap_y(-1)
            poly_a1 = poly_a2
            for e in range(0, 4):
                poly_a1 = poly_a1 * r + tap_y(e)
            poly_a = (poly_a1 * r + tap_y(4)) * r + tap_y(5)
            poly_b2 = tap_y(5) * r + tap_y(4)
            poly_b1 = poly_b2
            for e in (3, 2, 1, 0):
                poly_b1 = poly_b1 * r + tap_y(e)
            poly_b = (poly_b1 * r + tap_y(-1)) * r + tap_y(-2)
            far_scale = per_wrap * r * r
            turn_l = own * below[part] + other * below[mate] + below[8 + part]
            turn_r = own * above[part] + other * above[mate] + above[8 + part]
            drop = r - 1.0
            start = far_scale * poly_a * (turn_l + drop * below[4 + part])
            start = start + poly_a1 * turn[-1] + (drop * poly_a1 + tap_y(4)) * lift[-1]
            start = start + poly_a2 * turn[0] + (drop * poly_a2 + tap_y(0)) * lift[0]
            end = far_scale * poly_b * (r * turn_r - drop * above[4 + part])
            end = end + r * poly_b1 * turn[rows] - (drop * poly_b1 + tap_y(0)) * lift[rows]
            end = end + r * poly_b2 * turn[rows - 1] - (drop * poly_b2 + tap_y(4)) * lift[rows - 1]
            source = []
            for j in range(own_fine):
                m0, q = j // REFINE, j % REFINE
                total = None
                for m in (m0 - 1, m0, m0 + 1):
                    e = j - REFINE * m
                    if -2 <= e <= 5:
                        term = tap_y(e) * turn[m]
                        total = term if total is None else total + term
                    if -3 <= e <= 5:
                        scale = (tap_y(e + 1) if e < 5 else 0.0) - (tap_y(e) if e > -3 else 0.0)
                        total = total + scale * lift[m] if total is not None else scale * lift[m]
                source.append(total)
            ahead = [start]
            for j in range(own_fine):
                ahead.append(ahead[-1] * r + source[j])
            back = end
            pressure = [None] * (own_fine + 1)
            pressure[own_fine] = kappa * (ahead[own_fine] + back)
            for j in range(own_fine - 1, -1, -1):
                back = r * (back + source[j])
                pressure[j] = kappa * (ahead[j] + back)
            if part == 0:
                pressure = [pressure[j] + opening * zero_add[j] for j in range(own_fine + 1)]
            spot = pl.ds(slots[part], 8)
            for j in range(own_fine):
                spectrum[j, spot, :] = pressure[j + 1]
            for m in range(rows):
                at = REFINE * m
                total = pressure[at + 1]
                for q in range(1, REFINE):
                    total = total + pressure[at + 1 + q]
                mean_p[m, spot, :] = total * (1.0 / REFINE)
                step_p[m, spot, :] = (pressure[at + REFINE] - pressure[at]) * (1.0 / REFINE)
        return carry

    lax.fori_loop(0, half_rows // 8, sweep, 0)
    def left_three(count, stacked):
        hi, lo = halves(stacked)
        value = mm(rmats[0, 0:count, :], hi) + mm(rmats[0, 0:count, :], lo)
        return value + mm(rmats[1, 0:count, :], hi)

    def right_three(value, table):
        hi, lo = halves(value)
        return mm(hi, table[0]) + mm(lo, table[0]) + mm(hi, table[1])

    smooth = left_three(2 * width_x, jnp.concatenate([mean_p[m] for m in range(rows)], 1))
    slope = left_three(width_x, jnp.concatenate([step_p[m] for m in range(rows)], 1))
    mean_x, step_x = smooth[0:width_x], smooth[width_x : 2 * width_x]
    through = right_three(jnp.concatenate([step_x, slope, mean_x], 0), rz)
    part_w = through[2 * width_x : 3 * width_x, lanes:]
    through = through[:, 0:lanes]
    change = [
        -through[0:width_x],
        -through[width_x : 2 * width_x],
        -part_w,
        through[2 * width_x : 3 * width_x],
    ]

    for channel in range(channels):
        fresh[channel] = fresh[channel] + change[channel]
    @pl.when(group >= 0)
    def _():
        shifts = [info[farm_count + pair] for pair in range(pairs)]
        edge = width_x // pairs
        row_lanes = edge * per
        for pair in range(pairs):
            for channel in range(channels):
                for part in range(row_lanes // (2 * lanes)):
                    at = pair * edge + 2 * part * rows
                    block = swap_blocks(fresh[channel, at : at + 2 * rows, :], rows, per)
                    base = channel * row_lanes + 2 * part * lanes
                    out_stage[shifts[pair], :, base : base + lanes] = block[0:rows]
                    out_stage[shifts[pair], :, base + lanes : base + 2 * lanes] = block[rows:]
        for shift in range(farm_count):
            outs[shift][...] = out_stage[shift]
    give.wait()


def inverse_kernel(iz, mats, spectrum, out, middle):
    count, nfx, lanes = spectrum.shape
    for at in range(0, count, 4):
        hi, lo = halves(spectrum[at : at + 4].reshape(4 * nfx, lanes))
        both = mm(jnp.concatenate([hi, lo], 1), iz[...])
        middle[at : at + 4] = (both[:, 0:lanes] + both[:, lanes : 2 * lanes]).reshape(4, nfx, lanes)
    for at in range(0, count, 2):
        hi, lo = halves(jnp.concatenate([middle[at], middle[at + 1]], 1))
        upper = mm(mats[...], hi)
        final = upper[0:nfx] + upper[nfx : 2 * nfx] + mm(mats[0:nfx, :], lo)
        for row in range(2):
            out[:, at + row, :] = final[:, row * lanes : (row + 1) * lanes]


def patch_kernel(farm_count, info, base, *refs):
    tiles, out, sems = refs[:farm_count], refs[farm_count], refs[farm_count + 1]
    copies = []
    for shift in range(farm_count):
        copies.append(
            pltpu.make_async_copy(
                tiles[farm_count - 1 - shift], out.at[info[shift]], sems.at[shift]
            )
        )
        copies[-1].start()
    for copy in copies:
        copy.wait()


def in_vmem():
    return pl.BlockSpec(memory_space=pltpu.VMEM)


def in_smem():
    return pl.BlockSpec(memory_space=pltpu.SMEM)


def anywhere():
    return pl.BlockSpec(memory_space=pl.ANY)


def in_hbm():
    return pl.BlockSpec(memory_space=pltpu.HBM)


def keep_hbm(value):
    return pltpu.with_memory_space_constraint(value, pltpu.HBM)


def limit(mib):
    return pltpu.CompilerParams(vmem_limit_bytes=mib << 20)


def cost(flops, nbytes):
    return pl.CostEstimate(flops=flops, bytes_accessed=nbytes, transcendentals=0)


def flip(value, axis, bits):
    count = lax.axis_size(axis)
    return lax.ppermute(value, axis, [(i, i ^ bits) for i in range(count)])


def fast_local(coarse_tiles, prolong_taps, tile_lists, nest_owner):
    farm_count = lax.axis_size("farm")
    groups = lax.axis_size(GROUP)
    local_tiles, rows, row_width = coarse_tiles.shape
    pairs = tile_lists.shape[1]
    edge = row_width // (CH * TILE_Z)
    width_x = pairs * edge
    lanes = rows * TILE_Z
    own_fine = rows * REFINE
    table = tables(NFX, NFY, NFZ, rows)
    const = {key: jnp.asarray(value) for key, value in table.items()}
    bind = lambda kernel, *sizes: (lambda *refs: kernel(*sizes, *refs))
    tile_shape = jax.ShapeDtypeStruct((rows, row_width), F32)

    info, *picked = pl.pallas_call(
        bind(pick_kernel, local_tiles, farm_count, pairs),
        name="pick",
        out_shape=[jax.ShapeDtypeStruct((farm_count + pairs + 1,), jnp.int32)]
        + [tile_shape] * farm_count,
        in_specs=[in_hbm()] * 3,
        out_specs=[in_smem()] + [in_vmem()] * farm_count,
        scratch_shapes=[
            pltpu.SMEM(tile_lists.shape, jnp.int32),
            pltpu.SMEM(nest_owner.shape, jnp.int32),
            pltpu.SemaphoreType.DMA((farm_count + 2,)),
        ],
        compiler_params=limit(8),
        cost_estimate=cost(0, 1 << 18),
    )(keep_hbm(tile_lists), keep_hbm(nest_owner), keep_hbm(coarse_tiles))
    moved = {s: flip(picked[s], "farm", s) for s in range(farm_count - 1, 0, -1)}
    moved = [picked[0]] + [moved[s] for s in range(1, farm_count)]
    mats, rmats, wu, ww = pl.pallas_call(
        prep_kernel,
        name="prep",
        out_shape=[
            jax.ShapeDtypeStruct((2 * NFX, NFX), BF),
            jax.ShapeDtypeStruct((2, 2 * width_x, NFX), BF),
            jax.ShapeDtypeStruct((2 * lanes, 2 * NFZ), BF),
            jax.ShapeDtypeStruct((2 * lanes, 2 * NFZ), BF),
        ],
        in_specs=[in_smem(), in_vmem()],
        out_specs=[in_vmem()] * 4,
        compiler_params=limit(8),
        cost_estimate=cost(0, 6 << 20),
    )(prolong_taps, const["bank"])

    piece, own = pl.pallas_call(
        bind(arrange_kernel, farm_count, pairs),
        name="arrange",
        out_shape=[
            jax.ShapeDtypeStruct(((CH - 1) * width_x + width_x // 2, lanes), F32),
            jax.ShapeDtypeStruct((width_x, lanes), F32),
        ],
        in_specs=[in_smem(), anywhere()] + [in_vmem()] * farm_count,
        out_specs=[in_vmem()] * 2,
        scratch_shapes=[pltpu.VMEM((farm_count, rows, row_width), F32)],
        compiler_params=limit(8),
        cost_estimate=cost(0, 1 << 18),
    )(info, rmats, *moved[::-1])
    far_bit, core_bit, near_bit = 4, 2, 1
    held = {0: piece}
    for bits in (near_bit, far_bit, near_bit | far_bit):
        held[bits] = flip(piece, GROUP, bits)
    for bits in (0, near_bit, far_bit, near_bit | far_bit):
        held[bits | core_bit] = flip(held[bits], GROUP, core_bit)

    coarse_rows = 2 * width_x
    coarse_y = groups * rows
    spectrum, *fresh, base = pl.pallas_call(
        bind(solve_kernel, farm_count, pairs, groups),
        name="solve",
        out_shape=[jax.ShapeDtypeStruct((own_fine, NFX, NFZ), F32)]
        + [tile_shape] * farm_count
        + [jax.ShapeDtypeStruct(coarse_tiles.shape, F32)],
        in_specs=[in_smem()] * 2
        + [in_vmem()] * (groups + 7)
        + [in_hbm()],
        out_specs=[in_vmem()] * (farm_count + 1) + [in_hbm()],
        scratch_shapes=[
            pltpu.VMEM((3, 2 * groups * coarse_rows, 2 * lanes), BF),
            pltpu.VMEM((3, coarse_y, coarse_rows, NFZ), F32),
            pltpu.VMEM((rows, NFX, NFZ), F32),
            pltpu.VMEM((rows, NFX, NFZ), F32),
            pltpu.VMEM((CH, width_x, lanes), F32),
            pltpu.VMEM((farm_count, rows, row_width), F32),
            pltpu.VMEM((own_fine + 1, 8, lanes), F32),
            pltpu.VMEM(coarse_tiles.shape, F32),
            pltpu.SemaphoreType.DMA((2,)),
        ],
        compiler_params=limit(40),
        cost_estimate=cost(4 << 30, 8 << 20),
    )(
        info, prolong_taps,
        *[held[s] for s in range(groups)],
        own,
        const["fx"], wu, ww, const["planes"], rmats, const["rz"],
        keep_hbm(coarse_tiles),
    )
    returned = [fresh[0]] + [flip(fresh[s], "farm", s) for s in range(1, farm_count)]

    half = 8
    pressure = pl.pallas_call(
        inverse_kernel,
        name="inverse",
        out_shape=jax.ShapeDtypeStruct((NFX, own_fine, NFZ), F32),
        grid=(own_fine // half,),
        in_specs=[
            pl.BlockSpec((2 * NFZ, 2 * NFZ), lambda i: (0, 0)),
            pl.BlockSpec((2 * NFX, NFX), lambda i: (0, 0)),
            pl.BlockSpec((half, NFX, NFZ), lambda i: (i, 0, 0)),
        ],
        out_specs=pl.BlockSpec((NFX, half, NFZ), lambda i: (0, i, 0)),
        scratch_shapes=[pltpu.VMEM((half, NFX, NFZ), F32)],
        compiler_params=limit(24),
        cost_estimate=cost(4 << 30, 4 << 20),
    )(const["iz"], mats, spectrum)

    updated = pl.pallas_call(
        bind(patch_kernel, farm_count),
        name="patch",
        out_shape=jax.ShapeDtypeStruct(coarse_tiles.shape, F32),
        in_specs=[in_smem(), in_hbm()] + [in_vmem()] * farm_count,
        out_specs=in_hbm(),
        scratch_shapes=[pltpu.SemaphoreType.DMA((farm_count,))],
        input_output_aliases={1: 0},
        compiler_params=limit(8),
        cost_estimate=cost(0, 1 << 18),
    )(info, base, *returned[::-1])
    return updated, pressure[None]


def fits_fast(mesh):
    return dict(mesh.shape) == {"farm": 4, "nx": 4, "ny": 2}


def solution(mesh):
    def body(coarse_tiles, prolong_taps, tile_lists, nest_owner):
        rows, row_width = coarse_tiles.shape[1:]
        edge = row_width // (CH * TILE_Z)
        dense = rows * TILE_Z == NFZ and edge % (2 * rows) == 0
        whole = tile_lists.shape[1] * edge * REFINE == NFX
        if fits_fast(mesh) and dense and whole:
            return fast_local(coarse_tiles, prolong_taps, tile_lists, nest_owner)
        return local(coarse_tiles, prolong_taps, tile_lists, nest_owner)

    return jax.shard_map(
        body,
        mesh=mesh,
        in_specs=(P("farm", GROUP, None), P(), P(), P()),
        out_specs=(P("farm", GROUP, None), P("farm", None, GROUP, None)),
        check_vma=False,
    )
```

```python
import math

import jax
import jax.numpy as jnp
import numpy as np
from jax import lax
from jax.experimental import pallas as pl
from jax.experimental.pallas import tpu as pltpu
from jax.sharding import PartitionSpec as P

TILE_Z = 32
REFINE = 4
TAPS = 8
CH = 4
NFX = 256
NFY = 128
NFZ = 128


exact_mode = lax.Precision.HIGHEST


def with_halo(block, sides, width):
    for axis, dim in sides:
        count = lax.axis_size(axis)
        forward = [(i, i + 1) for i in range(count - 1)]
        forward.append((count - 1, 0))
        backward = [(target, source) for source, target in forward]
        low = lax.ppermute(
            lax.slice_in_dim(block, block.shape[dim] - width, None, axis=dim), axis, forward
        )
        high = lax.ppermute(lax.slice_in_dim(block, 0, width, axis=dim), axis, backward)
        block = jnp.concatenate([low, block, high], axis=dim)
    return block


def prolong_matrix(taps_row, fine_count, coarse_count, fine_start, coarse_start, period):
    fine_index = fine_start + jnp.arange(fine_count, dtype=jnp.int32)
    coarse_index = coarse_start + jnp.arange(coarse_count, dtype=jnp.int32)
    offset = jnp.mod(fine_index[:, None] - REFINE * coarse_index[None, :] + 2, period)
    tap_match = offset[:, :, None] == jnp.arange(TAPS, dtype=jnp.int32)[None, None, :]
    return jnp.sum(
        jnp.where(tap_match, taps_row[None, None, :], jnp.zeros((), jnp.float32)), axis=2
    )


def eigen_part(freq_start, freq_count, length):
    freq_index = (freq_start + jnp.arange(freq_count, dtype=jnp.int32)).astype(jnp.float32)
    return 4.0 * jnp.sin(freq_index * (math.pi / length)) ** 2


def slot_lists(tile_lists, nest_owner, slot_ids):
    owner_match = nest_owner[None, :] == slot_ids[:, None]
    return jnp.sum(jnp.where(owner_match[:, :, None], tile_lists[None, :, :], 0), axis=1)


def wave_tables(length):
    index_row = jnp.arange(length, dtype=jnp.int32)
    turns = jnp.mod(index_row[:, None] * index_row[None, :], length).astype(jnp.float32)
    phase_angle = turns * (2.0 * math.pi / length)
    return (jnp.cos(phase_angle), jnp.sin(phase_angle))


def apply_along(matrix, values, axis_id):
    moved = jnp.tensordot(matrix, values, axes=([1], [axis_id]), precision=exact_mode)
    return jnp.moveaxis(moved, 0, axis_id)


def forward_pair(real_part, imag_part, cosines, sines, axis_id):
    return (
        apply_along(cosines, real_part, axis_id) + apply_along(sines, imag_part, axis_id),
        apply_along(cosines, imag_part, axis_id) - apply_along(sines, real_part, axis_id),
    )


def inverse_pair(real_part, imag_part, cosines, sines, axis_id, length):
    return (
        (apply_along(cosines, real_part, axis_id) - apply_along(sines, imag_part, axis_id))
        / length,
        (apply_along(sines, real_part, axis_id) + apply_along(cosines, imag_part, axis_id))
        / length,
    )


def to_real_space(real_part, imag_part, cos_x, sin_x, cos_z, sin_z):
    real_z, imag_z = inverse_pair(real_part, imag_part, cos_z, sin_z, 2, NFZ)
    return (apply_along(cos_x, real_z, 0) - apply_along(sin_x, imag_z, 0)) / NFX


def local(coarse_tiles, prolong_taps, tile_lists, nest_owner):
    farm_count = lax.axis_size("farm")
    farm_index = lax.axis_index("farm")
    groups = lax.axis_size(("nx", "ny"))
    group_index = lax.axis_index(("nx", "ny"))
    local_tiles, row_count, row_width = coarse_tiles.shape
    tile_edge = row_width // (CH * TILE_Z)
    pair_count = tile_lists.shape[1]
    slot_ids = jnp.arange(farm_count, dtype=jnp.int32)
    slot_tiles = slot_lists(tile_lists, nest_owner, slot_ids)
    owned_ids = farm_index * local_tiles + jnp.arange(local_tiles, dtype=jnp.int32)
    selector = (slot_tiles[:, :, None] == owned_ids[None, None, :]).astype(jnp.float32)
    send_pick = jnp.sum(selector, axis=1)
    flat_tiles = coarse_tiles.reshape(local_tiles, row_count * row_width)
    outgoing = jnp.dot(send_pick, flat_tiles, precision=exact_mode)
    incoming = lax.all_to_all(
        outgoing.reshape(farm_count, row_count, row_width),
        "farm",
        split_axis=0,
        concat_axis=0,
        tiled=True,
    )
    my_tiles = slot_tiles[farm_index]
    home_index = my_tiles // local_tiles
    order_pick = (home_index[:, None] == slot_ids[None, :]).astype(jnp.float32)
    nest_rows = jnp.dot(
        order_pick, incoming.reshape(farm_count, row_count * row_width), precision=exact_mode
    )
    nest_rows = nest_rows.reshape(pair_count, row_count, row_width)
    framed = with_halo(nest_rows, ((("nx", "ny"), 1),), 1)
    width_x = pair_count * tile_edge
    coarse = framed.reshape(pair_count, row_count + 2, CH, tile_edge, TILE_Z).transpose(
        2, 0, 3, 1, 4
    )
    coarse = coarse.reshape(CH, width_x, row_count + 2, TILE_Z)
    fine_rows = REFINE * row_count
    matrix_x = prolong_matrix(prolong_taps[0], NFX, width_x, 0, 0, NFX)
    matrix_y = prolong_matrix(
        prolong_taps[1],
        fine_rows + 1,
        row_count + 2,
        fine_rows * group_index,
        row_count * group_index - 1,
        NFY,
    )
    matrix_z = prolong_matrix(prolong_taps[2], NFZ, TILE_Z, 0, 0, NFZ)
    refined = apply_along(matrix_x, coarse, 1)
    refined = apply_along(matrix_z, refined, 3)
    refined = apply_along(matrix_y, refined, 2)
    own_rows = refined[:, :, :fine_rows, :]
    spread = (
        jnp.roll(own_rows[0], -1, 0)
        - own_rows[0]
        + (refined[1, :, 1:, :] - own_rows[1])
        + (jnp.roll(own_rows[2], -1, 2) - own_rows[2])
    )
    cos_y, sin_y = wave_tables(NFY)
    cos_z, sin_z = wave_tables(NFZ)
    ahead_cos, ahead_sin = wave_tables(NFX)
    behind_cos, behind_sin = (ahead_cos, ahead_sin)
    real_x = apply_along(ahead_cos, spread, 0)
    imag_x = -apply_along(ahead_sin, spread, 0)
    real_xz, imag_xz = forward_pair(real_x, imag_x, cos_z, sin_z, 2)
    columns = lax.all_to_all(
        jnp.stack([real_xz, imag_xz]), ("nx", "ny"), split_axis=1, concat_axis=2, tiled=True
    )
    span = ahead_cos.shape[0] // groups
    real_y, imag_y = forward_pair(columns[0], columns[1], cos_y, sin_y, 1)
    eigen_y = eigen_part(0, NFY, NFY)
    eigen_z = eigen_part(0, NFZ, NFZ)
    eigen_sum = (
        eigen_part(group_index * span, span, NFX)[:, None, None]
        + eigen_y[None, :, None]
        + eigen_z[None, None, :]
    )
    nonzero = eigen_sum > 0
    factor = jnp.where(nonzero, -1.0 / jnp.where(nonzero, eigen_sum, 1.0), 0.0)
    real_p = real_y * factor
    imag_p = imag_y * factor
    back_real, back_imag = inverse_pair(real_p, imag_p, cos_y, sin_y, 1, NFY)
    theta = jnp.arange(NFY, dtype=jnp.float32) * (2.0 * math.pi / NFY)
    cos_diff = (1.0 - jnp.cos(theta))[None, :, None]
    sin_diff = jnp.sin(theta)[None, :, None]
    real_g = real_p * cos_diff - imag_p * sin_diff
    imag_g = real_p * sin_diff + imag_p * cos_diff
    grad_real, grad_imag = inverse_pair(real_g, imag_g, cos_y, sin_y, 1, NFY)
    returned = lax.all_to_all(
        jnp.stack([back_real, back_imag, grad_real, grad_imag]),
        ("nx", "ny"),
        split_axis=2,
        concat_axis=1,
        tiled=True,
    )
    pressure = to_real_space(returned[0], returned[1], behind_cos, behind_sin, cos_z, sin_z)
    grad_y = to_real_space(returned[2], returned[3], behind_cos, behind_sin, cos_z, sin_z)
    new_fields = jnp.stack(
        [
            own_rows[0] - (pressure - jnp.roll(pressure, 1, 0)),
            own_rows[1] - grad_y,
            own_rows[2] - (pressure - jnp.roll(pressure, 1, 2)),
            own_rows[3] + pressure,
        ]
    )
    blocks = new_fields.reshape(CH, width_x, REFINE, row_count, REFINE, TILE_Z, REFINE).mean(
        axis=(2, 4, 6)
    )
    restored = blocks.reshape(CH, pair_count, tile_edge, row_count, TILE_Z).transpose(1, 3, 0, 2, 4)
    restored = restored.reshape(pair_count, row_count * row_width)
    returning = jnp.dot(order_pick.T, restored, precision=exact_mode)
    arrived = lax.all_to_all(
        returning.reshape(farm_count, row_count, row_width),
        "farm",
        split_axis=0,
        concat_axis=0,
        tiled=True,
    )
    placed = jnp.dot(
        send_pick.T, arrived.reshape(farm_count, row_count * row_width), precision=exact_mode
    )
    covered = jnp.sum(send_pick, axis=0)
    updated = coarse_tiles * (1.0 - covered)[:, None, None] + placed.reshape(
        local_tiles, row_count, row_width
    )
    return (updated, pressure[None])


BF = jnp.bfloat16
F32 = jnp.float32
GROUP = ("nx", "ny")


def split_np(table):
    hi = jnp.asarray(table, F32).astype(BF)
    return hi


def halves(value):
    hi = value.astype(BF)
    return hi, (value - hi.astype(F32)).astype(BF)


def halves_np(table):
    table = np.asarray(table, np.float32)
    hi = table.astype(BF)
    return hi, (table - hi.astype(np.float32)).astype(BF)


def mm(left, right):
    return jnp.dot(left, right, preferred_element_type=F32)


def x_slots(nfx):
    quarter = nfx // 4
    low = np.arange(quarter)
    freq = np.concatenate([low, low, low + quarter, low + quarter])
    phase = np.concatenate(
        [np.ones(quarter), 1j * np.ones(quarter), np.ones(quarter), 1j * np.ones(quarter)]
    ).astype(np.complex128)
    freq[quarter] = nfx // 2
    phase[quarter] = 1.0
    phase[2 * quarter] = 1.0 - 1.0j
    weight = np.where((freq == 0) | (freq == nfx // 2), 1.0, 2.0)
    return freq, phase, weight


def z_slots(nfz):
    half = nfz // 2
    low = np.arange(half)
    freq = np.concatenate([low, low])
    imag = np.concatenate([np.zeros(half, bool), np.ones(half, bool)])
    freq[half] = half
    imag[half] = False
    weight = np.where((freq == 0) | (freq == half), 1.0, 2.0)
    return freq, imag, weight


def tables(nfx, nfy, nfz, rows):
    out = {}
    quarter = nfx // 4
    fx, phase, wx = x_slots(nfx)
    theta = 2 * np.pi * fx / nfx
    tap = np.arange(TAPS)[:, None] - 2
    gamma = (wx / nfx) * phase * np.exp(-1j * theta[None] * tap)
    mean = sum(np.exp(1j * theta * q) for q in range(REFINE)) / REFINE
    step = (np.exp(1j * theta * (REFINE - 1)) - np.exp(-1j * theta)) / REFINE
    gx = np.stack([gamma, gamma * mean, gamma * step])
    out["gx"] = np.stack([gx.real, gx.imag])
    turns = (np.arange(nfx)[:, None] * fx[None, :]) % nfx
    out["ex"] = np.stack([np.cos(turns * 2 * np.pi / nfx), np.sin(turns * 2 * np.pi / nfx)])
    out["e4"] = out["ex"][:, ::REFINE]
    fz, imag, wz = z_slots(nfz)
    phi = 2 * np.pi * fz / nfz
    psi = np.where(imag, -1j, 1.0)
    gz = psi * np.exp(-1j * phi[None] * tap)
    gz = np.stack([gz, gz * (np.exp(1j * phi) - 1.0)])
    out["gz"] = np.stack([gz.real, gz.imag])
    coarse_z = nfz // REFINE
    turns = (REFINE * np.arange(coarse_z)[:, None] * fz[None, :]) % nfz
    zz = np.stack([np.cos(turns * 2 * np.pi / nfz), np.sin(turns * 2 * np.pi / nfz)])
    out["zz"] = np.tile(zz, (1, rows, 1))
    turns = (fz[:, None] * np.arange(nfz)[None, :]) % nfz
    angle = turns * 2 * np.pi / nfz
    iz = (wz / nfz)[:, None] * np.where(imag[:, None], -np.sin(angle), np.cos(angle))
    hi, lo = halves_np(iz)
    out["iz"] = np.concatenate(
        [np.concatenate([hi, lo], 1), np.concatenate([hi, np.zeros_like(lo)], 1)], 0
    )
    rz = iz.reshape(nfz, coarse_z, REFINE).mean(2)
    dz = (iz[:, REFINE - 1 :: REFINE] - np.roll(iz, 1, 1)[:, ::REFINE]) / REFINE
    eye = np.eye(rows)
    big = [
        np.einsum("ij,kz->ikjz", eye, mat).reshape(rows * nfz, rows * coarse_z) for mat in (rz, dz)
    ]
    out["rz"] = np.stack(halves_np(np.concatenate(big, 1)))
    coarse = np.arange(quarter)
    turns = (coarse[:, None] * coarse[None, :]) % quarter
    angle = turns * 2 * np.pi / quarter
    fwd = np.concatenate([np.cos(angle), -np.sin(angle)], 0)
    fwd[quarter] = 1.0
    hi, lo = halves_np(fwd)
    out["fx"] = np.concatenate([hi, hi, lo], 1)
    mu = 4 * np.sin(np.pi * fx / nfx)[:, None] ** 2 + 4 * np.sin(np.pi * fz / nfz)[None, :] ** 2
    root = 1 + mu / 2 - np.sqrt(mu + mu * mu / 4)
    root = np.where(mu == 0, 0.0, root)
    kappa = -root / (1 - root**2)
    per = 1 / (1 - root**nfy)
    dx = np.exp(1j * theta) - 1
    own = dx.real.copy()
    other = np.concatenate(
        [-dx.imag[:quarter], dx.imag[:quarter], -dx.imag[2 * quarter : 3 * quarter],
         dx.imag[2 * quarter : 3 * quarter]]
    )
    own[0], own[quarter], own[2 * quarter], own[3 * quarter] = 0.0, -2.0, -1.0, 0.0
    other[[0, quarter, 2 * quarter, 3 * quarter]] = 0.0
    wide = np.ones((1, nfz))
    out["planes"] = np.stack([root, kappa, per, own[:, None] * wide, other[:, None] * wide])
    out["planes"] = out["planes"].astype(np.float32)
    flat = [out.pop("gx").reshape(-1, nfx), out.pop("ex").reshape(-1, nfx)]
    flat += [out.pop("e4").reshape(-1, nfx)]
    flat += [np.concatenate([part[0], part[1]], -1).reshape(-1, nfx) for part in (out.pop("gz"), out.pop("zz"))]
    out["bank"] = np.concatenate(flat, 0).astype(np.float32)
    return out


def find_tiles(me, lists, owner, local_tiles, farm_count, pairs):
    found, shifts, held = [], [], []
    size = jnp.int32(local_tiles)
    for nest in range(farm_count):
        tile = jnp.int32(0)
        for pair in range(pairs):
            entry = lists[nest, pair]
            tile = jnp.where(lax.div(entry, size) == me, entry, tile)
        held.append(tile)
    for shift in range(farm_count):
        target = me ^ shift
        tile = held[0]
        for nest in range(1, farm_count):
            tile = jnp.where(owner[nest] == target, held[nest], tile)
        found.append(tile - me * local_tiles)
    for pair in range(pairs):
        tile = jnp.int32(0)
        for nest in range(farm_count):
            tile = jnp.where(owner[nest] == me, lists[nest, pair], tile)
        shifts.append(lax.div(tile, size) ^ me)
    return found, shifts


def swap_blocks(value, rows, width):
    lane = lax.broadcasted_iota(jnp.int32, value.shape, 1) // width
    sub = lax.broadcasted_iota(jnp.int32, value.shape, 0) % rows
    delta = lane - sub
    result = value
    lanes = value.shape[1]
    height = value.shape[0]
    for shift in range(1, rows):
        for sign in (1, -1):
            amount = sign * shift
            moved = pltpu.roll(value, (amount * width) % lanes, 1)
            moved = pltpu.roll(moved, (-amount) % height, 0)
            result = jnp.where(delta == amount, moved, result)
    return result


def pick_kernel(local_tiles, farm_count, pairs, lists_any, owner_any, tiles, *refs):
    info, outs = refs[0], refs[1 : 1 + farm_count]
    lists, owner, sems = refs[1 + farm_count :]
    reads = [
        pltpu.make_async_copy(lists_any, lists, sems.at[farm_count]),
        pltpu.make_async_copy(owner_any, owner, sems.at[farm_count + 1]),
    ]
    for copy in reads:
        copy.start()
    for copy in reads:
        copy.wait()
    me = lax.axis_index("farm")
    found, shifts = find_tiles(me, lists, owner, local_tiles, farm_count, pairs)
    copies = []
    for shift in range(farm_count):
        copies.append(
            pltpu.make_async_copy(tiles.at[found[shift]], outs[shift], sems.at[shift])
        )
        copies[-1].start()
    for shift in range(farm_count):
        info[shift] = found[shift]
    for pair in range(pairs):
        info[farm_count + pair] = shifts[pair]
    info[farm_count + pairs] = lax.axis_index(GROUP)
    for copy in copies:
        copy.wait()


def arrange_kernel(farm_count, pairs, info, gate, *refs):
    tiles = refs[:farm_count]
    piece, own, stage = refs[farm_count:]
    for shift in range(farm_count):
        stage[shift] = tiles[farm_count - 1 - shift][...]
    rows = stage.shape[1]
    width_x, lanes = own.shape
    channels = stage.shape[2] * pairs // (width_x * (lanes // rows))
    edge = width_x // pairs
    per = lanes // rows
    row_lanes = edge * per
    for pair in range(pairs):
        tile = stage[info[farm_count + pair]]
        for channel in range(channels):
            for part in range(edge * per // (2 * lanes)):
                base = channel * row_lanes + 2 * part * lanes
                block = jnp.concatenate(
                    [tile[:, base : base + lanes], tile[:, base + lanes : base + 2 * lanes]], 0
                )
                at = pair * edge + 2 * part * rows
                if channel < channels - 1:
                    at = channel * width_x + at
                    piece[at : at + 2 * rows, :] = swap_blocks(block, rows, per)
                else:
                    own[at : at + 2 * rows, :] = swap_blocks(block, rows, per)
    rolled = pltpu.roll(own[...], per, 1)
    half = width_x // 2
    front = lax.broadcasted_iota(jnp.int32, (half, lanes), 1) < lanes // 2
    edges = jnp.where(front, rolled[0:half], pltpu.roll(rolled[half:], lanes // 2, 1))
    piece[(channels - 1) * width_x :, :] = edges


def prep_kernel(taps, bank, mats, rmats, wu, ww):
    nfx = mats.shape[1]
    quarter = nfx // REFINE
    lanes = wu.shape[0] // 2
    duo = lanes // 2
    at_ex = 6 * TAPS
    at_e4 = at_ex + 2 * nfx
    at_gz = at_e4 + 2 * quarter
    at_zz = at_gz + 2 * TAPS

    def weighted(at, axis):
        total = taps[axis, 0] * bank[at : at + 1, :]
        for tap in range(1, TAPS):
            total = total + taps[axis, tap] * bank[at + tap : at + tap + 1, :]
        return total

    full = weighted(0, 0) * bank[at_ex : at_ex + nfx, :]
    full = full - weighted(3 * TAPS, 0) * bank[at_ex + nfx : at_ex + 2 * nfx, :]
    hi, lo = halves(full)
    mats[0:nfx, :] = hi
    mats[nfx : 2 * nfx, :] = lo
    for which in (1, 2):
        at = (which - 1) * quarter
        coarse = weighted(which * TAPS, 0) * bank[at_e4 : at_e4 + quarter, :]
        second = bank[at_e4 + quarter : at_e4 + 2 * quarter, :]
        coarse = coarse - weighted((3 + which) * TAPS, 0) * second
        hi, lo = halves(coarse)
        rmats[0, at : at + quarter, :] = hi
        rmats[1, at : at + quarter, :] = lo
    band = lax.broadcasted_iota(jnp.int32, (duo, lanes), 0) // (duo // 2)
    for which, target in ((0, wu), (1, ww)):
        value = weighted(at_gz + which * TAPS, 2) * bank[at_zz : at_zz + lanes, :]
        value = value[:, 0:lanes] + value[:, lanes : 2 * lanes]
        for row in range(2):
            hi, lo = halves(jnp.where(band == row, value[0:duo], 0.0))
            at = row * lanes
            target[0:duo, at : at + lanes] = hi
            target[duo:lanes, at : at + lanes] = hi
            target[lanes : lanes + duo, at : at + lanes] = lo
            target[lanes + duo : 2 * lanes, at : at + lanes] = jnp.zeros_like(lo)


def solve_kernel(farm_count, pairs, groups, info, taps, *refs):
    blocks, own_q = refs[:groups], refs[groups]
    refs = refs[:groups] + refs[groups + 1 :]
    (fx, wu, ww, planes, rmats, rz, tiles, spectrum) = refs[groups : groups + 8]
    outs = refs[groups + 8 : groups + 8 + farm_count]
    base = refs[groups + 8 + farm_count]
    (left, field, mean_p, step_p, fresh, out_stage, zero_add, shelf, sems) = refs[
        groups + 9 + farm_count :
    ]
    take = pltpu.make_async_copy(tiles, shelf, sems.at[0])
    take.start()
    group = info[farm_count + pairs]
    width_x, lanes = own_q.shape
    channels = fresh.shape[0]
    pieces = [
        [block.at[pl.ds(channel * width_x, width_x)] for channel in range(channels - 1)]
        + [block.at[pl.ds((channels - 1) * width_x, width_x // 2)]]
        for block in blocks
    ]
    rows = mean_p.shape[0]
    per = lanes // rows
    coarse_y = groups * rows
    fine_y = coarse_y * REFINE
    own_fine = rows * REFINE
    coarse_rows = fx.shape[0]

    def band(axis):
        quarter = 1.0 / REFINE
        return (
            (taps[axis, 6] + taps[axis, 7]) * quarter,
            (taps[axis, 2] + taps[axis, 3] + taps[axis, 4] + taps[axis, 5]) * quarter,
            (taps[axis, 0] + taps[axis, 1]) * quarter,
        )

    lane = lax.broadcasted_iota(jnp.int32, (width_x, lanes), 1)
    previous = group ^ ((group + groups - 1) & (groups - 1))
    following = group ^ ((group + 1) & (groups - 1))

    def beside(shift, channel):
        value = pieces[1][channel][...]
        mark = 3
        while mark < groups:
            value = jnp.where(shift == mark, pieces[mark][channel][...], value)
            mark = 2 * mark + 1
        return value

    @pl.when(group >= 0)
    def _():
        for channel in range(channels):
            lag, mid, lead = band(1)
            if channel < channels - 1:
                here = pieces[0][channel][...]
                before = pltpu.roll(beside(previous, channel), per, 1)
                after = pltpu.roll(beside(following, channel), lanes - per, 1)
            else:
                here = own_q[...]
                prior, later = beside(previous, channel), beside(following, channel)
                before = jnp.concatenate([prior, pltpu.roll(prior, lanes // 2, 1)], 0)
                after = jnp.concatenate([pltpu.roll(later, lanes // 2, 1), later], 0)
            low = jnp.where(lane < per, before, pltpu.roll(here, per, 1))
            high = jnp.where(lane >= lanes - per, after, pltpu.roll(here, lanes - per, 1))
            value = mid * here + lag * low + lead * high
            lag, mid, lead = band(2)
            spot = lane % per
            low = jnp.where(spot == 0, pltpu.roll(value, lanes - per + 1, 1), pltpu.roll(value, 1, 1))
            high = jnp.where(
                spot == per - 1, pltpu.roll(value, per - 1, 1), pltpu.roll(value, lanes - 1, 1)
            )
            value = mid * value + lag * low + lead * high
            lag, mid, lead = band(0)
            value = (
                mid * value
                + lag * pltpu.roll(value, 1, 0)
                + lead * pltpu.roll(value, width_x - 1, 0)
            )
            fresh[channel] = value
    duo = lanes // 2
    ahead_half = lax.broadcasted_iota(jnp.int32, (coarse_rows, lanes), 1) < duo
    for block in range(groups):
        @pl.when(group >= 0)
        def _():
            hi, lo = halves(jnp.concatenate([pieces[block][channel][...] for channel in range(3)], 1))
            turned = mm(fx[...], jnp.concatenate([hi, lo, hi], 0))
            for channel in range(3):
                value = turned[:, channel * lanes : (channel + 1) * lanes]
                moved = pltpu.roll(value, duo, 1)
                twins = (
                    jnp.where(ahead_half, value, moved),
                    jnp.where(ahead_half, moved, value),
                )
                for pair in range(2):
                    value = twins[pair]
                    hi = value.astype(BF)
                    rest = jnp.where(ahead_half, value, value - hi.astype(F32)).astype(BF)
                    at = (2 * block + pair) * coarse_rows
                    left[channel, at : at + coarse_rows, :] = jnp.concatenate([rest, hi], 1)
    chunk = min(groups, 4)
    for channel in range(3):
        @pl.when(group >= 0)
        def _():
            weight = ww if channel == 2 else wu
            for block in range(0, groups, chunk):
                at = 2 * block * coarse_rows
                value = mm(left[channel, at : at + 2 * chunk * coarse_rows, :], weight[...])
                for inner in range(chunk):
                    for row in range(rows):
                        at_y = (((group ^ (block + inner)) - group) * rows + row) & (coarse_y - 1)
                        at = (2 * inner + row // 2) * coarse_rows
                        field[channel, at_y] = value[
                            at : at + coarse_rows, (row % 2) * lanes : (row % 2 + 1) * lanes
                        ]

    @pl.when(group >= 0)
    def _():
        sums = jnp.concatenate(
            [jnp.sum(pieces[block][1][...], axis=0, keepdims=True) for block in range(groups)], 0
        )
        total_z = taps[2, 0]
        for tap in range(1, TAPS):
            total_z = total_z + taps[2, tap]
        sums = sums * total_z
        shape = (groups, lanes)
        coarse_id = rows * (lax.broadcasted_iota(jnp.int32, shape, 0) ^ group)
        coarse_id = coarse_id + lax.broadcasted_iota(jnp.int32, shape, 1) // per
        corner = (lax.broadcasted_iota(jnp.int32, (8, lanes), 0) == 0) & (
            lax.broadcasted_iota(jnp.int32, (8, lanes), 1) == 0
        )
        for index in range(own_fine + 1):
            at = own_fine * group - 1 + index
            weight = jnp.zeros(shape, F32)
            for tap in range(TAPS):
                gap = (at - REFINE * coarse_id + 2 - tap) & (fine_y - 1)
                saw = 0.5 - (2 * gap + 1).astype(F32) * (0.5 / fine_y)
                weight = weight + taps[1, tap] * saw
            value = jnp.sum(jnp.sum(weight * sums, axis=1, keepdims=True), axis=0, keepdims=True)
            zero_add[index] = jnp.where(corner, value, 0.0)

    take.wait()
    give = pltpu.make_async_copy(shelf, base, sems.at[1])
    give.start()

    def at_row(offset):
        return offset % coarse_y

    def tap_y(offset):
        return taps[1, offset + 2]

    half_rows = coarse_rows // 2

    def sweep(step, carry):
        low = pl.multiple_of(8 * step, 8)
        spots = (low, half_rows + low)
        slots = [pl.multiple_of(part * half_rows + low, 8) for part in range(4)]

        def plane(which, part):
            return planes[which, pl.ds(slots[part], 8), :]

        def coarse(channel, row, side):
            return field[channel, row, pl.ds(spots[side], 8), :]

        root = [plane(0, part) for part in range(4)]
        quad = [value * value for value in root]
        quad = [value * value for value in quad]

        def horner(i, acc):
            spread = []
            for way, (offset, sign) in enumerate(((-2, -1), (rows + 1, 1))):
                row = at_row(offset + sign * (coarse_y - 1 - i))
                loaded = [[coarse(c, row, side) for side in range(2)] for c in range(3)]
                spread += [
                    acc[12 * way + c * 4 + part] * quad[part] + loaded[c][part % 2]
                    for c in range(3)
                    for part in range(4)
                ]
            return tuple(spread)

        sums_far = tuple(jnp.zeros((8, lanes), F32) for _ in range(24))
        for i in range(coarse_y):
            sums_far = horner(i, sums_far)
        below, above = sums_far[:12], sums_far[12:]
        opening = jnp.where(step == 0, 1.0, 0.0)
        near = list(range(-1, rows + 1))
        near_u = {m: [coarse(0, at_row(m), side) for side in range(2)] for m in near}
        near_v = {m: [coarse(1, at_row(m), side) for side in range(2)] for m in near}
        near_w = {m: [coarse(2, at_row(m), side) for side in range(2)] for m in near}
        for part in range(4):
            side = part % 2
            mate = part + 1 if side == 0 else part - 1
            r = root[part]
            kappa, per_wrap = plane(1, part), plane(2, part)
            own, other = plane(3, part), plane(4, part)
            turn = {
                m: own * near_u[m][side] + other * near_u[m][1 - side] + near_w[m][side]
                for m in near
            }
            lift = {m: near_v[m][side] for m in near}
            poly_a2 = tap_y(-2) * r + tap_y(-1)
            poly_a1 = poly_a2
            for e in range(0, 4):
                poly_a1 = poly_a1 * r + tap_y(e)
            poly_a = (poly_a1 * r + tap_y(4)) * r + tap_y(5)
            poly_b2 = tap_y(5) * r + tap_y(4)
            poly_b1 = poly_b2
            for e in (3, 2, 1, 0):
                poly_b1 = poly_b1 * r + tap_y(e)
            poly_b = (poly_b1 * r + tap_y(-1)) * r + tap_y(-2)
            far_scale = per_wrap * r * r
            turn_l = own * below[part] + other * below[mate] + below[8 + part]
            turn_r = own * above[part] + other * above[mate] + above[8 + part]
            drop = r - 1.0
            start = far_scale * poly_a * (turn_l + drop * below[4 + part])
            start = start + poly_a1 * turn[-1] + (drop * poly_a1 + tap_y(4)) * lift[-1]
            start = start + poly_a2 * turn[0] + (drop * poly_a2 + tap_y(0)) * lift[0]
            end = far_scale * poly_b * (r * turn_r - drop * above[4 + part])
            end = end + r * poly_b1 * turn[rows] - (drop * poly_b1 + tap_y(0)) * lift[rows]
            end = end + r * poly_b2 * turn[rows - 1] - (drop * poly_b2 + tap_y(4)) * lift[rows - 1]
            source = []
            for j in range(own_fine):
                m0, q = j // REFINE, j % REFINE
                total = None
                for m in (m0 - 1, m0, m0 + 1):
                    e = j - REFINE * m
                    if -2 <= e <= 5:
                        term = tap_y(e) * turn[m]
                        total = term if total is None else total + term
                    if -3 <= e <= 5:
                        scale = (tap_y(e + 1) if e < 5 else 0.0) - (tap_y(e) if e > -3 else 0.0)
                        total = total + scale * lift[m] if total is not None else scale * lift[m]
                source.append(total)
            ahead = [start]
            for j in range(own_fine):
                ahead.append(ahead[-1] * r + source[j])
            back = end
            pressure = [None] * (own_fine + 1)
            pressure[own_fine] = kappa * (ahead[own_fine] + back)
            for j in range(own_fine - 1, -1, -1):
                back = r * (back + source[j])
                pressure[j] = kappa * (ahead[j] + back)
            if part == 0:
                pressure = [pressure[j] + opening * zero_add[j] for j in range(own_fine + 1)]
            spot = pl.ds(slots[part], 8)
            for j in range(own_fine):
                spectrum[j, spot, :] = pressure[j + 1]
            for m in range(rows):
                at = REFINE * m
                total = pressure[at + 1]
                for q in range(1, REFINE):
                    total = total + pressure[at + 1 + q]
                mean_p[m, spot, :] = total * (1.0 / REFINE)
                step_p[m, spot, :] = (pressure[at + REFINE] - pressure[at]) * (1.0 / REFINE)
        return carry

    lax.fori_loop(0, half_rows // 8, sweep, 0)
    def left_three(count, stacked):
        hi, lo = halves(stacked)
        value = mm(rmats[0, 0:count, :], hi) + mm(rmats[0, 0:count, :], lo)
        return value + mm(rmats[1, 0:count, :], hi)

    def right_three(value, table):
        hi, lo = halves(value)
        return mm(hi, table[0]) + mm(lo, table[0]) + mm(hi, table[1])

    smooth = left_three(2 * width_x, jnp.concatenate([mean_p[m] for m in range(rows)], 1))
    slope = left_three(width_x, jnp.concatenate([step_p[m] for m in range(rows)], 1))
    mean_x, step_x = smooth[0:width_x], smooth[width_x : 2 * width_x]
    through = right_three(jnp.concatenate([step_x, slope, mean_x], 0), rz)
    part_w = through[2 * width_x : 3 * width_x, lanes:]
    through = through[:, 0:lanes]
    change = [
        -through[0:width_x],
        -through[width_x : 2 * width_x],
        -part_w,
        through[2 * width_x : 3 * width_x],
    ]

    for channel in range(channels):
        fresh[channel] = fresh[channel] + change[channel]
    @pl.when(group >= 0)
    def _():
        shifts = [info[farm_count + pair] for pair in range(pairs)]
        edge = width_x // pairs
        row_lanes = edge * per
        for pair in range(pairs):
            for channel in range(channels):
                for part in range(row_lanes // (2 * lanes)):
                    at = pair * edge + 2 * part * rows
                    block = swap_blocks(fresh[channel, at : at + 2 * rows, :], rows, per)
                    base = channel * row_lanes + 2 * part * lanes
                    out_stage[shifts[pair], :, base : base + lanes] = block[0:rows]
                    out_stage[shifts[pair], :, base + lanes : base + 2 * lanes] = block[rows:]
        for shift in range(farm_count):
            outs[shift][...] = out_stage[shift]
    give.wait()


def inverse_kernel(iz, mats, spectrum, out, middle):
    count, nfx, lanes = spectrum.shape
    for at in range(0, count, 4):
        hi, lo = halves(spectrum[at : at + 4].reshape(4 * nfx, lanes))
        both = mm(jnp.concatenate([hi, lo], 1), iz[...])
        middle[at : at + 4] = (both[:, 0:lanes] + both[:, lanes : 2 * lanes]).reshape(4, nfx, lanes)
    for at in range(0, count, 2):
        hi, lo = halves(jnp.concatenate([middle[at], middle[at + 1]], 1))
        upper = mm(mats[...], hi)
        final = upper[0:nfx] + upper[nfx : 2 * nfx] + mm(mats[0:nfx, :], lo)
        for row in range(2):
            out[:, at + row, :] = final[:, row * lanes : (row + 1) * lanes]


def patch_kernel(farm_count, info, base, *refs):
    tiles, out, sems = refs[:farm_count], refs[farm_count], refs[farm_count + 1]
    copies = []
    for shift in range(farm_count):
        copies.append(
            pltpu.make_async_copy(
                tiles[farm_count - 1 - shift], out.at[info[shift]], sems.at[shift]
            )
        )
        copies[-1].start()
    for copy in copies:
        copy.wait()


def in_vmem():
    return pl.BlockSpec(memory_space=pltpu.VMEM)


def in_smem():
    return pl.BlockSpec(memory_space=pltpu.SMEM)


def anywhere():
    return pl.BlockSpec(memory_space=pl.ANY)


def in_hbm():
    return pl.BlockSpec(memory_space=pltpu.HBM)


def keep_hbm(value):
    return pltpu.with_memory_space_constraint(value, pltpu.HBM)


def limit(mib):
    return pltpu.CompilerParams(vmem_limit_bytes=mib << 20)


def cost(flops, nbytes):
    return pl.CostEstimate(flops=flops, bytes_accessed=nbytes, transcendentals=0)


def flip(value, axis, bits):
    count = lax.axis_size(axis)
    return lax.ppermute(value, axis, [(i, i ^ bits) for i in range(count)])


def fast_local(coarse_tiles, prolong_taps, tile_lists, nest_owner):
    farm_count = lax.axis_size("farm")
    groups = lax.axis_size(GROUP)
    local_tiles, rows, row_width = coarse_tiles.shape
    pairs = tile_lists.shape[1]
    edge = row_width // (CH * TILE_Z)
    width_x = pairs * edge
    lanes = rows * TILE_Z
    own_fine = rows * REFINE
    table = tables(NFX, NFY, NFZ, rows)
    const = {key: jnp.asarray(value) for key, value in table.items()}
    bind = lambda kernel, *sizes: (lambda *refs: kernel(*sizes, *refs))
    tile_shape = jax.ShapeDtypeStruct((rows, row_width), F32)

    info, *picked = pl.pallas_call(
        bind(pick_kernel, local_tiles, farm_count, pairs),
        name="pick",
        out_shape=[jax.ShapeDtypeStruct((farm_count + pairs + 1,), jnp.int32)]
        + [tile_shape] * farm_count,
        in_specs=[in_hbm()] * 3,
        out_specs=[in_smem()] + [in_vmem()] * farm_count,
        scratch_shapes=[
            pltpu.SMEM(tile_lists.shape, jnp.int32),
            pltpu.SMEM(nest_owner.shape, jnp.int32),
            pltpu.SemaphoreType.DMA((farm_count + 2,)),
        ],
        compiler_params=limit(8),
        cost_estimate=cost(0, 1 << 18),
    )(keep_hbm(tile_lists), keep_hbm(nest_owner), keep_hbm(coarse_tiles))
    moved = {s: flip(picked[s], "farm", s) for s in range(farm_count - 1, 0, -1)}
    moved = [picked[0]] + [moved[s] for s in range(1, farm_count)]
    mats, rmats, wu, ww = pl.pallas_call(
        prep_kernel,
        name="prep",
        out_shape=[
            jax.ShapeDtypeStruct((2 * NFX, NFX), BF),
            jax.ShapeDtypeStruct((2, 2 * width_x, NFX), BF),
            jax.ShapeDtypeStruct((2 * lanes, 2 * NFZ), BF),
            jax.ShapeDtypeStruct((2 * lanes, 2 * NFZ), BF),
        ],
        in_specs=[in_smem(), in_vmem()],
        out_specs=[in_vmem()] * 4,
        compiler_params=limit(8),
        cost_estimate=cost(0, 6 << 20),
    )(prolong_taps, const["bank"])

    piece, own = pl.pallas_call(
        bind(arrange_kernel, farm_count, pairs),
        name="arrange",
        out_shape=[
            jax.ShapeDtypeStruct(((CH - 1) * width_x + width_x // 2, lanes), F32),
            jax.ShapeDtypeStruct((width_x, lanes), F32),
        ],
        in_specs=[in_smem(), anywhere()] + [in_vmem()] * farm_count,
        out_specs=[in_vmem()] * 2,
        scratch_shapes=[pltpu.VMEM((farm_count, rows, row_width), F32)],
        compiler_params=limit(8),
        cost_estimate=cost(0, 1 << 18),
    )(info, rmats, *moved[::-1])
    far_bit, core_bit, near_bit = 4, 2, 1
    held = {0: piece}
    for bits in (near_bit, far_bit, near_bit | far_bit):
        held[bits] = flip(piece, GROUP, bits)
    for bits in (0, near_bit, far_bit, near_bit | far_bit):
        held[bits | core_bit] = flip(held[bits], GROUP, core_bit)

    coarse_rows = 2 * width_x
    coarse_y = groups * rows
    spectrum, *fresh, base = pl.pallas_call(
        bind(solve_kernel, farm_count, pairs, groups),
        name="solve",
        out_shape=[jax.ShapeDtypeStruct((own_fine, NFX, NFZ), F32)]
        + [tile_shape] * farm_count
        + [jax.ShapeDtypeStruct(coarse_tiles.shape, F32)],
        in_specs=[in_smem()] * 2
        + [in_vmem()] * (groups + 7)
        + [in_hbm()],
        out_specs=[in_vmem()] * (farm_count + 1) + [in_hbm()],
        scratch_shapes=[
            pltpu.VMEM((3, 2 * groups * coarse_rows, 2 * lanes), BF),
            pltpu.VMEM((3, coarse_y, coarse_rows, NFZ), F32),
            pltpu.VMEM((rows, NFX, NFZ), F32),
            pltpu.VMEM((rows, NFX, NFZ), F32),
            pltpu.VMEM((CH, width_x, lanes), F32),
            pltpu.VMEM((farm_count, rows, row_width), F32),
            pltpu.VMEM((own_fine + 1, 8, lanes), F32),
            pltpu.VMEM(coarse_tiles.shape, F32),
            pltpu.SemaphoreType.DMA((2,)),
        ],
        compiler_params=limit(40),
        cost_estimate=cost(4 << 30, 8 << 20),
    )(
        info, prolong_taps,
        *[held[s] for s in range(groups)],
        own,
        const["fx"], wu, ww, const["planes"], rmats, const["rz"],
        keep_hbm(coarse_tiles),
    )
    returned = [fresh[0]] + [flip(fresh[s], "farm", s) for s in range(1, farm_count)]

    half = 8
    pressure = pl.pallas_call(
        inverse_kernel,
        name="inverse",
        out_shape=jax.ShapeDtypeStruct((NFX, own_fine, NFZ), F32),
        grid=(own_fine // half,),
        in_specs=[
            pl.BlockSpec((2 * NFZ, 2 * NFZ), lambda i: (0, 0)),
            pl.BlockSpec((2 * NFX, NFX), lambda i: (0, 0)),
            pl.BlockSpec((half, NFX, NFZ), lambda i: (i, 0, 0)),
        ],
        out_specs=pl.BlockSpec((NFX, half, NFZ), lambda i: (0, i, 0)),
        scratch_shapes=[pltpu.VMEM((half, NFX, NFZ), F32)],
        compiler_params=limit(24),
        cost_estimate=cost(4 << 30, 4 << 20),
    )(const["iz"], mats, spectrum)

    updated = pl.pallas_call(
        bind(patch_kernel, farm_count),
        name="patch",
        out_shape=jax.ShapeDtypeStruct(coarse_tiles.shape, F32),
        in_specs=[in_smem(), in_hbm()] + [in_vmem()] * farm_count,
        out_specs=in_hbm(),
        scratch_shapes=[pltpu.SemaphoreType.DMA((farm_count,))],
        input_output_aliases={1: 0},
        compiler_params=limit(8),
        cost_estimate=cost(0, 1 << 18),
    )(info, base, *returned[::-1])
    return updated, pressure[None]


def fits_fast(mesh):
    return dict(mesh.shape) == {"farm": 4, "nx": 4, "ny": 2}


def solution(mesh):
    def body(coarse_tiles, prolong_taps, tile_lists, nest_owner):
        rows, row_width = coarse_tiles.shape[1:]
        edge = row_width // (CH * TILE_Z)
        dense = rows * TILE_Z == NFZ and edge % (2 * rows) == 0
        whole = tile_lists.shape[1] * edge * REFINE == NFX
        if fits_fast(mesh) and dense and whole:
            return fast_local(coarse_tiles, prolong_taps, tile_lists, nest_owner)
        return local(coarse_tiles, prolong_taps, tile_lists, nest_owner)

    return jax.shard_map(
        body,
        mesh=mesh,
        in_specs=(P("farm", GROUP, None), P(), P(), P()),
        out_specs=(P("farm", GROUP, None), P("farm", None, GROUP, None)),
        check_vma=False,
    )
```
